32 devices in a mesh: dp: 8 (over z, x), tensor: 4 (over y, core).
Axes of the slice: x: 2, y: 2, z: 4, core: 2. Of those that a mesh axis runs over, the one named last changes fastest.
Arguments:
- block_input: bfloat16 [1024, 8, 1024], P('tensor', 'dp'), may hold values from -6 to 6
- pre_gain: float32 [1024], replicated, may hold values from 0.25 to 1.75
- w_zx: bfloat16 [1024, 2, 2048], P('dp', None, 'tensor'), may hold values from -0.1875 to 0.1875
- w_dt: bfloat16 [1024, 32], P('dp', 'tensor'), may hold values from -0.1875 to 0.1875
- w_bc: bfloat16 [1024, 256], P('dp'), may hold values from -0.1875 to 0.1875
- conv_x_w: float32 [4, 2048], P(None, 'tensor'), may hold values from -3 to 3
- conv_x_b: float32 [2048], P('tensor'), may hold values from -3 to 3
- conv_bc_w: float32 [4, 256], replicated, may hold values from -3 to 3
- conv_bc_b: float32 [256], replicated, may hold values from -3 to 3
- dt_bias: float32 [32], P('tensor'), may hold values from -4 to -1
- a_log: float32 [32], P('tensor'), may hold values from -7.6 to -0.7
- d_skip: float32 [32], P('tensor'), may hold values from 0.5 to 1.5
- gate_gain: float32 [2048], P('tensor'), may hold values from 0.25 to 1.75
- w_out: bfloat16 [2048, 1024], P('tensor', 'dp'), may hold values from -0.125 to 0.125
- cotangent: bfloat16 [1024, 8, 1024], P('tensor', 'dp'), may hold values from -6 to 6
Outputs:
- block_output: float32 [1024, 8, 1024], P('tensor', 'dp')
- input_grad: float32 [1024, 8, 1024], P('tensor', 'dp')
- grad_pre_gain: float32 [1024], replicated
- grad_w_zx: float32 [1024, 2, 2048], P('dp', None, 'tensor')
- grad_w_dt: float32 [1024, 32], P('dp', 'tensor')
- grad_w_bc: float32 [1024, 256], P('dp')
- grad_conv_x_w: float32 [4, 2048], P(None, 'tensor')
- grad_conv_x_b: float32 [2048], P('tensor')
- grad_conv_bc_w: float32 [4, 256], replicated
- grad_conv_bc_b: float32 [256], replicated
- grad_dt_bias: float32 [32], P('tensor')
- grad_a_log: float32 [32], P('tensor')
- grad_d_skip: float32 [32], P('tensor')
- grad_gate_gain: float32 [2048], P('tensor')
- grad_w_out: float32 [2048, 1024], P('tensor', 'dp')
The draws below stay inside these ranges and needn't reach their ends.
All inputs are finite; a program needn't handle non-finite values.
Results may differ from the reference program's by a relative error of at most 0.0094.
Values may be sent and summed in bfloat16 or wider, within the bound.
No kernel may reach another device: no remote copies, remote signals or barrier semaphores. Data moves between devices by JAX's collectives and lax.ppermute only.
A program may use at most 128 MiB of HBM per device.

```python
import jax
import jax.numpy as jnp
from jax import lax

D = 1024
HEADS = 32
HEAD_DIM = 64
STATE = 128
KERNEL = 4
SPAN = 256
SEQ = 1024
DI = 2048
SEQS = 8


def draw_a_log(key, part):
    first = jax.random.fold_in(key, 0)
    return jax.random.uniform(first, (HEADS,), jnp.float32, -6.2, -0.7)


def raised(values, own_key, source, target, shards_of, factor):
    def block_of(dim):
        return (jnp.arange(values.shape[dim]) // (values.shape[dim] // shards_of)).reshape((-1,) + (1,) * (values.ndim - 1 - dim))

    first = jax.random.permutation(own_key, shards_of)[block_of(target)]
    far = (block_of(target) + shards_of // 2) % shards_of
    return jnp.where((block_of(source) == first) | (block_of(source) == far), factor * values, values)


def block_levels(rng, extent, cuts, smallest, high):
    def one(axis_at, parts):
        heights = jax.random.uniform(jax.random.fold_in(jax.random.fold_in(rng, 6), axis_at), (parts,), jnp.float32, smallest / len(cuts), high / len(cuts))
        return jnp.repeat(jnp.exp(heights), extent[axis_at] // parts).reshape((-1,) + (1,) * (len(extent) - axis_at - 1))

    factor_of = one(*cuts[0])
    for cut in cuts[1:]:
        factor_of = factor_of * one(*cut)
    return factor_of


def scatter_about(key, dims, deviation, limit, cuts=(), dtype=jnp.bfloat16):
    array = jax.random.normal(key, dims, jnp.float32) * deviation
    if len(cuts) > 0:
        array = block_levels(key, dims, cuts, -0.22, 0.18) * array
    return jnp.clip(array, min=-limit, max=limit).astype(dtype)


def bell_draw_with(own_key, shape, scale, most, shards, heavy, held_as=jnp.bfloat16):
    values = scale * jax.random.normal(own_key, shape, jnp.float32)
    if shards:
        values = values * block_levels(own_key, shape, shards, -0.22, 0.18)
    return jnp.clip(raised(values, jax.random.fold_in(own_key, 3), *heavy), -most, most).astype(held_as)


def setup_inputs(seed: int = 0) -> dict:
    splits = jax.random.split(jax.random.key(seed), 16)
    block_input = bell_draw_with(splits[0], (SEQ, SEQS, D), 1.0, 6.0, ((0, 4), (1, 8)), (1, 2, 8, 2.0))
    pre_gain = jnp.clip(1.0 + 0.15 * jax.random.normal(splits[1], (D,), jnp.float32), 0.25, 1.75)
    w_zx = scatter_about(splits[2], (D, 2, DI), D ** -0.5, 0.1875, ((0, 8), (2, 4)))
    w_dt = scatter_about(splits[3], (D, HEADS), D ** -0.5, 0.1875, ((0, 8), (1, 4)))
    w_bc = scatter_about(splits[4], (D, 2 * STATE), D ** -0.5, 0.1875, ((0, 8),))
    conv_x_w = scatter_about(splits[5], (KERNEL, DI), KERNEL ** -0.5, 3.0, ((1, 4),), jnp.float32)
    conv_x_b = scatter_about(splits[6], (DI,), 0.5, 3.0, ((0, 4),), jnp.float32)
    conv_bc_w = scatter_about(splits[7], (KERNEL, 2 * STATE), KERNEL ** -0.5, 3.0, (), jnp.float32)
    conv_bc_b = scatter_about(splits[8], (2 * STATE,), 0.5, 3.0, (), jnp.float32)
    dt_bias = jnp.clip(-4.0 + 3.0 * jax.random.uniform(splits[9], (HEADS,), jnp.float32) ** block_levels(splits[9], (HEADS,), ((0, 4),), -0.2, 0.2), -4.0, -1.0)
    a_log = draw_a_log(jax.random.fold_in(splits[15], 71), 0)
    d_skip = jnp.clip(0.5 + 1.0 * jax.random.uniform(splits[11], (HEADS,), jnp.float32) ** block_levels(splits[11], (HEADS,), ((0, 4),), -0.2, 0.2), 0.5, 1.5)
    gate_gain = jnp.clip(1.0 + 0.15 * jax.random.normal(splits[12], (DI,), jnp.float32), 0.25, 1.75)
    w_out = scatter_about(splits[13], (DI, D), DI ** -0.5, 0.125, ((0, 4), (1, 8)))
    cotangent = bell_draw_with(splits[14], (SEQ, SEQS, D), 1.0, 6.0, ((0, 4), (1, 8)), (1, 2, 8, 2.0))
    return {"block_input": block_input, "pre_gain": pre_gain, "w_zx": w_zx, "w_dt": w_dt, "w_bc": w_bc, "conv_x_w": conv_x_w, "conv_x_b": conv_x_b, "conv_bc_w": conv_bc_w, "conv_bc_b": conv_bc_b, "dt_bias": dt_bias, "a_log": a_log, "d_skip": d_skip, "gate_gain": gate_gain, "w_out": w_out, "cotangent": cotangent}


epsilon = 1e-05
highest = lax.Precision.HIGHEST

def causal_conv(values, kernel, offset):
    width = kernel.shape[0]
    length = values.shape[0]
    padded = jnp.pad(values, ((width - 1, 0), (0, 0)))
    total = jnp.zeros_like(values) + offset
    for tap in range(width):
        total = total + kernel[tap] * padded[tap:tap + length]
    return total

def scan_heads(inputs, steps, rates, keys, queries, skip):
    length, heads, width = inputs.shape
    count = length // SPAN
    inputs_block = inputs.reshape(count, SPAN, heads, width)
    steps_block = steps.reshape(count, SPAN, heads)
    keys_block = keys.reshape(count, SPAN, keys.shape[-1])
    queries_block = queries.reshape(count, SPAN, queries.shape[-1])
    logs = jnp.cumsum(steps_block * rates, axis=1)
    gaps = logs[:, :, None, :] - logs[:, None, :, :]
    lower = jnp.arange(SPAN)[:, None] >= jnp.arange(SPAN)[None, :]
    decay = jnp.exp(jnp.where(lower[None, :, :, None], gaps, -jnp.inf))
    scores = jnp.einsum('ctn,csn->cts', queries_block, keys_block, precision=highest)
    weights = scores[..., None] * decay * steps_block[:, None, :, :]
    within = jnp.einsum('ctsh,cshp->cthp', weights, inputs_block, precision=highest)
    ends = logs[:, -1:, :] - logs
    scaled = inputs_block * (jnp.exp(ends) * steps_block)[..., None]
    states = jnp.einsum('csn,cshp->chnp', keys_block, scaled, precision=highest)
    totals = jnp.exp(logs[:, -1, :])

    def carry_step(state, pair):
        factor, fresh = pair
        return (factor[:, None, None] * state + fresh, state)
    initial = jnp.zeros(states.shape[1:], jnp.float32)
    final_state, previous = lax.scan(carry_step, initial, (totals, states))
    across = jnp.einsum('ctn,chnp->cthp', queries_block, previous, precision=highest) * jnp.exp(logs)[..., None]
    output = (within + across).reshape(length, heads, width)
    return output + skip[:, None] * inputs

def mixer_one(raw_x, raw_dt, raw_bc, kernel_x, offset_x, kernel_bc, offset_bc, dt_offset, log_rates, skip):
    inner = jax.nn.silu(causal_conv(raw_x, kernel_x, offset_x))
    mixed_bc = jax.nn.silu(causal_conv(raw_bc, kernel_bc, offset_bc))
    half = mixed_bc.shape[-1] // 2
    steps = jax.nn.softplus(raw_dt + dt_offset)
    rates = -jnp.exp(log_rates)
    heads = steps.shape[-1]
    inputs = inner.reshape(inner.shape[0], heads, inner.shape[1] // heads)
    result = scan_heads(inputs, steps, rates, mixed_bc[:, :half], mixed_bc[:, half:], skip)
    return result.reshape(inner.shape)

def middle(gate_raw, raw_x, raw_dt, raw_bc, kernel_x, offset_x, kernel_bc, offset_bc, dt_offset, log_rates, skip, gain):
    mixed = mixer_one(raw_x, raw_dt, raw_bc, kernel_x, offset_x, kernel_bc, offset_bc, dt_offset, log_rates, skip)
    gated = mixed * jax.nn.silu(gate_raw)
    gate_inverse = lax.rsqrt(lax.optimization_barrier(jnp.mean(gated * gated, axis=-1, keepdims=True)) + epsilon)
    return gated * gate_inverse * gain

def reference(block_input, pre_gain, w_zx, w_dt, w_bc, conv_x_w, conv_x_b, conv_bc_w, conv_bc_b, dt_bias, a_log, d_skip, gate_gain, w_out, cotangent):
    inner_total = HEADS * HEAD_DIM
    zx_flat = w_zx.reshape(D, 2 * inner_total)
    params = (conv_x_w, conv_x_b, conv_bc_w, conv_bc_b, dt_bias, a_log, d_skip, gate_gain)

    def one_sequence(carry, pair):
        sequence, upstream = pair
        wide = sequence.astype(jnp.float32)
        inverse = lax.rsqrt(lax.optimization_barrier(jnp.mean(wide * wide, axis=-1, keepdims=True)) + epsilon)
        normed = (wide * inverse * pre_gain).astype(jnp.bfloat16)
        proj_zx = jnp.dot(normed, zx_flat, preferred_element_type=jnp.float32).reshape(SEQ, 2, inner_total)
        raw_dt = jnp.dot(normed, w_dt, preferred_element_type=jnp.float32)
        raw_bc = jnp.dot(normed, w_bc, preferred_element_type=jnp.float32)
        scaled, pullback = jax.vjp(middle, proj_zx[:, 0], proj_zx[:, 1], raw_dt, raw_bc, *params)
        scaled_half = scaled.astype(jnp.bfloat16)
        output = wide + jnp.dot(scaled_half, w_out, preferred_element_type=jnp.float32)
        grad_scaled = jnp.dot(upstream, w_out.T, preferred_element_type=jnp.float32)
        grad_out = jnp.dot(scaled_half.T, upstream, preferred_element_type=jnp.float32)
        grads = pullback(grad_scaled)
        grad_zx = jnp.stack([grads[0], grads[1]], axis=1).reshape(SEQ, 2 * inner_total).astype(jnp.bfloat16)
        grad_dt = grads[2].astype(jnp.bfloat16)
        grad_bc = grads[3].astype(jnp.bfloat16)
        grad_normed = jnp.dot(grad_zx, zx_flat.T, preferred_element_type=jnp.float32)
        grad_normed = grad_normed + jnp.dot(grad_dt, w_dt.T, preferred_element_type=jnp.float32)
        grad_normed = grad_normed + jnp.dot(grad_bc, w_bc.T, preferred_element_type=jnp.float32)
        weighted = grad_normed * pre_gain
        inner_dot = lax.optimization_barrier(jnp.mean(weighted * wide, axis=-1, keepdims=True))
        row_grad = upstream.astype(jnp.float32) + inverse * weighted - wide * inverse ** 3 * inner_dot
        gain_part = lax.optimization_barrier(jnp.sum(grad_normed * wide * inverse, axis=0))
        new_carry = (carry[0] + gain_part, carry[1] + jnp.dot(normed.T, grad_zx, preferred_element_type=jnp.float32), carry[2] + jnp.dot(normed.T, grad_dt, preferred_element_type=jnp.float32), carry[3] + jnp.dot(normed.T, grad_bc, preferred_element_type=jnp.float32), carry[4] + grad_out) + tuple((carry[5 + index] + grads[4 + index] for index in range(8)))
        return (new_carry, (output, row_grad))
    start = (jnp.zeros((D,), jnp.float32), jnp.zeros((D, 2 * inner_total), jnp.float32), jnp.zeros((D, HEADS), jnp.float32), jnp.zeros((D, 2 * STATE), jnp.float32), jnp.zeros((inner_total, D), jnp.float32)) + tuple((jnp.zeros(param.shape, jnp.float32) for param in params))
    sequences = jnp.moveaxis(block_input, 1, 0)
    upstreams = jnp.moveaxis(cotangent, 1, 0)
    totals, stacked = lax.scan(one_sequence, start, (sequences, upstreams))
    block_output = jnp.moveaxis(stacked[0], 0, 1)
    input_grad = jnp.moveaxis(stacked[1], 0, 1)
    return (block_output, input_grad, totals[0], totals[1].reshape(D, 2, inner_total), totals[2], totals[3], totals[5], totals[6], totals[7], totals[8], totals[9], totals[10], totals[11], totals[12], totals[4])
```

```python
import jax
import jax.numpy as jnp
from jax import lax
from jax.experimental import pallas as pl
from jax.experimental.pallas import tpu as pltpu
from jax.sharding import PartitionSpec as P


CHUNK = 128
ROWS = 256
LANES = 128
epsilon = 1e-05
highest = lax.Precision.HIGHEST
f32 = jnp.float32
bf16 = jnp.bfloat16

NN = (((1,), (0,)), ((), ()))
NT = (((1,), (1,)), ((), ()))
TN = (((0,), (0,)), ((), ()))


def mm(a, b, dims=NN):
    return lax.dot_general(a, b, dims, preferred_element_type=f32)


def halves(v):
    high = v.astype(bf16)
    return high, (v - high.astype(f32)).astype(bf16)


def fine(a, b, dims=NN):
    a_high, a_low = halves(a)
    b_high, b_low = halves(b)
    return mm(a_high, b_high, dims) + mm(a_high, b_low, dims) + mm(a_low, b_high, dims)


def swap(value, axis, bits):
    size = lax.axis_size(axis)
    return lax.ppermute(value, axis, [(i, i ^ bits) for i in range(size)])


def gather(value, axis):
    size = lax.axis_size(axis)
    pieces = {0: value}
    for k in range(2, size, 2):
        pieces[k] = swap(value, axis, k)
    if size > 1:
        for k in range(0, size, 2):
            pieces[k ^ 1] = swap(pieces[k], axis, 1)
    return [pieces[k] for k in range(size)]


def near_first(parts, axis):
    size = lax.axis_size(axis)
    rows = parts.shape[0] // size

    def piece(k):
        return parts[k * rows : (k + 1) * rows]

    terms = [piece(0)]
    if size == 1:
        return terms
    for k in range(size - 2, 0, -2):
        other = swap(piece(k ^ 1), axis, 1)
        both = piece(k).astype(f32) + other.astype(f32)
        terms.append(swap(both.astype(bf16), axis, k))
    terms.append(swap(piece(1), axis, 1))
    return terms


def far_first(parts, axis):
    size = lax.axis_size(axis)
    rows = parts.shape[0] // size
    if size == 1:
        return [parts]
    pairs = [parts[: 2 * rows]]
    for k in range(2, size, 2):
        pairs.append(swap(parts[k * rows : (k + 2) * rows], axis, k))
    other = sum(pair[rows:].astype(f32) for pair in pairs).astype(bf16)
    return [pair[:rows] for pair in pairs] + [swap(other, axis, 1)]


def total_of(terms):
    return sum(term.astype(f32) for term in terms)


def direct_terms(value, axis):
    terms = [value]
    for k in range(1, lax.axis_size(axis)):
        terms.append(swap(value, axis, k))
    return terms


def all_sum(value, axis):
    size = lax.axis_size(axis)
    if size == 1:
        return value
    value = value + swap(value, axis, 1)
    total = value
    for k in range(2, size, 2):
        total = total + swap(value, axis, k)
    return total


def softplus(v):
    return jnp.maximum(v, 0.0) + jnp.log1p(jnp.exp(-jnp.abs(v)))


def lower(size):
    return lax.broadcasted_iota(jnp.int32, (size, size), 0) >= lax.broadcasted_iota(
        jnp.int32, (size, size), 1
    )


def pick(values, lane_head):
    out = values[0]
    for j in range(1, len(values)):
        out = jnp.where(lane_head == j, values[j], out)
    return out


def take(out, refs, which):
    for k, ref in enumerate(refs):

        @pl.when(which == k)
        def _(ref=ref):
            out[...] = ref[...]


def join(out, refs):
    rows = refs[0].shape[0]
    for k, ref in enumerate(refs):
        out[k * rows : (k + 1) * rows, :] = ref[...]


def forward_kernel(width, head_dim, count, pieces, per, start):
    per_group = LANES // head_dim

    def kernel(place, *refs):
        token_refs, refs = refs[:count], refs[count:]
        weight_refs, refs = refs[:pieces], refs[pieces:]
        taps_x, taps_bc, per_head, skip, *carried = refs[:7]
        refs = refs[7 + (0 if start == 0 else 7) :]
        pre_x, pre_bc, raw_x, raw_bc, dt_out, mixed, before, state, halo_x, halo_bc = refs[:10]
        if start == 0:
            weights, refs = refs[10], refs[11:]
        else:
            weights, refs = weight_refs[0], refs[10:]
        ext_x, ext_bc, normed = refs
        size = normed.shape[0]
        take(normed, token_refs, ((pl.program_id(0) + start) // per) ^ place[0])
        inner = mixed.shape[1]
        twice = pre_bc.shape[1]
        states = twice // 2

        @pl.when(pl.program_id(0) == 0)
        def _():
            state[...] = carried[0][...]
            ext_x[0:8, :] = carried[1][...]
            ext_bc[0:8, :] = carried[2][...]
            if start == 0:
                join(weights, weight_refs)

        raw = mm(normed[...], weights[...])

        def conv(ext, values, taps, raw_ref, pre_ref, halo):
            ext[8 : 8 + size, :] = values
            raw_ref[...] = values.astype(bf16)
            total = taps[width : width + 1, :]
            for k in range(width):
                start = 8 - (width - 1) + k
                total = total + taps[k : k + 1, :] * ext[start : start + size, :]
            halo[...] = ext[size : size + 8, :]
            ext[0:8, :] = halo[...]
            pre_ref[...] = total
            return total * jax.nn.sigmoid(total)

        x = conv(ext_x, raw[:, :inner], taps_x, raw_x, pre_x, halo_x)
        bc = conv(ext_bc, raw[:, inner : inner + twice], taps_bc, raw_bc, pre_bc, halo_bc)
        dt = raw[:, inner + twice :] + per_head[0:1, :]
        dt_out[...] = dt
        steps = softplus(dt)
        below = lower(size)
        logs = lax.dot_general(
            below.astype(f32), steps * per_head[1:2, :], NN, precision=highest,
            preferred_element_type=f32,
        )
        logs_t = logs.T
        keys = bc[:, :states]
        keys_t = keys.T
        queries = bc[:, states:]
        scores = jnp.where(below, fine(queries, keys, NT), 0.0)
        lane_head = lax.broadcasted_iota(jnp.int32, (size, LANES), 1) // head_dim
        for group in range(inner // LANES):
            lanes = slice(group * LANES, (group + 1) * LANES)
            x_g = x[:, lanes]
            heads = [group * per_group + j for j in range(per_group)]
            step_e = pick(
                [jnp.broadcast_to(steps[:, h : h + 1], (size, LANES)) for h in heads], lane_head
            )
            log_e = pick(
                [jnp.broadcast_to(logs[:, h : h + 1], (size, LANES)) for h in heads], lane_head
            )
            xs = x_g * step_e
            total = skip[0:1, lanes] * x_g
            for j, h in enumerate(heads):
                gap = logs[:, h : h + 1] - logs_t[h : h + 1, :]
                weights_h = scores * jnp.exp(jnp.minimum(gap, 0.0))
                total = total + fine(weights_h, jnp.where(lane_head == j, xs, 0.0))
            old = state[:, lanes]
            before[0, :, lanes] = old.astype(bf16)
            total = total + jnp.exp(log_e) * fine(queries, old)
            mixed[:, lanes] = total
            last = log_e[size - 1 : size, :]
            fresh = fine(keys_t, jnp.exp(last - log_e) * xs)
            state[:, lanes] = jnp.exp(last) * old + fresh

    return kernel


def backward_kernel(width, head_dim, resumed):
    per_group = LANES // head_dim

    def kernel(place, *refs):
        d_mixed, pre_x, pre_bc, raw_x, raw_bc, dt_in, mixed, before, *refs = refs
        taps_x, taps_bc, per_head, skip, *refs = refs
        carried, refs = refs[:7], refs[7 + resumed :]
        columns, *results, ext_x, ext_bc = refs
        grad_x, grad_bc, grad_head, d_state, after, halo_x, halo_bc = results
        size = d_mixed.shape[0]
        inner = d_mixed.shape[1]
        twice = pre_bc.shape[1]
        states = twice // 2

        @pl.when(pl.program_id(0) == 0)
        def _():
            for result, value in zip(results, carried):
                result[...] = value[...]
            ext_x[size : size + 8, :] = halo_x[...]
            ext_bc[size : size + 8, :] = halo_bc[...]

        dt = dt_in[...]
        steps = softplus(dt)
        rates = per_head[1:2, :]
        below = lower(size)
        logs = lax.dot_general(
            below.astype(f32), steps * rates, NN, precision=highest, preferred_element_type=f32
        )
        logs_t = logs.T
        p_bc = pre_bc[...]
        sig_bc = jax.nn.sigmoid(p_bc)
        bc = p_bc * sig_bc
        keys = bc[:, :states].astype(bf16)
        queries = bc[:, states:].astype(bf16)
        queries_t = bc[:, states:].T
        above = lax.broadcasted_iota(jnp.int32, (size, size), 0) <= lax.broadcasted_iota(
            jnp.int32, (size, size), 1
        )
        scores_t = jnp.where(above, mm(keys, queries, NT), 0.0)
        lane_head = lax.broadcasted_iota(jnp.int32, (size, LANES), 1) // head_dim
        d_scores_t = jnp.zeros((size, size), f32)
        d_keys = jnp.zeros((size, states), f32)
        d_queries = jnp.zeros((size, states), f32)
        head_of = lax.broadcasted_iota(jnp.int32, (LANES, LANES), 0) // head_dim
        lane_of = lax.broadcasted_iota(jnp.int32, (LANES, LANES), 1)
        log_sum = jnp.zeros((size, LANES), f32)
        step_sum = jnp.zeros((size, LANES), f32)
        end_sum = jnp.zeros((8, LANES), f32)
        for group in range(inner // LANES):
            lanes = slice(group * LANES, (group + 1) * LANES)
            heads = [group * per_group + j for j in range(per_group)]
            p_x = pre_x[:, lanes]
            sig_x = jax.nn.sigmoid(p_x)
            x_g = p_x * sig_x
            dy = d_mixed[:, lanes]
            step_e = pick(
                [jnp.broadcast_to(steps[:, h : h + 1], (size, LANES)) for h in heads], lane_head
            )
            log_e = pick(
                [jnp.broadcast_to(logs[:, h : h + 1], (size, LANES)) for h in heads], lane_head
            )
            xs = x_g * step_e
            last = log_e[size - 1 : size, :]
            fade = jnp.exp(last - log_e)
            old = before[0, :, lanes]
            d_new = d_state[:, lanes]
            d_new_half = d_new.astype(bf16)
            dxs = fade * mm(keys, d_new_half)
            for j, h in enumerate(heads):
                mine = lane_head == j
                gap = logs_t[h : h + 1, :] - logs[:, h : h + 1]
                decay = jnp.exp(jnp.minimum(gap, 0.0))
                dxs = dxs + mm(
                    (scores_t * decay).astype(bf16), jnp.where(mine, dy, 0.0).astype(bf16)
                )
                d_scores_t = d_scores_t + decay * fine(jnp.where(mine, xs, 0.0), dy, NT)
            e_dy = jnp.exp(log_e) * dy
            d_queries = d_queries + sum(mm(half, old, NT) for half in halves(e_dy))
            d_keys = d_keys + fine(fade * xs, d_new, NT)
            skip_g = skip[0:1, lanes]
            log_lane = dy * (mixed[:, lanes] - skip_g * x_g) - xs * dxs
            step_lane = dxs * x_g
            end_lane = jnp.sum(d_new * after[:, lanes], axis=0, keepdims=True)
            to_head = (head_of + group * per_group == lane_of).astype(bf16)
            for high_low in halves(log_lane):
                log_sum = log_sum + mm(high_low, to_head)
            for high_low in halves(step_lane):
                step_sum = step_sum + mm(high_low, to_head)
            for high_low in halves(jnp.broadcast_to(end_lane, (8, LANES))):
                end_sum = end_sum + mm(high_low, to_head)
            d_state[:, lanes] = jnp.exp(last) * d_new + fine(queries_t, e_dy)
            after[:, lanes] = old.astype(f32)
            grad_x[width + 1 : width + 2, lanes] += jnp.sum(dy * x_g, axis=0, keepdims=True)
            dx = dxs * step_e + skip_g * dy
            d_pre = dx * (sig_x + x_g * (1.0 - sig_x))
            ext_x[0:size, lanes] = d_pre
            grad_x[width : width + 1, lanes] += jnp.sum(d_pre, axis=0, keepdims=True)
            total = jnp.zeros((size, LANES), f32)
            raw = raw_x[:, lanes].astype(f32)
            for k in range(width):
                moved = ext_x[width - 1 - k : width - 1 - k + size, lanes]
                total = total + taps_x[k : k + 1, lanes] * moved
                grad_x[k : k + 1, lanes] += jnp.sum(raw * moved, axis=0, keepdims=True)
            columns[:, lanes] = total.astype(bf16)
            halo_x[:, lanes] = ext_x[0:8, lanes]
            ext_x[size : size + 8, lanes] = halo_x[:, lanes]
        d_scores_t = jnp.where(above, d_scores_t, 0.0)
        d_keys = d_keys + fine(d_scores_t, bc[:, states:])
        d_queries = d_queries + fine(d_scores_t.T, bc[:, :states])
        at_end = lax.broadcasted_iota(jnp.int32, (size, LANES), 0) == size - 1
        d_log = log_sum + jnp.where(at_end, end_sum[0:1, :], 0.0)
        d_rate = lax.dot_general(
            above.astype(f32), d_log, NN, precision=highest, preferred_element_type=f32
        )
        grad_head[1:2, :] += rates * jnp.sum(steps * d_rate, axis=0, keepdims=True)
        d_dt = (step_sum + rates * d_rate) * jax.nn.sigmoid(dt)
        grad_head[0:1, :] += jnp.sum(d_dt, axis=0, keepdims=True)
        columns[:, inner + twice :] = d_dt.astype(bf16)
        slope = sig_bc + bc * (1.0 - sig_bc)
        ext_bc[0:size, :states] = d_keys * slope[:, :states]
        ext_bc[0:size, states:] = d_queries * slope[:, states:]
        grad_bc[width : width + 1, :] += jnp.sum(ext_bc[0:size, :], axis=0, keepdims=True)
        total = jnp.zeros((size, twice), f32)
        raw = raw_bc[...].astype(f32)
        for k in range(width):
            moved = ext_bc[width - 1 - k : width - 1 - k + size, :]
            total = total + taps_bc[k : k + 1, :] * moved
            grad_bc[k : k + 1, :] += jnp.sum(raw * moved, axis=0, keepdims=True)
        columns[:, inner : inner + twice] = total.astype(bf16)
        halo_bc[...] = ext_bc[0:8, :]
        ext_bc[size : size + 8, :] = halo_bc[...]

    return kernel


def gate_kernel(count, pieces, parts):
    def kernel(place, *refs):
        token_refs, refs = refs[:count], refs[count:]
        weight_refs, refs = refs[:pieces], refs[pieces:]
        mixed, gain, gate_raw, grad_scaled, sums, tokens, weights = refs

        @pl.when(pl.program_id(0) == 0)
        def _():
            join(weights, weight_refs)

        take(tokens, token_refs, pl.program_id(0) // parts)
        gate_body(tokens, weights, mixed, gain, gate_raw, grad_scaled, sums)

    return kernel


def gate_body(tokens, weights, mixed, gain, gate_raw, grad_scaled, sums):
    model = weights.shape[0]
    inner = mixed.shape[1]
    gate = mm(tokens[:, :model], weights[:, :inner])
    grads = mm(tokens[:, model:], weights[:, inner:])
    gate_raw[...] = gate
    grad_scaled[...] = grads
    gated = mixed[...] * (gate * jax.nn.sigmoid(gate))
    ones = jnp.ones((8, gated.shape[1]), bf16)
    rows = lax.broadcasted_iota(jnp.int32, sums.shape[1:], 0)
    square = sum(mm(ones, part, NT) for part in halves(gated * gated))
    cross = sum(mm(ones, part, NT) for part in halves(gated * (grads * gain[...])))
    sums[0] = jnp.where(rows == 0, square, cross)


def norm_kernel(inner_total, count):
    def kernel(place, *refs):
        terms, refs = refs[:count], refs[count:]
        gate_raw, grad_scaled, mixed, gain, scaled, d_mixed, d_gate, grad_gain = refs

        @pl.when(pl.program_id(0) == 0)
        def _():
            grad_gain[...] = jnp.zeros(grad_gain.shape, f32)

        total = terms[0][0]
        for term in terms[1:]:
            total = total + term[0]
        column = total.T
        inverse = lax.rsqrt(column[:, 0:1] / inner_total + epsilon)
        pull = inverse * inverse * inverse * (column[:, 1:2] / inner_total)
        gate = gate_raw[...]
        sig = jax.nn.sigmoid(gate)
        act = gate * sig
        mix = mixed[...]
        grads = grad_scaled[...]
        unit = mix * act * inverse
        scaled[...] = (unit * gain[...]).astype(bf16)
        grad_gain[0:1, :] += jnp.sum(grads * unit, axis=0, keepdims=True)
        d_gated = inverse * (grads * gain[...]) - (mix * act) * pull
        d_mixed[...] = d_gated * act
        d_gate[...] = (d_gated * mix * (sig + act * (1.0 - sig))).astype(bf16)

    return kernel


def entry_kernel(blocks):
    def kernel(place, tokens, upstream, gain, out):
        model = tokens.shape[1]
        size = model // blocks
        wide = tokens[...].astype(f32)
        inverse = lax.rsqrt(jnp.mean(wide * wide, axis=-1, keepdims=True) + epsilon)
        normed = (wide * inverse * gain[...]).astype(bf16)
        for k in range(blocks):
            at = pl.multiple_of((place[0] ^ k) * size, size)
            out[:, pl.ds(at, size)] = normed[:, k * size : (k + 1) * size]
            out[:, pl.ds(model + at, size)] = upstream[:, k * size : (k + 1) * size]

    return kernel


def output_kernel(blocks, count):
    def kernel(place, tokens, *refs):
        out = refs[count]
        size = tokens.shape[1] // blocks
        for k in range(blocks):
            at = pl.multiple_of((place[0] ^ k) * size, size)
            total = tokens[:, k * size : (k + 1) * size].astype(f32)
            for term in refs[:count]:
                total = total + term[:, pl.ds(at, size)].astype(f32)
            out[:, 0, k * size : (k + 1) * size] = total

    return kernel


def input_kernel(blocks, count):
    def kernel(place, tokens, upstream, gain, *refs):
        out, grads = refs[count:]
        model = tokens.shape[1]
        size = model // blocks
        wide = tokens[...].astype(f32)
        inverse = lax.rsqrt(jnp.mean(wide * wide, axis=-1, keepdims=True) + epsilon)
        for k in range(blocks):
            at = pl.multiple_of((place[0] ^ k) * size, size)
            total = refs[0][:, pl.ds(at, size)].astype(f32)
            for term in refs[1:count]:
                total = total + term[:, pl.ds(at, size)].astype(f32)
            grads[:, k * size : (k + 1) * size] = total
        weighted = grads[...] * gain[...]
        inner_dot = jnp.mean(weighted * wide, axis=-1, keepdims=True)
        out[:, 0, :] = (
            upstream[...].astype(f32)
            + inverse * weighted
            - wide * (inverse * inverse * inverse * inner_dot)
        )

    return kernel


def normed_kernel(place, tokens, d_gate, columns, w_gate, w_scan, out, grad_gain):
    total = mm(d_gate[...], w_gate[...], NT) + mm(columns[...], w_scan[...], NT)
    out[...] = total.astype(bf16)
    total = total * tokens[...].astype(f32)
    grad_gain[...] = jnp.broadcast_to(jnp.sum(total, axis=0, keepdims=True), grad_gain.shape)


def whole(shape):
    return pl.BlockSpec(shape, lambda c, place: (0,) * len(shape))


def rows_of(size, cols, column=0):
    return pl.BlockSpec((size, cols), lambda c, place: (c, column))


def call(kernel, grid, ins, outs, shapes, scratch=(), aliases=None):
    return pl.pallas_call(
        kernel,
        grid_spec=pltpu.PrefetchScalarGridSpec(
            num_scalar_prefetch=1, grid=(grid,), in_specs=ins, out_specs=outs,
            scratch_shapes=scratch,
        ),
        out_shape=[jax.ShapeDtypeStruct(*one) for one in shapes],
        input_output_aliases=aliases or {},
    )


def exchange_blocks(values, axis, blocks):
    index = lax.axis_index(axis)
    rows, cols = values.shape
    bits = 1
    while bits < blocks:
        split = values.reshape(rows, blocks // (2 * bits), 2, bits * (cols // blocks))
        split = jnp.where((index & bits) != 0, split[:, :, ::-1], split)
        values = split.reshape(rows, cols)
        bits *= 2
    return values


def per_device(
    block_input, pre_gain, w_zx, w_dt, w_bc, conv_x_w, conv_x_b, conv_bc_w, conv_bc_b,
    dt_bias, a_log, d_skip, gate_gain, w_out, cotangent,
):
    rows_local, seqs, model = block_input.shape
    assert seqs == 1
    dp = lax.axis_size("dp")
    tensor = lax.axis_size("tensor")
    length = rows_local * tensor
    inner = w_zx.shape[2]
    twice = w_bc.shape[1]
    states = twice // 2
    heads = w_dt.shape[1]
    head_dim = inner // heads
    width = conv_x_w.shape[0]
    wide_cols = inner + twice + LANES
    inner_total = inner * tensor
    chunk = min(CHUNK, rows_local)
    block = min(ROWS, rows_local)
    chunks = length // chunk
    place_dp = lax.axis_index("dp").astype(jnp.int32).reshape(1)
    place_tensor = lax.axis_index("tensor").astype(jnp.int32).reshape(1)
    narrow = (model // dp) % LANES != 0
    blocks = 1 if narrow else dp
    place_entry = place_dp * 0 if narrow else place_dp

    tokens_local = block_input.reshape(rows_local, model)
    upstream_local = cotangent.reshape(rows_local, model)
    gain_in = pre_gain.reshape(1, model)
    w_scan = jnp.concatenate(
        [w_zx[:, 1, :], w_bc, w_dt, jnp.zeros((w_dt.shape[0], LANES - heads), bf16)], axis=1
    )
    w_late = jnp.concatenate([w_zx[:, 0, :], w_out.T], axis=1)
    (both_local,) = call(
        entry_kernel(blocks), 1,
        [whole((rows_local, model)), whole((rows_local, model)), whole((1, model))],
        [whole((rows_local, 2 * model))],
        [((rows_local, 2 * model), bf16)],
    )(place_entry, tokens_local, upstream_local, gain_in)
    if narrow:
        both_local = jnp.concatenate(
            [exchange_blocks(half, "dp", dp) for half in jnp.split(both_local, 2, axis=1)], axis=1
        )
    scan_pieces = gather(w_scan, "dp")
    token_pieces = gather(both_local, "tensor")
    late_pieces = gather(w_late, "dp")

    def stack(rows, cols):
        rows = [r.reshape(-1, r.shape[-1]) for r in rows]
        packed = jnp.concatenate(rows, axis=0)
        return jnp.pad(packed, ((0, 8 - packed.shape[0]), (0, cols - packed.shape[1])))

    taps_x = stack([conv_x_w, conv_x_b], inner)
    taps_bc = stack([conv_bc_w, conv_bc_b], twice)
    per_head = stack([dt_bias, -jnp.exp(a_log)], LANES)
    skip = jnp.repeat(d_skip, head_dim).reshape(1, inner)
    gain = gate_gain.reshape(1, inner)

    per = rows_local // chunk

    def stored(c, place):
        return ((c // per) ^ place[0]) * per + c % per

    def ahead(cols, start):
        return pl.BlockSpec((chunk, cols), lambda c, place: (stored(c + start, place), 0))

    def back(cols, start):
        return pl.BlockSpec((chunk, cols), lambda c, place: (stored(start - c, place), 0))

    def token_piece(k, start):
        def index(c, place):
            c = c + start
            return jnp.where((c // per) ^ place[0] == k, c % per, 0), 0

        return pl.BlockSpec((chunk, model), index)

    anywhere = pl.BlockSpec(memory_space=pl.ANY)
    calls = 2 if chunks % 2 == 0 else 1
    span = chunks // calls
    carry_shapes = [((states, inner), f32), ((8, inner), f32), ((8, twice), f32)]
    carry = [jnp.zeros(*one) for one in carry_shapes]
    saved, weights = [], scan_pieces
    for start in range(0, chunks, span):
        results = call(
            forward_kernel(width, head_dim, tensor, len(weights), per, start),
            span,
            [token_piece(k, start) for k in range(tensor)]
            + [whole(one.shape) for one in weights]
            + [whole((8, inner)), whole((8, twice)), whole((8, LANES)), whole((1, inner))]
            + [whole(one.shape) for one in carry]
            + [anywhere] * len(saved),
            [ahead(cols, start) for cols in (inner, twice, inner, twice, LANES, inner)]
            + [pl.BlockSpec((1, states, inner), lambda c, place, start=start: (c + start, 0, 0))]
            + [whole(one.shape) for one in carry]
            + [whole((model, wide_cols))] * (start == 0),
            [
                ((length, inner), f32), ((length, twice), f32), ((length, inner), bf16),
                ((length, twice), bf16), ((length, LANES), f32), ((length, inner), f32),
                ((chunks, states, inner), bf16), *carry_shapes,
            ]
            + [((model, wide_cols), bf16)] * (start == 0),
            [
                pltpu.VMEM((chunk + 8, inner), f32), pltpu.VMEM((chunk + 8, twice), f32),
                pltpu.VMEM((chunk, model), bf16),
            ],
            {1 + tensor + len(weights) + 7 + k: k for k in range(len(saved))},
        )(place_tensor, *token_pieces, *weights, taps_x, taps_bc, per_head, skip, *carry, *saved)
        saved, carry = results[:7], results[7:10]
        if start == 0:
            full_scan = results[10]
            weights = [full_scan]
    pre_x, pre_bc, raw_x, raw_bc, dt, mixed, before = saved

    parts = rows_local // block
    in_order = pl.BlockSpec(
        (1, 8, block), lambda c, place: (((c // parts) ^ place[0]) * parts + c % parts, 0, 0)
    )

    def gate_piece(k):
        return pl.BlockSpec(
            (block, 2 * model), lambda c, place: (jnp.where(c // parts == k, c % parts, 0), 0)
        )

    gate_raw, grad_scaled, sums, tokens, full_late = call(
        gate_kernel(tensor, dp, parts), length // block,
        [gate_piece(k) for k in range(tensor)]
        + [whole((model // dp, 2 * inner))] * dp
        + [rows_of(block, inner), whole((1, inner))],
        [
            rows_of(block, inner), rows_of(block, inner), in_order, rows_of(block, 2 * model),
            whole((model, 2 * inner)),
        ],
        [
            ((length, inner), f32), ((length, inner), f32), ((length // block, 8, block), f32),
            ((length, 2 * model), bf16), ((model, 2 * inner), bf16),
        ],
    )(place_tensor, *token_pieces, *late_pieces, mixed, gain)

    sum_terms = direct_terms(sums, "tensor")

    scaled, d_mixed, d_gate, grad_gain = call(
        norm_kernel(inner_total, tensor), length // block,
        [in_order] * tensor
        + [rows_of(block, inner), rows_of(block, inner), rows_of(block, inner), whole((1, inner))],
        [rows_of(block, inner), rows_of(block, inner), rows_of(block, inner), whole((8, inner))],
        [
            ((length, inner), bf16), ((length, inner), f32), ((length, inner), bf16),
            ((8, inner), f32),
        ],
    )(place_tensor, *sum_terms, gate_raw, grad_scaled, mixed, gain)

    normed = tokens[:, :model]
    upstream = tokens[:, model:]
    out_part = lax.dot_general(upstream, scaled, TN, preferred_element_type=f32).astype(bf16)
    gate_part = lax.dot_general(normed, d_gate, TN, preferred_element_type=f32).astype(bf16)
    branch_part = mm(scaled, full_late[:, inner:], NT).astype(bf16)
    out_terms = far_first(out_part, "dp")
    gate_terms = near_first(gate_part, "dp")
    branch_terms = near_first(branch_part, "tensor")
    if narrow:
        branch_terms = [exchange_blocks(term, "dp", dp) for term in branch_terms]
    out_block = pl.BlockSpec((rows_local, 1, model), lambda c, place: (0, 0, 0))
    (block_output,) = call(
        output_kernel(blocks, len(branch_terms)), 1,
        [whole((rows_local, model))] * (1 + len(branch_terms)),
        [out_block],
        [((rows_local, 1, model), f32)],
    )(place_entry, tokens_local, *branch_terms)

    carry_shapes = [((8, inner), f32), ((8, twice), f32), ((8, LANES), f32)]
    carry_shapes += [((states, inner), f32)] * 2 + [((8, inner), f32), ((8, twice), f32)]
    carry = [jnp.zeros(*one) for one in carry_shapes]
    columns = []
    for at in range(calls):
        start = chunks - 1 - at * span
        columns, *carry = call(
            backward_kernel(width, head_dim, len(columns)), span,
            [back(cols, start) for cols in (inner, inner, twice, inner, twice, LANES, inner)]
            + [pl.BlockSpec((1, states, inner), lambda c, place, start=start: (start - c, 0, 0))]
            + [whole((8, inner)), whole((8, twice)), whole((8, LANES)), whole((1, inner))]
            + [whole(one.shape) for one in carry]
            + [anywhere] * len(columns),
            [back(wide_cols, start)] + [whole(one.shape) for one in carry],
            [((length, wide_cols), bf16), *carry_shapes],
            [pltpu.VMEM((chunk + 8, inner), f32), pltpu.VMEM((chunk + 8, twice), f32)],
            {1 + 8 + 4 + 7: 0} if columns else {},
        )(
            place_tensor, d_mixed, pre_x, pre_bc, raw_x, raw_bc, dt, mixed, before, taps_x,
            taps_bc, per_head, skip, *carry, *columns,
        )
        columns = [columns]
    columns = columns[0]
    grad_x, grad_bc, grad_head = carry[:3]

    scan_part = lax.dot_general(normed, columns, TN, preferred_element_type=f32).astype(bf16)
    scan_terms = near_first(scan_part, "dp")
    features = model // 4
    normed_part, pre_part = call(
        normed_kernel, 4,
        [
            pl.BlockSpec((length, features), lambda c, place: (0, c)),
            whole((length, inner)), whole((length, wide_cols)),
            rows_of(features, inner), rows_of(features, wide_cols),
        ],
        [
            pl.BlockSpec((length, features), lambda c, place: (0, c)),
            pl.BlockSpec((8, features), lambda c, place: (0, c)),
        ],
        [((length, model), bf16), ((8, model), f32)],
    )(place_tensor, tokens, d_gate, columns, full_late, full_scan)
    normed_terms = near_first(normed_part, "tensor")
    if narrow:
        normed_terms = [exchange_blocks(term, "dp", dp) for term in normed_terms]
    input_grad, _ = call(
        input_kernel(blocks, len(normed_terms)), 1,
        [whole((rows_local, model))] * 2 + [whole((1, model))]
        + [whole((rows_local, model))] * len(normed_terms),
        [out_block, whole((rows_local, model))],
        [((rows_local, 1, model), f32), ((rows_local, model), f32)],
    )(place_entry, tokens_local, upstream_local, gain_in, *normed_terms)

    grad_w_scan = total_of(scan_terms)
    grad_w_out = total_of(out_terms).T
    grad_w_gate = total_of(gate_terms)
    grad_w_bc = total_of(direct_terms(grad_w_scan[:, inner : inner + twice], "tensor"))
    grad_w_dt = grad_w_scan[:, inner + twice : inner + twice + heads]
    grad_w_zx = jnp.stack([grad_w_gate, grad_w_scan[:, :inner]], axis=1)

    pre_part = exchange_blocks(pre_part[:1], "dp", dp)[0] / pre_gain
    kept = width + 2
    local = jnp.concatenate([grad_x[:kept].reshape(-1), grad_gain[0], grad_head[:2].reshape(-1)])
    shared = jnp.concatenate([grad_bc[: width + 1].reshape(-1), pre_part])
    small = all_sum(jnp.concatenate([local, shared]), "dp")
    local = small[: local.shape[0]]
    shared = total_of(direct_terms(small[local.shape[0] :], "tensor"))
    of_x = local[: kept * inner].reshape(kept, inner)
    sum_gain = local[kept * inner : (kept + 1) * inner]
    of_head = local[(kept + 1) * inner :].reshape(2, LANES)
    of_bc = shared[: (width + 1) * twice].reshape(width + 1, twice)
    return (
        block_output,
        input_grad,
        shared[(width + 1) * twice :],
        grad_w_zx,
        grad_w_dt,
        grad_w_bc,
        of_x[:width],
        of_x[width],
        of_bc[:width],
        of_bc[width],
        of_head[0, :heads],
        of_head[1, :heads],
        of_x[width + 1].reshape(heads, head_dim).sum(axis=1),
        sum_gain,
        grad_w_out,
    )


def solution(mesh):
    placed = (
        P("tensor", "dp", None), P(), P("dp", None, "tensor"), P("dp", "tensor"), P("dp", None),
        P(None, "tensor"), P("tensor"), P(), P(), P("tensor"), P("tensor"), P("tensor"),
        P("tensor"), P("tensor", "dp"), P("tensor", "dp", None),
    )
    results = (
        P("tensor", "dp", None), P("tensor", "dp", None), P(), P("dp", None, "tensor"),
        P("dp", "tensor"), P("dp", None), P(None, "tensor"), P("tensor"), P(), P(), P("tensor"),
        P("tensor"), P("tensor"), P("tensor"), P("tensor", "dp"),
    )

    return jax.shard_map(per_device, mesh=mesh, in_specs=placed, out_specs=results, check_vma=False)
```

```python
import jax
import jax.numpy as jnp
from jax import lax
from jax.experimental import pallas as pl
from jax.experimental.pallas import tpu as pltpu
from jax.sharding import PartitionSpec as P


CHUNK = 128
ROWS = 256
LANES = 128
epsilon = 1e-05
highest = lax.Precision.HIGHEST
f32 = jnp.float32
bf16 = jnp.bfloat16

NN = (((1,), (0,)), ((), ()))
NT = (((1,), (1,)), ((), ()))
TN = (((0,), (0,)), ((), ()))


def mm(a, b, dims=NN):
    return lax.dot_general(a, b, dims, preferred_element_type=f32)


def halves(v):
    high = v.astype(bf16)
    return high, (v - high.astype(f32)).astype(bf16)


def fine(a, b, dims=NN):
    a_high, a_low = halves(a)
    b_high, b_low = halves(b)
    return mm(a_high, b_high, dims) + mm(a_high, b_low, dims) + mm(a_low, b_high, dims)


def swap(value, axis, bits):
    size = lax.axis_size(axis)
    return lax.ppermute(value, axis, [(i, i ^ bits) for i in range(size)])


def order_of(size):
    return list(range(0, size, 2)) + list(range(1, size, 2))


def position(k, size):
    return k // 2 + (k % 2) * ((size + 1) // 2)


def at_position(p, size):
    half = (size + 1) // 2
    return jnp.where(p < half, 2 * p, 2 * (p - half) + 1)


def gather_far(value, axis):
    pieces = {0: value}
    for k in range(2, lax.axis_size(axis), 2):
        pieces[k] = swap(value, axis, k)
    return pieces


def gather_near(pieces, axis):
    size = lax.axis_size(axis)
    pieces = dict(pieces)
    if size > 1:
        for k in range(0, size, 2):
            pieces[k ^ 1] = swap(pieces[k], axis, 1)
    return [pieces[k] for k in range(size)]


def gather(value, axis):
    return gather_near(gather_far(value, axis), axis)


def near_first(own, near, axis):
    size = lax.axis_size(axis)
    if size == 1:
        return [(own, 0)]
    half = size // 2
    rows = own.shape[0] // half
    terms = [(own, 0)]
    sent_on = []
    start = half
    for sent in near:
        other = swap(sent, axis, 1)
        other, *_ = lax.optimization_barrier((other, *sent_on))
        stop, start = start, start - sent.shape[0] // rows
        for i in range(stop - 1, start - 1, -1):
            if i == 0:
                terms.append((other, 0))
                continue
            got = other[(i - start) * rows : (i - start + 1) * rows]
            both = own[i * rows : (i + 1) * rows].astype(f32) + got.astype(f32)
            sent_on.append(both.astype(bf16))
            terms.append((swap(sent_on[-1], axis, 2 * i), 0))
    return terms


def far_first(pairs, axis):
    if lax.axis_size(axis) == 1:
        return [(pairs[0], 0)]
    rows = pairs[0].shape[0] // 2
    got = [pairs[0]]
    for i in range(1, len(pairs)):
        got.append(swap(pairs[i], axis, 2 * i))
    other = sum(both[rows:].astype(f32) for both in got).astype(bf16)
    return [(both, 0) for both in got] + [(swap(other, axis, 1), 0)]


def block_of(term, rows):
    array, index = term
    return array[index * rows : (index + 1) * rows].astype(f32)


def total_of(terms):
    return sum(term.astype(f32) for term in terms)


def direct_terms(value, axis):
    terms = [value]
    for k in range(1, lax.axis_size(axis)):
        terms.append(swap(value, axis, k))
    return terms


def all_sum(value, axis):
    size = lax.axis_size(axis)
    if size == 1:
        return value
    value = value + swap(value, axis, 1)
    total = value
    for k in range(2, size, 2):
        total = total + swap(value, axis, k)
    return total


def softplus(v):
    return jnp.maximum(v, 0.0) + jnp.log1p(jnp.exp(-jnp.abs(v)))


def lower(size):
    return lax.broadcasted_iota(jnp.int32, (size, size), 0) >= lax.broadcasted_iota(
        jnp.int32, (size, size), 1
    )


def pick(values, lane_head):
    out = values[0]
    for j in range(1, len(values)):
        out = jnp.where(lane_head == j, values[j], out)
    return out


def take(out, refs, which):
    for k, ref in enumerate(refs):

        @pl.when(which == k)
        def _(ref=ref):
            out[...] = ref[...]


def join(out, refs, start=0):
    rows = refs[0].shape[0]
    cols = out.shape[1]
    for k, ref in enumerate(refs):
        out[k * rows : (k + 1) * rows, :] = ref[:, start : start + cols]


def forward_kernel(width, head_dim, count, pieces, per, start):
    per_group = LANES // head_dim

    def kernel(place, *refs):
        token_refs, refs = refs[:count], refs[count:]
        weight_refs, refs = refs[:pieces], refs[pieces:]
        taps_x, taps_bc, per_head, skip, *carried = refs[:7]
        refs = refs[7 + (0 if start == 0 else 7) :]
        pre_x, pre_bc, raw_x, raw_bc, dt_out, mixed, before, state, halo_x, halo_bc = refs[:10]
        if start == 0:
            weights, refs = refs[10], refs[11:]
        else:
            weights, refs = weight_refs[0], refs[10:]
        ext_x, ext_bc, normed = refs
        size = normed.shape[0]
        take(normed, token_refs, ((pl.program_id(0) + start) // per) ^ place[0])
        inner = mixed.shape[1]
        twice = pre_bc.shape[1]
        states = twice // 2

        @pl.when(pl.program_id(0) == 0)
        def _():
            state[...] = carried[0][...]
            ext_x[0:8, :] = carried[1][...]
            ext_bc[0:8, :] = carried[2][...]
            if start == 0:
                join(weights, weight_refs)

        raw = mm(normed[...], weights[...])

        def conv(ext, values, taps, raw_ref, pre_ref, halo):
            ext[8 : 8 + size, :] = values
            raw_ref[...] = values.astype(bf16)
            total = taps[width : width + 1, :]
            for k in range(width):
                start = 8 - (width - 1) + k
                total = total + taps[k : k + 1, :] * ext[start : start + size, :]
            halo[...] = ext[size : size + 8, :]
            ext[0:8, :] = halo[...]
            pre_ref[...] = total
            return total * jax.nn.sigmoid(total)

        x = conv(ext_x, raw[:, :inner], taps_x, raw_x, pre_x, halo_x)
        bc = conv(ext_bc, raw[:, inner : inner + twice], taps_bc, raw_bc, pre_bc, halo_bc)
        dt = raw[:, inner + twice :] + per_head[0:1, :]
        dt_out[...] = dt
        steps = softplus(dt)
        below = lower(size)
        logs = lax.dot_general(
            below.astype(f32), steps * per_head[1:2, :], NN, precision=highest,
            preferred_element_type=f32,
        )
        logs_t = logs.T
        keys = bc[:, :states]
        keys_t = keys.T
        queries = bc[:, states:]
        scores = jnp.where(below, fine(queries, keys, NT), 0.0)
        lane_head = lax.broadcasted_iota(jnp.int32, (size, LANES), 1) // head_dim
        for group in range(inner // LANES):
            lanes = slice(group * LANES, (group + 1) * LANES)
            x_g = x[:, lanes]
            heads = [group * per_group + j for j in range(per_group)]
            step_e = pick(
                [jnp.broadcast_to(steps[:, h : h + 1], (size, LANES)) for h in heads], lane_head
            )
            log_e = pick(
                [jnp.broadcast_to(logs[:, h : h + 1], (size, LANES)) for h in heads], lane_head
            )
            xs = x_g * step_e
            xs_half = xs.astype(bf16)
            total = skip[0:1, lanes] * x_g
            for j, h in enumerate(heads):
                gap = logs[:, h : h + 1] - logs_t[h : h + 1, :]
                weights_h = (scores * jnp.exp(jnp.minimum(gap, 0.0))).astype(bf16)
                total = total + mm(weights_h, jnp.where(lane_head == j, xs_half, 0.0))
            old = state[:, lanes]
            before[0, :, lanes] = old.astype(bf16)
            total = total + jnp.exp(log_e) * fine(queries, old)
            mixed[:, lanes] = total
            last = log_e[size - 1 : size, :]
            fresh = fine(keys_t, jnp.exp(last - log_e) * xs)
            state[:, lanes] = jnp.exp(last) * old + fresh

    return kernel


def backward_kernel(width, head_dim, resumed):
    per_group = LANES // head_dim

    def kernel(place, *refs):
        d_mixed, pre_x, pre_bc, raw_x, raw_bc, dt_in, mixed, before, *refs = refs
        taps_x, taps_bc, per_head, skip, *refs = refs
        carried, refs = refs[:7], refs[7 + resumed :]
        columns, *results, ext_x, ext_bc = refs
        grad_x, grad_bc, grad_head, d_state, after, halo_x, halo_bc = results
        size = d_mixed.shape[0]
        inner = d_mixed.shape[1]
        twice = pre_bc.shape[1]
        states = twice // 2

        @pl.when(pl.program_id(0) == 0)
        def _():
            for result, value in zip(results, carried):
                result[...] = value[...]
            ext_x[size : size + 8, :] = halo_x[...]
            ext_bc[size : size + 8, :] = halo_bc[...]

        dt = dt_in[...]
        steps = softplus(dt)
        rates = per_head[1:2, :]
        below = lower(size)
        logs = lax.dot_general(
            below.astype(f32), steps * rates, NN, precision=highest, preferred_element_type=f32
        )
        logs_t = logs.T
        p_bc = pre_bc[...]
        sig_bc = jax.nn.sigmoid(p_bc)
        bc = p_bc * sig_bc
        keys = bc[:, :states].astype(bf16)
        queries = bc[:, states:].astype(bf16)
        queries_t = bc[:, states:].T
        above = lax.broadcasted_iota(jnp.int32, (size, size), 0) <= lax.broadcasted_iota(
            jnp.int32, (size, size), 1
        )
        scores_t = jnp.where(above, mm(keys, queries, NT), 0.0)
        lane_head = lax.broadcasted_iota(jnp.int32, (size, LANES), 1) // head_dim
        d_scores_t = jnp.zeros((size, size), f32)
        d_keys = jnp.zeros((size, states), f32)
        d_queries = jnp.zeros((size, states), f32)
        head_of = lax.broadcasted_iota(jnp.int32, (LANES, LANES), 0) // head_dim
        lane_of = lax.broadcasted_iota(jnp.int32, (LANES, LANES), 1)
        log_sum = jnp.zeros((size, LANES), f32)
        step_sum = jnp.zeros((size, LANES), f32)
        end_sum = jnp.zeros((8, LANES), f32)
        for group in range(inner // LANES):
            lanes = slice(group * LANES, (group + 1) * LANES)
            heads = [group * per_group + j for j in range(per_group)]
            p_x = pre_x[:, lanes]
            sig_x = jax.nn.sigmoid(p_x)
            x_g = p_x * sig_x
            dy = d_mixed[:, lanes]
            step_e = pick(
                [jnp.broadcast_to(steps[:, h : h + 1], (size, LANES)) for h in heads], lane_head
            )
            log_e = pick(
                [jnp.broadcast_to(logs[:, h : h + 1], (size, LANES)) for h in heads], lane_head
            )
            xs = x_g * step_e
            xs_half, dy_half = xs.astype(bf16), dy.astype(bf16)
            last = log_e[size - 1 : size, :]
            fade = jnp.exp(last - log_e)
            old = before[0, :, lanes]
            d_new = d_state[:, lanes]
            d_new_half = d_new.astype(bf16)
            dxs = fade * mm(keys, d_new_half)
            for j, h in enumerate(heads):
                mine = lane_head == j
                gap = logs_t[h : h + 1, :] - logs[:, h : h + 1]
                decay = jnp.exp(jnp.minimum(gap, 0.0))
                dxs = dxs + mm(
                    (scores_t * decay).astype(bf16), jnp.where(mine, dy_half, 0.0)
                )
                d_scores_t = d_scores_t + decay * mm(jnp.where(mine, xs_half, 0.0), dy_half, NT)
            e_dy = jnp.exp(log_e) * dy
            d_queries = d_queries + sum(mm(half, old, NT) for half in halves(e_dy))
            d_keys = d_keys + fine(fade * xs, d_new, NT)
            skip_g = skip[0:1, lanes]
            log_lane = dy * (mixed[:, lanes] - skip_g * x_g) - xs * dxs
            step_lane = dxs * x_g
            end_lane = jnp.sum(d_new * after[:, lanes], axis=0, keepdims=True)
            to_head = (head_of + group * per_group == lane_of).astype(bf16)
            for high_low in halves(log_lane):
                log_sum = log_sum + mm(high_low, to_head)
            for high_low in halves(step_lane):
                step_sum = step_sum + mm(high_low, to_head)
            for high_low in halves(jnp.broadcast_to(end_lane, (8, LANES))):
                end_sum = end_sum + mm(high_low, to_head)
            d_state[:, lanes] = jnp.exp(last) * d_new + fine(queries_t, e_dy)
            after[:, lanes] = old.astype(f32)
            grad_x[width + 1 : width + 2, lanes] += jnp.sum(dy * x_g, axis=0, keepdims=True)
            dx = dxs * step_e + skip_g * dy
            d_pre = dx * (sig_x + x_g * (1.0 - sig_x))
            ext_x[0:size, lanes] = d_pre
            grad_x[width : width + 1, lanes] += jnp.sum(d_pre, axis=0, keepdims=True)
            total = jnp.zeros((size, LANES), f32)
            raw = raw_x[:, lanes].astype(f32)
            for k in range(width):
                moved = ext_x[width - 1 - k : width - 1 - k + size, lanes]
                total = total + taps_x[k : k + 1, lanes] * moved
                grad_x[k : k + 1, lanes] += jnp.sum(raw * moved, axis=0, keepdims=True)
            columns[:, lanes] = total.astype(bf16)
            halo_x[:, lanes] = ext_x[0:8, lanes]
            ext_x[size : size + 8, lanes] = halo_x[:, lanes]
        d_scores_t = jnp.where(above, d_scores_t, 0.0)
        d_keys = d_keys + fine(d_scores_t, bc[:, states:])
        d_queries = d_queries + fine(d_scores_t.T, bc[:, :states])
        at_end = lax.broadcasted_iota(jnp.int32, (size, LANES), 0) == size - 1
        d_log = log_sum + jnp.where(at_end, end_sum[0:1, :], 0.0)
        d_rate = lax.dot_general(
            above.astype(f32), d_log, NN, precision=highest, preferred_element_type=f32
        )
        grad_head[1:2, :] += rates * jnp.sum(steps * d_rate, axis=0, keepdims=True)
        d_dt = (step_sum + rates * d_rate) * jax.nn.sigmoid(dt)
        grad_head[0:1, :] += jnp.sum(d_dt, axis=0, keepdims=True)
        columns[:, inner + twice :] = d_dt.astype(bf16)
        slope = sig_bc + bc * (1.0 - sig_bc)
        ext_bc[0:size, :states] = d_keys * slope[:, :states]
        ext_bc[0:size, states:] = d_queries * slope[:, states:]
        grad_bc[width : width + 1, :] += jnp.sum(ext_bc[0:size, :], axis=0, keepdims=True)
        total = jnp.zeros((size, twice), f32)
        raw = raw_bc[...].astype(f32)
        for k in range(width):
            moved = ext_bc[width - 1 - k : width - 1 - k + size, :]
            total = total + taps_bc[k : k + 1, :] * moved
            grad_bc[k : k + 1, :] += jnp.sum(raw * moved, axis=0, keepdims=True)
        columns[:, inner : inner + twice] = total.astype(bf16)
        halo_bc[...] = ext_bc[0:8, :]
        ext_bc[size : size + 8, :] = halo_bc[...]

    return kernel


def gate_kernel(count, pieces, parts):
    def kernel(place, *refs):
        normed_refs, upstream_refs, refs = refs[:count], refs[count : 2 * count], refs[2 * count :]
        weight_refs, refs = refs[:pieces], refs[pieces:]
        mixed, gain, gate_raw, grad_scaled, sums, normed, upstream, w_gate, w_out = refs

        @pl.when(pl.program_id(0) == 0)
        def _():
            join(w_gate, [weight_refs[k] for k in order_of(pieces)])
            join(w_out, weight_refs, w_gate.shape[1])

        take(normed, normed_refs, pl.program_id(0) // parts)
        take(upstream, upstream_refs, pl.program_id(0) // parts)
        gate_body(normed, upstream, w_gate, w_out, mixed, gain, gate_raw, grad_scaled, sums)

    return kernel


def gate_body(normed, upstream, w_gate, w_out, mixed, gain, gate_raw, grad_scaled, sums):
    gate = mm(normed[...], w_gate[...])
    grads = mm(upstream[...], w_out[...])
    gate_raw[...] = gate
    grad_scaled[...] = grads
    gated = mixed[...] * (gate * jax.nn.sigmoid(gate))
    ones = jnp.ones((8, gated.shape[1]), bf16)
    rows = lax.broadcasted_iota(jnp.int32, sums.shape[1:], 0)
    square = sum(mm(ones, part, NT) for part in halves(gated * gated))
    cross = sum(mm(ones, part, NT) for part in halves(gated * (grads * gain[...])))
    sums[0] = jnp.where(rows == 0, square, cross)


def norm_kernel(inner_total, count):
    def kernel(place, *refs):
        terms, refs = refs[:count], refs[count:]
        gate_raw, grad_scaled, mixed, gain, scaled, d_mixed, d_gate, grad_gain = refs

        @pl.when(pl.program_id(0) == 0)
        def _():
            grad_gain[...] = jnp.zeros(grad_gain.shape, f32)

        total = terms[0][0]
        for term in terms[1:]:
            total = total + term[0]
        column = total.T
        inverse = lax.rsqrt(column[:, 0:1] / inner_total + epsilon)
        pull = inverse * inverse * inverse * (column[:, 1:2] / inner_total)
        gate = gate_raw[...]
        sig = jax.nn.sigmoid(gate)
        act = gate * sig
        mix = mixed[...]
        grads = grad_scaled[...]
        unit = mix * act * inverse
        scaled[...] = (unit * gain[...]).astype(bf16)
        grad_gain[0:1, :] += jnp.sum(grads * unit, axis=0, keepdims=True)
        d_gated = inverse * (grads * gain[...]) - (mix * act) * pull
        d_mixed[...] = d_gated * act
        d_gate[...] = (d_gated * mix * (sig + act * (1.0 - sig))).astype(bf16)

    return kernel


def place_of(place, k, blocks, size):
    return pl.multiple_of(position(place[0] ^ k, blocks) * size, size)


def entry_kernel(blocks):
    def kernel(place, tokens, upstream, gain, normed_out, upstream_out):
        size = tokens.shape[1] // blocks
        wide = tokens[...].astype(f32)
        inverse = lax.rsqrt(jnp.mean(wide * wide, axis=-1, keepdims=True) + epsilon)
        normed = (wide * inverse * gain[...]).astype(bf16)
        for k in range(blocks):
            at = pl.ds(place_of(place, k, blocks, size), size)
            normed_out[:, at] = normed[:, k * size : (k + 1) * size]
            at = pl.ds(pl.multiple_of((place[0] ^ k) * size, size), size)
            upstream_out[:, at] = upstream[:, k * size : (k + 1) * size]

    return kernel


def pack_kernel(blocks, cols):
    def kernel(place, grad_x, grad_gain, grad_bc, grad_head, pre_part, gain, out, row):
        twice = grad_bc.shape[1]
        inner = grad_x.shape[1]
        model = row.shape[1]
        size = model // blocks
        out[...] = jnp.zeros(out.shape, f32)
        out[0:8, :inner] = grad_x[...]
        out[8:16, :inner] = grad_gain[...]
        out[16:24, :twice] = grad_bc[...]
        out[16:24, twice : twice + LANES] = grad_head[...]
        for k in range(blocks):
            at = pl.ds(place_of(place, k, blocks, size), size)
            row[:, k * size : (k + 1) * size] = pre_part[:, at]
        for k in range(model // cols):
            part = slice(k * cols, (k + 1) * cols)
            out[24 + k : 25 + k, :] = row[0:1, part] / gain[0:1, part]

    return kernel


def output_kernel(blocks, count):
    def kernel(place, tokens, *refs):
        out = refs[count]
        size = tokens.shape[1] // blocks
        for k in range(blocks):
            at = pl.multiple_of((place[0] ^ k) * size, size)
            total = tokens[:, k * size : (k + 1) * size].astype(f32)
            for term in refs[:count]:
                total = total + term[:, pl.ds(at, size)].astype(f32)
            out[:, 0, k * size : (k + 1) * size] = total

    return kernel


def input_kernel(blocks, count):
    def kernel(place, tokens, upstream, gain, *refs):
        out, grads = refs[count:]
        model = tokens.shape[1]
        size = model // blocks
        wide = tokens[...].astype(f32)
        inverse = lax.rsqrt(jnp.mean(wide * wide, axis=-1, keepdims=True) + epsilon)
        for k in range(blocks):
            at = place_of(place, k, blocks, size)
            total = refs[0][:, pl.ds(at, size)].astype(f32)
            for term in refs[1:count]:
                total = total + term[:, pl.ds(at, size)].astype(f32)
            grads[:, k * size : (k + 1) * size] = total
        weighted = grads[...] * gain[...]
        inner_dot = jnp.mean(weighted * wide, axis=-1, keepdims=True)
        out[:, 0, :] = (
            upstream[...].astype(f32)
            + inverse * weighted
            - wide * (inverse * inverse * inverse * inner_dot)
        )

    return kernel


def normed_kernel(place, tokens, d_gate, columns, w_gate, w_scan, own, near, grad_gain):
    total = mm(d_gate[...], w_gate[...], NT) + mm(columns[...], w_scan[...], NT)
    own[...] = total[: own.shape[0]].astype(bf16)
    near[...] = total[-near.shape[0] :].astype(bf16)
    total = total * tokens[...].astype(f32)
    grad_gain[...] = jnp.broadcast_to(jnp.sum(total, axis=0, keepdims=True), grad_gain.shape)


def whole(shape):
    return pl.BlockSpec(shape, lambda c, place: (0,) * len(shape))


def rows_of(size, cols, column=0):
    return pl.BlockSpec((size, cols), lambda c, place: (c, column))


def call(kernel, grid, ins, outs, shapes, scratch=(), aliases=None):
    return pl.pallas_call(
        kernel,
        grid_spec=pltpu.PrefetchScalarGridSpec(
            num_scalar_prefetch=1, grid=(grid,), in_specs=ins, out_specs=outs,
            scratch_shapes=scratch,
        ),
        out_shape=[jax.ShapeDtypeStruct(*one) for one in shapes],
        input_output_aliases=aliases or {},
    )


def exchange_blocks(values, axis, blocks, back=False, ordered=True):
    index = lax.axis_index(axis)
    order = order_of(blocks)
    blocked = values.reshape(values.shape[0], blocks, -1)
    if back and ordered:
        blocked = jnp.stack([blocked[:, order.index(k)] for k in range(blocks)], axis=1)
    bits = 1
    while bits < blocks:
        split = blocked.reshape(blocked.shape[0], blocks // (2 * bits), 2, -1)
        blocked = jnp.where((index & bits) != 0, split[:, :, ::-1], split)
        blocked = blocked.reshape(blocked.shape[0], blocks, -1)
        bits *= 2
    if ordered and not back:
        blocked = jnp.stack([blocked[:, k] for k in order], axis=1)
    return blocked.reshape(values.shape)


def per_device(
    block_input, pre_gain, w_zx, w_dt, w_bc, conv_x_w, conv_x_b, conv_bc_w, conv_bc_b,
    dt_bias, a_log, d_skip, gate_gain, w_out, cotangent,
):
    rows_local, seqs, model = block_input.shape
    assert seqs == 1
    dp = lax.axis_size("dp")
    tensor = lax.axis_size("tensor")
    length = rows_local * tensor
    inner = w_zx.shape[2]
    twice = w_bc.shape[1]
    states = twice // 2
    heads = w_dt.shape[1]
    head_dim = inner // heads
    width = conv_x_w.shape[0]
    wide_cols = inner + twice + LANES
    inner_total = inner * tensor
    chunk = min(CHUNK, rows_local)
    block = min(ROWS, rows_local)
    chunks = length // chunk
    place_dp = lax.axis_index("dp").astype(jnp.int32).reshape(1)
    place_tensor = lax.axis_index("tensor").astype(jnp.int32).reshape(1)
    narrow = (model // dp) % LANES != 0
    blocks = 1 if narrow else dp
    place_entry = place_dp * 0 if narrow else place_dp

    slab = rows_local
    tokens_local = block_input.reshape(rows_local, model)
    upstream_local = cotangent.reshape(rows_local, model)
    gain_in = pre_gain.reshape(1, model)
    w_scan = jnp.concatenate(
        [w_zx[:, 1, :], w_bc, w_dt, jnp.zeros((w_dt.shape[0], LANES - heads), bf16)], axis=1
    )
    w_late = jnp.concatenate([w_zx[:, 0, :], w_out.T], axis=1)
    normed_local, upstream_sent = call(
        entry_kernel(blocks), rows_local // slab,
        [rows_of(slab, model), rows_of(slab, model), whole((1, model))],
        [rows_of(slab, model)] * 2,
        [((rows_local, model), bf16)] * 2,
    )(place_entry, tokens_local, upstream_local, gain_in)
    if narrow:
        normed_local = exchange_blocks(normed_local, "dp", dp)
        upstream_sent = exchange_blocks(upstream_sent, "dp", dp, ordered=False)

    def stack(rows, cols):
        rows = [r.reshape(-1, r.shape[-1]) for r in rows]
        packed = jnp.concatenate(rows, axis=0)
        return jnp.pad(packed, ((0, 8 - packed.shape[0]), (0, cols - packed.shape[1])))

    taps_x = stack([conv_x_w, conv_x_b], inner)
    taps_bc = stack([conv_bc_w, conv_bc_b], twice)
    per_head = stack([dt_bias, -jnp.exp(a_log)], LANES)
    skip = jnp.repeat(d_skip, head_dim).reshape(1, inner)
    gain = gate_gain.reshape(1, inner)
    forward_shapes = [((states, inner), f32), ((8, inner), f32), ((8, twice), f32)]
    backward_shapes = [((8, inner), f32), ((8, twice), f32), ((8, LANES), f32)]
    backward_shapes += [((states, inner), f32)] * 2 + [((8, inner), f32), ((8, twice), f32)]
    forward_carry = [jnp.zeros(*one) for one in forward_shapes]

    scan_far = gather_far(w_scan, "dp")
    scan_far[0], taps_x, taps_bc, per_head, skip, gain, forward_carry = lax.optimization_barrier(
        (scan_far[0], taps_x, taps_bc, per_head, skip, gain, forward_carry)
    )
    scan_pieces = gather_near(scan_far, "dp")
    normed_pieces = gather(normed_local, "tensor")
    late_pieces = gather(w_late, "dp")
    upstream_pieces = gather(upstream_sent, "tensor")
    dp_order, tensor_order = order_of(dp), order_of(tensor)

    per = rows_local // chunk

    def stored(c, place):
        return position((c // per) ^ place[0], tensor) * per + c % per

    def ahead(cols, start):
        return pl.BlockSpec((chunk, cols), lambda c, place: (stored(c + start, place), 0))

    def back(cols, start):
        return pl.BlockSpec((chunk, cols), lambda c, place: (stored(start - c, place), 0))

    def token_piece(k, start):
        def index(c, place):
            c = c + start
            return jnp.where((c // per) ^ place[0] == k, c % per, 0), 0

        return pl.BlockSpec((chunk, model), index)

    anywhere = pl.BlockSpec(memory_space=pl.ANY)
    calls = 2 if chunks % 2 == 0 else 1
    span = chunks // calls
    first = -(-chunks * 5 // 8)
    carry = forward_carry
    saved, weights = [], [scan_pieces[k] for k in dp_order]
    for start, stop in ((0, first), (first, chunks)):
        results = call(
            forward_kernel(width, head_dim, tensor, len(weights), per, start),
            stop - start,
            [token_piece(k, start) for k in range(tensor)]
            + [whole(one.shape) for one in weights]
            + [whole((8, inner)), whole((8, twice)), whole((8, LANES)), whole((1, inner))]
            + [whole(one.shape) for one in carry]
            + [anywhere] * len(saved),
            [ahead(cols, start) for cols in (inner, twice, inner, twice, LANES, inner)]
            + [pl.BlockSpec((1, states, inner), lambda c, place, start=start: (c + start, 0, 0))]
            + [whole(one.shape) for one in carry]
            + [whole((model, wide_cols))] * (start == 0),
            [
                ((length, inner), f32), ((length, twice), f32), ((length, inner), bf16),
                ((length, twice), bf16), ((length, LANES), f32), ((length, inner), f32),
                ((chunks, states, inner), bf16), *forward_shapes,
            ]
            + [((model, wide_cols), bf16)] * (start == 0),
            [
                pltpu.VMEM((chunk + 8, inner), f32), pltpu.VMEM((chunk + 8, twice), f32),
                pltpu.VMEM((chunk, model), bf16),
            ],
            {1 + tensor + len(weights) + 7 + k: k for k in range(len(saved))},
        )(place_tensor, *normed_pieces, *weights, taps_x, taps_bc, per_head, skip, *carry, *saved)
        saved, carry = results[:7], results[7:10]
        if start == 0:
            full_scan = results[10]
            weights = [full_scan]
    pre_x, pre_bc, raw_x, raw_bc, dt, mixed, before = saved

    parts = rows_local // block
    in_order = pl.BlockSpec(
        (1, 8, block), lambda c, place: ((at_position(c // parts, tensor) ^ place[0]) * parts + c % parts, 0, 0)
    )

    def gate_piece(p):
        return pl.BlockSpec(
            (block, model), lambda c, place: (jnp.where(c // parts == p, c % parts, 0), 0)
        )

    gate_raw, grad_scaled, sums, normed, upstream, full_gate, full_out = call(
        gate_kernel(tensor, dp, parts), length // block,
        [gate_piece(p) for p in range(tensor)] * 2
        + [whole((model // dp, 2 * inner))] * dp
        + [rows_of(block, inner), whole((1, inner))],
        [
            rows_of(block, inner), rows_of(block, inner), in_order, rows_of(block, model),
            rows_of(block, model), whole((model, inner)), whole((model, inner)),
        ],
        [
            ((length, inner), f32), ((length, inner), f32), ((length // block, 8, block), f32),
            ((length, model), bf16), ((length, model), bf16), ((model, inner), bf16),
            ((model, inner), bf16),
        ],
    )(
        place_tensor, *[normed_pieces[k] for k in tensor_order],
        *[upstream_pieces[k] for k in tensor_order], *late_pieces,
        mixed, gain,
    )

    sum_terms = direct_terms(sums, "tensor")

    scaled, d_mixed, d_gate, grad_gain = call(
        norm_kernel(inner_total, tensor), length // block,
        [in_order] * tensor
        + [rows_of(block, inner), rows_of(block, inner), rows_of(block, inner), whole((1, inner))],
        [rows_of(block, inner), rows_of(block, inner), rows_of(block, inner), whole((8, inner))],
        [
            ((length, inner), bf16), ((length, inner), f32), ((length, inner), bf16),
            ((8, inner), f32),
        ],
    )(place_tensor, *sum_terms, gate_raw, grad_scaled, mixed, gain)

    def tn(left, right):
        return lax.dot_general(left, right, TN, preferred_element_type=f32).astype(bf16)

    share = model // dp
    out_pairs = [tn(upstream[:, k * share : (k + 2) * share], scaled) for k in range(0, dp, 2)]
    even = share * ((dp + 1) // 2)
    gate_near = tn(normed[:, even:], d_gate)
    gate_own = tn(normed[:, :even], d_gate)
    stay = rows_local * ((tensor + 1) // 2)
    branch_near = mm(scaled[stay:], full_out, NT).astype(bf16)
    branch_own = mm(scaled[:stay], full_out, NT).astype(bf16)
    out_terms = far_first(out_pairs, "dp")
    gate_terms = near_first(gate_own, [gate_near], "dp")
    branch_terms = near_first(branch_own, [branch_near], "tensor")
    if narrow:
        branch_terms = [
            (exchange_blocks(array, "dp", dp, True, False), k) for array, k in branch_terms
        ]
    slabs = rows_local // slab
    out_block = pl.BlockSpec((slab, 1, model), lambda c, place: (c, 0, 0))

    def one_block(k):
        return pl.BlockSpec((slab, model), lambda c, place: (k * slabs + c, 0))

    (block_output,) = call(
        output_kernel(blocks, len(branch_terms)), slabs,
        [rows_of(slab, model)] + [one_block(k) for _, k in branch_terms],
        [out_block],
        [((rows_local, 1, model), f32)],
    )(place_entry, tokens_local, *[array for array, _ in branch_terms])

    carry = [jnp.zeros(*one) for one in backward_shapes]
    columns = []
    for at in range(calls):
        start = chunks - 1 - at * span
        columns, *carry = call(
            backward_kernel(width, head_dim, len(columns)), span,
            [back(cols, start) for cols in (inner, inner, twice, inner, twice, LANES, inner)]
            + [pl.BlockSpec((1, states, inner), lambda c, place, start=start: (start - c, 0, 0))]
            + [whole((8, inner)), whole((8, twice)), whole((8, LANES)), whole((1, inner))]
            + [whole(one.shape) for one in carry]
            + [anywhere] * len(columns),
            [back(wide_cols, start)] + [whole(one.shape) for one in carry],
            [((length, wide_cols), bf16), *backward_shapes],
            [pltpu.VMEM((chunk + 8, inner), f32), pltpu.VMEM((chunk + 8, twice), f32)],
            {1 + 8 + 4 + 7: 0} if columns else {},
        )(
            place_tensor, d_mixed, pre_x, pre_bc, raw_x, raw_bc, dt, mixed, before, taps_x,
            taps_bc, per_head, skip, *carry, *columns,
        )
        columns = [columns]
    columns = columns[0]
    grad_x, grad_bc, grad_head = carry[:3]

    later = even + (model - even) // 2 if dp % 4 == 0 else even
    scan_near = [tn(normed[:, later:], columns)]
    if later > even:
        scan_near.append(tn(normed[:, even:later], columns))
    scan_own = tn(normed[:, :even], columns)
    scan_terms = near_first(scan_own, scan_near, "dp")
    features = model // 4
    leave = max(length - stay, rows_local)
    normed_own, normed_near, pre_part = call(
        normed_kernel, 4,
        [
            pl.BlockSpec((length, features), lambda c, place: (0, c)),
            whole((length, inner)), whole((length, wide_cols)),
            rows_of(features, inner), rows_of(features, wide_cols),
        ],
        [
            pl.BlockSpec((stay, features), lambda c, place: (0, c)),
            pl.BlockSpec((leave, features), lambda c, place: (0, c)),
            pl.BlockSpec((8, features), lambda c, place: (0, c)),
        ],
        [((stay, model), bf16), ((leave, model), bf16), ((8, model), f32)],
    )(place_tensor, normed, d_gate, columns, full_gate, full_scan)
    normed_terms = near_first(normed_own, [normed_near], "tensor")
    if narrow:
        normed_terms = [(exchange_blocks(array, "dp", dp, True), k) for array, k in normed_terms]
    (input_grad,) = call(
        input_kernel(blocks, len(normed_terms)), slabs,
        [rows_of(slab, model)] * 2 + [whole((1, model))]
        + [one_block(k) for _, k in normed_terms],
        [out_block], [((rows_local, 1, model), f32)], [pltpu.VMEM((slab, model), f32)],
    )(place_entry, tokens_local, upstream_local, gain_in, *[array for array, _ in normed_terms])

    grad_w_scan = sum(block_of(term, share) for term in scan_terms)
    grad_w_out = sum(block_of(term, share) for term in out_terms).T
    grad_w_gate = sum(block_of(term, share) for term in gate_terms)
    cols = max(inner, twice + LANES)
    cols += -cols % 512
    if narrow:
        pre_part = exchange_blocks(pre_part, "dp", dp, True)
    rows = 24 + max(model // cols, 8)
    (packed,) = call(
        pack_kernel(blocks, cols), 1,
        [
            whole((8, inner)), whole((8, inner)), whole((8, twice)), whole((8, LANES)),
            whole((8, model)), whole((1, model)),
        ],
        [whole((rows, cols))], [((rows, cols), f32)], [pltpu.VMEM((8, model), f32)],
    )(place_entry, grad_x, grad_gain, grad_bc, grad_head, pre_part, gain_in)
    small = all_sum(packed, "dp")

    assert cols % twice == 0 and model % cols == 0
    across = [small[16:, k : k + twice] for k in range(0, cols, twice)]
    across = jnp.concatenate(across, axis=0)
    keys_rows = grad_w_scan.shape[0]
    across = jnp.concatenate([grad_w_scan[:, inner : inner + twice], across], axis=0)
    across = total_of(direct_terms(across, "tensor"))
    grad_w_bc = across[:keys_rows]
    of_bc = across[keys_rows:]
    count = rows - 16
    pre_rows = [of_bc[k * count + 8 : k * count + 8 + model // cols] for k in range(cols // twice)]
    sum_pre = jnp.concatenate(pre_rows, axis=1).reshape(-1)
    grad_w_dt = grad_w_scan[:, inner + twice : inner + twice + heads]
    grad_w_zx = jnp.stack([grad_w_gate, grad_w_scan[:, :inner]], axis=1)
    of_x = small[:8, :inner]
    sum_gain = small[8, :inner]
    of_head = small[16:24, twice : twice + LANES]
    return (
        block_output,
        input_grad,
        sum_pre,
        grad_w_zx,
        grad_w_dt,
        grad_w_bc,
        of_x[:width],
        of_x[width],
        of_bc[:width],
        of_bc[width],
        of_head[0, :heads],
        of_head[1, :heads],
        of_x[width + 1].reshape(heads, head_dim).sum(axis=1),
        sum_gain,
        grad_w_out,
    )


def solution(mesh):
    placed = (
        P("tensor", "dp", None), P(), P("dp", None, "tensor"), P("dp", "tensor"), P("dp", None),
        P(None, "tensor"), P("tensor"), P(), P(), P("tensor"), P("tensor"), P("tensor"),
        P("tensor"), P("tensor", "dp"), P("tensor", "dp", None),
    )
    results = (
        P("tensor", "dp", None), P("tensor", "dp", None), P(), P("dp", None, "tensor"),
        P("dp", "tensor"), P("dp", None), P(None, "tensor"), P("tensor"), P(), P(), P("tensor"),
        P("tensor"), P("tensor"), P("tensor"), P("tensor", "dp"),
    )

    return jax.shard_map(per_device, mesh=mesh, in_specs=placed, out_specs=results, check_vma=False)
```

```python
import jax
import jax.numpy as jnp
from jax import lax
from jax.experimental import pallas as pl
from jax.experimental.pallas import tpu as pltpu
from jax.sharding import PartitionSpec as P


DP, TP = "dp", "tensor"

CHUNK = 128
ROWS = 256
LANES = 128
epsilon = 1e-05
highest = lax.Precision.HIGHEST
f32 = jnp.float32
bf16 = jnp.bfloat16

NN = (((1,), (0,)), ((), ()))
NT = (((1,), (1,)), ((), ()))
TN = (((0,), (0,)), ((), ()))


def mm(a, b, dims=NN):
    return lax.dot_general(a, b, dims, preferred_element_type=f32)


def halves(v):
    high = v.astype(bf16)
    return high, (v - high.astype(f32)).astype(bf16)


def fine(a, b, dims=NN):
    a_high, a_low = halves(a)
    b_high, b_low = halves(b)
    return mm(a_high, b_high, dims) + mm(a_high, b_low, dims) + mm(a_low, b_high, dims)


def swap(value, axis, bits):
    size = lax.axis_size(axis)
    return lax.ppermute(value, axis, [(i, i ^ bits) for i in range(size)])


def order_of(size):
    return list(range(0, size, 2)) + list(range(1, size, 2))


def position(k, size):
    return k // 2 + (k % 2) * ((size + 1) // 2)


def at_position(p, size):
    half = (size + 1) // 2
    return jnp.where(p < half, 2 * p, 2 * (p - half) + 1)


def gather_far(value, axis):
    pieces = {0: value}
    for k in range(2, lax.axis_size(axis), 2):
        pieces[k] = swap(value, axis, k)
    return pieces


def gather_near(pieces, axis):
    size = lax.axis_size(axis)
    pieces = dict(pieces)
    if size > 1:
        for k in range(0, size, 2):
            pieces[k ^ 1] = swap(pieces[k], axis, 1)
    return [pieces[k] for k in range(size)]


def gather(value, axis):
    return gather_near(gather_far(value, axis), axis)


def near_first(own, near, axis):
    size = lax.axis_size(axis)
    if size == 1:
        return [(own, 0)]
    half = size // 2
    rows = own.shape[0] // half
    terms = [(own, 0)]
    sent_on = []
    start = half
    for sent in near:
        other = swap(sent, axis, 1)
        other, *_ = lax.optimization_barrier((other, *sent_on))
        stop, start = start, start - sent.shape[0] // rows
        for i in range(stop - 1, start - 1, -1):
            if i == 0:
                terms.append((other, 0))
                continue
            got = other[(i - start) * rows : (i - start + 1) * rows]
            both = own[i * rows : (i + 1) * rows].astype(f32) + got.astype(f32)
            sent_on.append(both.astype(bf16))
            terms.append((swap(sent_on[-1], axis, 2 * i), 0))
    return terms


def far_first(pairs, axis):
    if lax.axis_size(axis) == 1:
        return [(pairs[0], 0)]
    rows = pairs[0].shape[0] // 2
    got = [pairs[0]]
    for i in range(1, len(pairs)):
        got.append(swap(pairs[i], axis, 2 * i))
    other = sum(both[rows:].astype(f32) for both in got).astype(bf16)
    return [(both, 0) for both in got] + [(swap(other, axis, 1), 0)]


def block_of(term, rows):
    array, index = term
    return array[index * rows : (index + 1) * rows].astype(f32)


def total_of(terms):
    return sum(term.astype(f32) for term in terms)


def direct_terms(value, axis):
    terms = [value]
    for k in range(1, lax.axis_size(axis)):
        terms.append(swap(value, axis, k))
    return terms


def all_sum(value, axis):
    size = lax.axis_size(axis)
    if size == 1:
        return value
    value = value + swap(value, axis, 1)
    total = value
    for k in range(2, size, 2):
        total = total + swap(value, axis, k)
    return total


def softplus(v):
    return jnp.maximum(v, 0.0) + jnp.log1p(jnp.exp(-jnp.abs(v)))


def lower(size):
    return lax.broadcasted_iota(jnp.int32, (size, size), 0) >= lax.broadcasted_iota(
        jnp.int32, (size, size), 1
    )


def pick(values, lane_head):
    out = values[0]
    for j in range(1, len(values)):
        out = jnp.where(lane_head == j, values[j], out)
    return out


def take(out, refs, which):
    for k, ref in enumerate(refs):

        @pl.when(which == k)
        def _(ref=ref):
            out[...] = ref[...]


def join(out, refs, start=0):
    rows = refs[0].shape[0]
    cols = out.shape[1]
    for k, ref in enumerate(refs):
        out[k * rows : (k + 1) * rows, :] = ref[:, start : start + cols]


def forward_kernel(width, head_dim, count, pieces, per, start):
    per_group = LANES // head_dim

    def kernel(place, *refs):
        token_refs, refs = refs[:count], refs[count:]
        weight_refs, refs = refs[:pieces], refs[pieces:]
        taps_x, taps_bc, per_head, skip, *refs = refs
        if start:
            carried, refs = refs[:3], refs[10:]
        pre_x, pre_bc, raw_x, raw_bc, dt_out, mixed, before, state, halo_x, halo_bc = refs[:10]
        if start == 0:
            weights, refs = refs[10], refs[11:]
        else:
            weights, refs = weight_refs[0], refs[10:]
        ext_x, ext_bc, normed = refs
        size = normed.shape[0]
        take(normed, token_refs, ((pl.program_id(0) + start) // per) ^ place[0])
        inner = mixed.shape[1]
        twice = pre_bc.shape[1]
        states = twice // 2

        @pl.when(pl.program_id(0) == 0)
        def _():
            if start:
                state[...] = carried[0][...]
                ext_x[0:8, :] = carried[1][...]
                ext_bc[0:8, :] = carried[2][...]
            else:
                state[...] = jnp.zeros(state.shape, f32)
                ext_x[0:8, :] = jnp.zeros((8, inner), f32)
                ext_bc[0:8, :] = jnp.zeros((8, twice), f32)
                join(weights, weight_refs)

        raw = mm(normed[...], weights[...])

        def conv(ext, values, taps, raw_ref, pre_ref, halo):
            ext[8 : 8 + size, :] = values
            raw_ref[...] = values.astype(bf16)
            total = taps[width : width + 1, :]
            for k in range(width):
                start = 8 - (width - 1) + k
                total = total + taps[k : k + 1, :] * ext[start : start + size, :]
            halo[...] = ext[size : size + 8, :]
            ext[0:8, :] = halo[...]
            pre_ref[...] = total
            return total * jax.nn.sigmoid(total)

        x = conv(ext_x, raw[:, :inner], taps_x, raw_x, pre_x, halo_x)
        bc = conv(ext_bc, raw[:, inner : inner + twice], taps_bc, raw_bc, pre_bc, halo_bc)
        dt = raw[:, inner + twice :] + per_head[0:1, :]
        dt_out[...] = dt
        steps = softplus(dt)
        below = lower(size)
        logs = lax.dot_general(
            below.astype(f32), steps * per_head[1:2, :], NN, precision=highest,
            preferred_element_type=f32,
        )
        logs_t = logs.T
        keys = bc[:, :states]
        keys_t = keys.T
        queries = bc[:, states:]
        scores = jnp.where(below, fine(queries, keys, NT), 0.0)
        lane_head = lax.broadcasted_iota(jnp.int32, (size, LANES), 1) // head_dim
        for group in range(inner // LANES):
            lanes = slice(group * LANES, (group + 1) * LANES)
            x_g = x[:, lanes]
            heads = [group * per_group + j for j in range(per_group)]
            step_e = pick(
                [jnp.broadcast_to(steps[:, h : h + 1], (size, LANES)) for h in heads], lane_head
            )
            log_e = pick(
                [jnp.broadcast_to(logs[:, h : h + 1], (size, LANES)) for h in heads], lane_head
            )
            xs = x_g * step_e
            xs_half = xs.astype(bf16)
            total = skip[0:1, lanes] * x_g
            for j, h in enumerate(heads):
                gap = logs[:, h : h + 1] - logs_t[h : h + 1, :]
                weights_h = (scores * jnp.exp(jnp.minimum(gap, 0.0))).astype(bf16)
                total = total + mm(weights_h, jnp.where(lane_head == j, xs_half, 0.0))
            old = state[:, lanes]
            before[0, :, lanes] = old.astype(bf16)
            total = total + jnp.exp(log_e) * fine(queries, old)
            mixed[:, lanes] = total
            last = log_e[size - 1 : size, :]
            fresh = fine(keys_t, jnp.exp(last - log_e) * xs)
            state[:, lanes] = jnp.exp(last) * old + fresh

    return kernel


def backward_kernel(width, head_dim, resumed):
    per_group = LANES // head_dim

    def kernel(place, *refs):
        d_mixed, pre_x, pre_bc, raw_x, raw_bc, dt_in, mixed, before, *refs = refs
        taps_x, taps_bc, per_head, skip, *refs = refs
        if resumed:
            carried, refs = refs[:7], refs[8:]
        columns, *results, ext_x, ext_bc = refs
        grad_x, grad_bc, grad_head, d_state, after, halo_x, halo_bc = results
        size = d_mixed.shape[0]
        inner = d_mixed.shape[1]
        twice = pre_bc.shape[1]
        states = twice // 2

        @pl.when(pl.program_id(0) == 0)
        def _():
            for k, result in enumerate(results):
                result[...] = carried[k][...] if resumed else jnp.zeros(result.shape, f32)
            ext_x[size : size + 8, :] = halo_x[...]
            ext_bc[size : size + 8, :] = halo_bc[...]

        dt = dt_in[...]
        steps = softplus(dt)
        rates = per_head[1:2, :]
        below = lower(size)
        logs = lax.dot_general(
            below.astype(f32), steps * rates, NN, precision=highest, preferred_element_type=f32
        )
        logs_t = logs.T
        p_bc = pre_bc[...]
        sig_bc = jax.nn.sigmoid(p_bc)
        bc = p_bc * sig_bc
        keys = bc[:, :states].astype(bf16)
        queries = bc[:, states:].astype(bf16)
        queries_t = bc[:, states:].T
        above = lax.broadcasted_iota(jnp.int32, (size, size), 0) <= lax.broadcasted_iota(
            jnp.int32, (size, size), 1
        )
        scores_t = jnp.where(above, mm(keys, queries, NT), 0.0)
        lane_head = lax.broadcasted_iota(jnp.int32, (size, LANES), 1) // head_dim
        d_scores_t = jnp.zeros((size, size), f32)
        d_keys = jnp.zeros((size, states), f32)
        d_queries = jnp.zeros((size, states), f32)
        head_of = lax.broadcasted_iota(jnp.int32, (LANES, LANES), 0) // head_dim
        lane_of = lax.broadcasted_iota(jnp.int32, (LANES, LANES), 1)
        log_sum = jnp.zeros((size, LANES), f32)
        step_sum = jnp.zeros((size, LANES), f32)
        end_sum = jnp.zeros((8, LANES), f32)
        for group in range(inner // LANES):
            lanes = slice(group * LANES, (group + 1) * LANES)
            heads = [group * per_group + j for j in range(per_group)]
            p_x = pre_x[:, lanes]
            sig_x = jax.nn.sigmoid(p_x)
            x_g = p_x * sig_x
            dy = d_mixed[:, lanes]
            step_e = pick(
                [jnp.broadcast_to(steps[:, h : h + 1], (size, LANES)) for h in heads], lane_head
            )
            log_e = pick(
                [jnp.broadcast_to(logs[:, h : h + 1], (size, LANES)) for h in heads], lane_head
            )
            xs = x_g * step_e
            xs_half, dy_half = xs.astype(bf16), dy.astype(bf16)
            last = log_e[size - 1 : size, :]
            fade = jnp.exp(last - log_e)
            old = before[0, :, lanes]
            d_new = d_state[:, lanes]
            d_new_half = d_new.astype(bf16)
            dxs = fade * mm(keys, d_new_half)
            for j, h in enumerate(heads):
                mine = lane_head == j
                gap = logs_t[h : h + 1, :] - logs[:, h : h + 1]
                decay = jnp.exp(jnp.minimum(gap, 0.0))
                dxs = dxs + mm(
                    (scores_t * decay).astype(bf16), jnp.where(mine, dy_half, 0.0)
                )
                d_scores_t = d_scores_t + decay * mm(jnp.where(mine, xs_half, 0.0), dy_half, NT)
            e_dy = jnp.exp(log_e) * dy
            d_queries = d_queries + sum(mm(half, old, NT) for half in halves(e_dy))
            d_keys = d_keys + fine(fade * xs, d_new, NT)
            skip_g = skip[0:1, lanes]
            log_lane = dy * (mixed[:, lanes] - skip_g * x_g) - xs * dxs
            step_lane = dxs * x_g
            end_lane = jnp.sum(d_new * after[:, lanes], axis=0, keepdims=True)
            to_head = (head_of + group * per_group == lane_of).astype(bf16)
            for high_low in halves(log_lane):
                log_sum = log_sum + mm(high_low, to_head)
            for high_low in halves(step_lane):
                step_sum = step_sum + mm(high_low, to_head)
            for high_low in halves(jnp.broadcast_to(end_lane, (8, LANES))):
                end_sum = end_sum + mm(high_low, to_head)
            d_state[:, lanes] = jnp.exp(last) * d_new + fine(queries_t, e_dy)
            after[:, lanes] = old.astype(f32)
            grad_x[width + 1 : width + 2, lanes] += jnp.sum(dy * x_g, axis=0, keepdims=True)
            dx = dxs * step_e + skip_g * dy
            d_pre = dx * (sig_x + x_g * (1.0 - sig_x))
            ext_x[0:size, lanes] = d_pre
            grad_x[width : width + 1, lanes] += jnp.sum(d_pre, axis=0, keepdims=True)
            total = jnp.zeros((size, LANES), f32)
            raw = raw_x[:, lanes].astype(f32)
            for k in range(width):
                moved = ext_x[width - 1 - k : width - 1 - k + size, lanes]
                total = total + taps_x[k : k + 1, lanes] * moved
                grad_x[k : k + 1, lanes] += jnp.sum(raw * moved, axis=0, keepdims=True)
            columns[:, lanes] = total.astype(bf16)
            halo_x[:, lanes] = ext_x[0:8, lanes]
            ext_x[size : size + 8, lanes] = halo_x[:, lanes]
        d_scores_t = jnp.where(above, d_scores_t, 0.0)
        d_keys = d_keys + fine(d_scores_t, bc[:, states:])
        d_queries = d_queries + fine(d_scores_t.T, bc[:, :states])
        at_end = lax.broadcasted_iota(jnp.int32, (size, LANES), 0) == size - 1
        d_log = log_sum + jnp.where(at_end, end_sum[0:1, :], 0.0)
        d_rate = lax.dot_general(
            above.astype(f32), d_log, NN, precision=highest, preferred_element_type=f32
        )
        grad_head[1:2, :] += rates * jnp.sum(steps * d_rate, axis=0, keepdims=True)
        d_dt = (step_sum + rates * d_rate) * jax.nn.sigmoid(dt)
        grad_head[0:1, :] += jnp.sum(d_dt, axis=0, keepdims=True)
        columns[:, inner + twice :] = d_dt.astype(bf16)
        slope = sig_bc + bc * (1.0 - sig_bc)
        ext_bc[0:size, :states] = d_keys * slope[:, :states]
        ext_bc[0:size, states:] = d_queries * slope[:, states:]
        grad_bc[width : width + 1, :] += jnp.sum(ext_bc[0:size, :], axis=0, keepdims=True)
        total = jnp.zeros((size, twice), f32)
        raw = raw_bc[...].astype(f32)
        for k in range(width):
            moved = ext_bc[width - 1 - k : width - 1 - k + size, :]
            total = total + taps_bc[k : k + 1, :] * moved
            grad_bc[k : k + 1, :] += jnp.sum(raw * moved, axis=0, keepdims=True)
        columns[:, inner : inner + twice] = total.astype(bf16)
        halo_bc[...] = ext_bc[0:8, :]
        ext_bc[size : size + 8, :] = halo_bc[...]

    return kernel


def gate_kernel(count, pieces, parts):
    def kernel(place, *refs):
        normed_refs, upstream_refs, refs = refs[:count], refs[count : 2 * count], refs[2 * count :]
        weight_refs, refs = refs[:pieces], refs[pieces:]
        mixed, gain, gate_raw, grad_scaled, sums, normed, upstream, w_gate, w_out = refs

        @pl.when(pl.program_id(0) == 0)
        def _():
            join(w_gate, [weight_refs[k] for k in order_of(pieces)])
            join(w_out, weight_refs, w_gate.shape[1])

        take(normed, normed_refs, pl.program_id(0) // parts)
        take(upstream, upstream_refs, pl.program_id(0) // parts)
        gate_body(normed, upstream, w_gate, w_out, mixed, gain, gate_raw, grad_scaled, sums)

    return kernel


def gate_body(normed, upstream, w_gate, w_out, mixed, gain, gate_raw, grad_scaled, sums):
    gate = mm(normed[...], w_gate[...])
    grads = mm(upstream[...], w_out[...])
    gate_raw[...] = gate
    grad_scaled[...] = grads
    gated = mixed[...] * (gate * jax.nn.sigmoid(gate))
    ones = jnp.ones((8, gated.shape[1]), bf16)
    rows = lax.broadcasted_iota(jnp.int32, sums.shape[1:], 0)
    square = sum(mm(ones, part, NT) for part in halves(gated * gated))
    cross = sum(mm(ones, part, NT) for part in halves(gated * (grads * gain[...])))
    sums[0] = jnp.where(rows == 0, square, cross)


def norm_kernel(inner_total, count):
    def kernel(place, *refs):
        terms, refs = refs[:count], refs[count:]
        gate_raw, grad_scaled, mixed, gain, scaled, d_mixed, d_gate, grad_gain = refs

        @pl.when(pl.program_id(0) == 0)
        def _():
            grad_gain[...] = jnp.zeros(grad_gain.shape, f32)

        total = terms[0][0]
        for term in terms[1:]:
            total = total + term[0]
        column = total.T
        inverse = lax.rsqrt(column[:, 0:1] / inner_total + epsilon)
        pull = inverse * inverse * inverse * (column[:, 1:2] / inner_total)
        gate = gate_raw[...]
        sig = jax.nn.sigmoid(gate)
        act = gate * sig
        mix = mixed[...]
        grads = grad_scaled[...]
        unit = mix * act * inverse
        scaled[...] = (unit * gain[...]).astype(bf16)
        grad_gain[0:1, :] += jnp.sum(grads * unit, axis=0, keepdims=True)
        d_gated = inverse * (grads * gain[...]) - (mix * act) * pull
        d_mixed[...] = d_gated * act
        d_gate[...] = (d_gated * mix * (sig + act * (1.0 - sig))).astype(bf16)

    return kernel


def place_of(place, k, blocks, size):
    return pl.multiple_of(position(place[0] ^ k, blocks) * size, size)


def entry_kernel(blocks):
    def kernel(place, tokens, upstream, gain, normed_out, upstream_out):
        size = tokens.shape[1] // blocks
        wide = tokens[...].astype(f32)
        inverse = lax.rsqrt(jnp.mean(wide * wide, axis=-1, keepdims=True) + epsilon)
        normed = (wide * inverse * gain[...]).astype(bf16)
        for k in range(blocks):
            at = pl.ds(place_of(place, k, blocks, size), size)
            normed_out[:, at] = normed[:, k * size : (k + 1) * size]
            at = pl.ds(pl.multiple_of((place[0] ^ k) * size, size), size)
            upstream_out[:, at] = upstream[:, k * size : (k + 1) * size]

    return kernel


def pack_kernel(blocks, cols):
    def kernel(place, grad_x, grad_gain, grad_bc, grad_head, pre_part, gain, out, row):
        twice = grad_bc.shape[1]
        inner = grad_x.shape[1]
        model = row.shape[1]
        size = model // blocks
        out[...] = jnp.zeros(out.shape, f32)
        out[0:8, :inner] = grad_x[...]
        out[8:16, :inner] = grad_gain[...]
        out[16:24, :twice] = grad_bc[...]
        out[16:24, twice : twice + LANES] = grad_head[...]
        for k in range(blocks):
            at = pl.ds(place_of(place, k, blocks, size), size)
            row[:, k * size : (k + 1) * size] = pre_part[:, at]
        for k in range(model // cols):
            part = slice(k * cols, (k + 1) * cols)
            out[24 + k : 25 + k, :] = row[0:1, part] / gain[0:1, part]

    return kernel


def output_kernel(blocks, count):
    def kernel(place, tokens, *refs):
        out = refs[count]
        size = tokens.shape[1] // blocks
        for k in range(blocks):
            at = pl.multiple_of((place[0] ^ k) * size, size)
            total = tokens[:, k * size : (k + 1) * size].astype(f32)
            for term in refs[:count]:
                total = total + term[:, pl.ds(at, size)].astype(f32)
            out[:, 0, k * size : (k + 1) * size] = total

    return kernel


def input_kernel(blocks, count):
    def kernel(place, tokens, upstream, gain, *refs):
        out, grads = refs[count:]
        model = tokens.shape[1]
        size = model // blocks
        wide = tokens[...].astype(f32)
        inverse = lax.rsqrt(jnp.mean(wide * wide, axis=-1, keepdims=True) + epsilon)
        for k in range(blocks):
            at = place_of(place, k, blocks, size)
            total = refs[0][:, pl.ds(at, size)].astype(f32)
            for term in refs[1:count]:
                total = total + term[:, pl.ds(at, size)].astype(f32)
            grads[:, k * size : (k + 1) * size] = total
        weighted = grads[...] * gain[...]
        inner_dot = jnp.mean(weighted * wide, axis=-1, keepdims=True)
        out[:, 0, :] = (
            upstream[...].astype(f32)
            + inverse * weighted
            - wide * (inverse * inverse * inverse * inner_dot)
        )

    return kernel


def normed_kernel(place, tokens, d_gate, columns, w_gate, w_scan, own, near, grad_gain):
    total = mm(d_gate[...], w_gate[...], NT) + mm(columns[...], w_scan[...], NT)
    own[...] = total[: own.shape[0]].astype(bf16)
    near[...] = total[-near.shape[0] :].astype(bf16)
    total = total * tokens[...].astype(f32)
    grad_gain[...] = jnp.broadcast_to(jnp.sum(total, axis=0, keepdims=True), grad_gain.shape)


def product_kernel(bounds):
    def kernel(place, left, right, *outs):
        at = pl.program_id(0)
        value = mm(left[...], right[...], TN).astype(bf16)
        for i, out in enumerate(outs):

            @pl.when((at >= bounds[i]) & (at < bounds[i + 1]))
            def _(out=out):
                out[...] = value

    return kernel


def whole(shape):
    return pl.BlockSpec(shape, lambda c, place: (0,) * len(shape))


def rows_of(size, cols, column=0):
    return pl.BlockSpec((size, cols), lambda c, place: (c, column))


def call(kernel, grid, ins, outs, shapes, scratch=(), aliases=None):
    return pl.pallas_call(
        kernel,
        grid_spec=pltpu.PrefetchScalarGridSpec(
            num_scalar_prefetch=1, grid=(grid,), in_specs=ins, out_specs=outs,
            scratch_shapes=scratch,
        ),
        out_shape=[jax.ShapeDtypeStruct(*one) for one in shapes],
        input_output_aliases=aliases or {},
    )


def exchange_blocks(values, axis, blocks, back=False, ordered=True):
    index = lax.axis_index(axis)
    order = order_of(blocks)
    blocked = values.reshape(values.shape[0], blocks, -1)
    if back and ordered:
        blocked = jnp.stack([blocked[:, order.index(k)] for k in range(blocks)], axis=1)
    bits = 1
    while bits < blocks:
        split = blocked.reshape(blocked.shape[0], blocks // (2 * bits), 2, -1)
        blocked = jnp.where((index & bits) != 0, split[:, :, ::-1], split)
        blocked = blocked.reshape(blocked.shape[0], blocks, -1)
        bits *= 2
    if ordered and not back:
        blocked = jnp.stack([blocked[:, k] for k in order], axis=1)
    return blocked.reshape(values.shape)


def per_device(
    block_input, pre_gain, w_zx, w_dt, w_bc, conv_x_w, conv_x_b, conv_bc_w, conv_bc_b,
    dt_bias, a_log, d_skip, gate_gain, w_out, cotangent,
):
    rows_local, seqs, model = block_input.shape
    assert seqs == 1
    dp = lax.axis_size(DP)
    tensor = lax.axis_size(TP)
    length = rows_local * tensor
    inner = w_zx.shape[2]
    twice = w_bc.shape[1]
    states = twice // 2
    heads = w_dt.shape[1]
    head_dim = inner // heads
    width = conv_x_w.shape[0]
    wide_cols = inner + twice + LANES
    inner_total = inner * tensor
    chunk = min(CHUNK, rows_local)
    block = min(ROWS, rows_local)
    chunks = length // chunk
    place_dp = lax.axis_index(DP).astype(jnp.int32).reshape(1)
    place_tensor = lax.axis_index(TP).astype(jnp.int32).reshape(1)
    narrow = (model // dp) % LANES != 0
    blocks = 1 if narrow else dp
    place_entry = place_dp * 0 if narrow else place_dp

    slab = rows_local
    tokens_local = block_input.reshape(rows_local, model)
    upstream_local = cotangent.reshape(rows_local, model)
    gain_in = pre_gain.reshape(1, model)
    w_scan = jnp.concatenate(
        [w_zx[:, 1, :], w_bc, w_dt, jnp.zeros((w_dt.shape[0], LANES - heads), bf16)], axis=1
    )
    w_late = jnp.concatenate([w_zx[:, 0, :], w_out.T], axis=1)
    normed_local, upstream_sent = call(
        entry_kernel(blocks), rows_local // slab,
        [rows_of(slab, model), rows_of(slab, model), whole((1, model))],
        [rows_of(slab, model)] * 2,
        [((rows_local, model), bf16)] * 2,
    )(place_entry, tokens_local, upstream_local, gain_in)
    if narrow:
        normed_local = exchange_blocks(normed_local, DP, dp)
        upstream_sent = exchange_blocks(upstream_sent, DP, dp, ordered=False)

    def stack(rows, cols):
        rows = [r.reshape(-1, r.shape[-1]) for r in rows]
        packed = jnp.concatenate(rows, axis=0)
        return jnp.pad(packed, ((0, 8 - packed.shape[0]), (0, cols - packed.shape[1])))

    taps_x = stack([conv_x_w, conv_x_b], inner)
    taps_bc = stack([conv_bc_w, conv_bc_b], twice)
    per_head = stack([dt_bias, -jnp.exp(a_log)], LANES)
    skip = jnp.repeat(d_skip, head_dim).reshape(1, inner)
    gain = gate_gain.reshape(1, inner)
    forward_shapes = [((states, inner), f32), ((8, inner), f32), ((8, twice), f32)]
    backward_shapes = [((8, inner), f32), ((8, twice), f32), ((8, LANES), f32)]
    backward_shapes += [((states, inner), f32)] * 2 + [((8, inner), f32), ((8, twice), f32)]

    scan_far = gather_far(w_scan, DP)
    scan_far[0], taps_x, taps_bc, per_head, skip, gain = lax.optimization_barrier(
        (scan_far[0], taps_x, taps_bc, per_head, skip, gain)
    )
    scan_pieces = gather_near(scan_far, DP)
    normed_pieces = gather(normed_local, TP)
    late_pieces = gather(w_late, DP)
    upstream_pieces = gather(upstream_sent, TP)
    dp_order, tensor_order = order_of(dp), order_of(tensor)

    per = rows_local // chunk

    def stored(c, place):
        return position((c // per) ^ place[0], tensor) * per + c % per

    def ahead(cols, start):
        return pl.BlockSpec((chunk, cols), lambda c, place: (stored(c + start, place), 0))

    def back(cols, start):
        return pl.BlockSpec((chunk, cols), lambda c, place: (stored(start - c, place), 0))

    def token_piece(k, start):
        def index(c, place):
            c = c + start
            return jnp.where((c // per) ^ place[0] == k, c % per, 0), 0

        return pl.BlockSpec((chunk, model), index)

    anywhere = pl.BlockSpec(memory_space=pl.ANY)
    calls = 2 if chunks % 2 == 0 else 1
    span = chunks // calls
    first = -(-chunks * 5 // 8)
    carry, saved, weights = [], [], [scan_pieces[k] for k in dp_order]
    for start, stop in ((0, first), (first, chunks)):
        results = call(
            forward_kernel(width, head_dim, tensor, len(weights), per, start),
            stop - start,
            [token_piece(k, start) for k in range(tensor)]
            + [whole(one.shape) for one in weights]
            + [whole((8, inner)), whole((8, twice)), whole((8, LANES)), whole((1, inner))]
            + [whole(one.shape) for one in carry]
            + [anywhere] * len(saved),
            [ahead(cols, start) for cols in (inner, twice, inner, twice, LANES, inner)]
            + [pl.BlockSpec((1, states, inner), lambda c, place, start=start: (c + start, 0, 0))]
            + [whole(one) for one, _ in forward_shapes]
            + [whole((model, wide_cols))] * (start == 0),
            [
                ((length, inner), f32), ((length, twice), f32), ((length, inner), bf16),
                ((length, twice), bf16), ((length, LANES), f32), ((length, inner), f32),
                ((chunks, states, inner), bf16), *forward_shapes,
            ]
            + [((model, wide_cols), bf16)] * (start == 0),
            [
                pltpu.VMEM((chunk + 8, inner), f32), pltpu.VMEM((chunk + 8, twice), f32),
                pltpu.VMEM((chunk, model), bf16),
            ],
            {1 + tensor + len(weights) + 7 + k: k for k in range(len(saved))},
        )(place_tensor, *normed_pieces, *weights, taps_x, taps_bc, per_head, skip, *carry, *saved)
        saved, carry = results[:7], results[7:10]
        if start == 0:
            full_scan = results[10]
            weights = [full_scan]
    pre_x, pre_bc, raw_x, raw_bc, dt, mixed, before = saved

    parts = rows_local // block
    in_order = pl.BlockSpec(
        (1, 8, block), lambda c, place: ((at_position(c // parts, tensor) ^ place[0]) * parts + c % parts, 0, 0)
    )

    def gate_piece(p):
        return pl.BlockSpec(
            (block, model), lambda c, place: (jnp.where(c // parts == p, c % parts, 0), 0)
        )

    gate_raw, grad_scaled, sums, normed, upstream, full_gate, full_out = call(
        gate_kernel(tensor, dp, parts), length // block,
        [gate_piece(p) for p in range(tensor)] * 2
        + [whole((model // dp, 2 * inner))] * dp
        + [rows_of(block, inner), whole((1, inner))],
        [
            rows_of(block, inner), rows_of(block, inner), in_order, rows_of(block, model),
            rows_of(block, model), whole((model, inner)), whole((model, inner)),
        ],
        [
            ((length, inner), f32), ((length, inner), f32), ((length // block, 8, block), f32),
            ((length, model), bf16), ((length, model), bf16), ((model, inner), bf16),
            ((model, inner), bf16),
        ],
    )(
        place_tensor, *[normed_pieces[k] for k in tensor_order],
        *[upstream_pieces[k] for k in tensor_order], *late_pieces,
        mixed, gain,
    )

    sum_terms = direct_terms(sums, TP)

    scaled, d_mixed, d_gate, grad_gain = call(
        norm_kernel(inner_total, tensor), length // block,
        [in_order] * tensor
        + [rows_of(block, inner), rows_of(block, inner), rows_of(block, inner), whole((1, inner))],
        [rows_of(block, inner), rows_of(block, inner), rows_of(block, inner), whole((8, inner))],
        [
            ((length, inner), bf16), ((length, inner), f32), ((length, inner), bf16),
            ((8, inner), f32),
        ],
    )(place_tensor, *sum_terms, gate_raw, grad_scaled, mixed, gain)

    share = model // dp
    wide_share = share * min(2, dp)
    steps = model // wide_share

    def products(left, right, bounds):
        cols = right.shape[1]

        def piece(i):
            count = bounds[i + 1] - bounds[i]
            return pl.BlockSpec(
                (wide_share, cols),
                lambda c, place: (jnp.clip(c - bounds[i], 0, count - 1), 0),
            )

        return call(
            product_kernel(bounds), steps,
            [pl.BlockSpec((length, wide_share), lambda c, place: (0, c)), whole(right.shape)],
            [piece(i) for i in range(len(bounds) - 1)],
            [
                (((high - low) * wide_share, cols), bf16)
                for low, high in zip(bounds, bounds[1:])
            ],
        )(place_tensor, left, right)

    middle = (steps + 1) // 2
    out_pairs = products(upstream, scaled, list(range(steps + 1)))
    gate_own, *gate_near = products(normed, d_gate, sorted({0, middle, steps}))
    stay = rows_local * ((tensor + 1) // 2)
    branch_near = mm(scaled[stay:], full_out, NT).astype(bf16)
    branch_own = mm(scaled[:stay], full_out, NT).astype(bf16)
    out_terms = far_first(out_pairs, DP)
    gate_terms = near_first(gate_own, gate_near, DP)
    branch_terms = near_first(branch_own, [branch_near], TP)
    if narrow:
        branch_terms = [
            (exchange_blocks(array, DP, dp, True, False), k) for array, k in branch_terms
        ]
    slabs = rows_local // slab
    out_block = pl.BlockSpec((slab, 1, model), lambda c, place: (c, 0, 0))

    def one_block(k):
        return pl.BlockSpec((slab, model), lambda c, place: (k * slabs + c, 0))

    (block_output,) = call(
        output_kernel(blocks, len(branch_terms)), slabs,
        [rows_of(slab, model)] + [one_block(k) for _, k in branch_terms],
        [out_block],
        [((rows_local, 1, model), f32)],
    )(place_entry, tokens_local, *[array for array, _ in branch_terms])

    carry = []
    columns = []
    for at in range(calls):
        start = chunks - 1 - at * span
        columns, *carry = call(
            backward_kernel(width, head_dim, len(columns)), span,
            [back(cols, start) for cols in (inner, inner, twice, inner, twice, LANES, inner)]
            + [pl.BlockSpec((1, states, inner), lambda c, place, start=start: (start - c, 0, 0))]
            + [whole((8, inner)), whole((8, twice)), whole((8, LANES)), whole((1, inner))]
            + [whole(one.shape) for one in carry]
            + [anywhere] * len(columns),
            [back(wide_cols, start)] + [whole(one) for one, _ in backward_shapes],
            [((length, wide_cols), bf16), *backward_shapes],
            [pltpu.VMEM((chunk + 8, inner), f32), pltpu.VMEM((chunk + 8, twice), f32)],
            {1 + 8 + 4 + 7: 0} if columns else {},
        )(
            place_tensor, d_mixed, pre_x, pre_bc, raw_x, raw_bc, dt, mixed, before, taps_x,
            taps_bc, per_head, skip, *carry, *columns,
        )
        columns = [columns]
    columns = columns[0]
    grad_x, grad_bc, grad_head = carry[:3]

    later = (middle + steps) // 2
    scan_own, *scan_near = products(normed, columns, sorted({0, middle, later, steps}))
    scan_terms = near_first(scan_own, scan_near[::-1], DP)
    features = model // 4
    leave = max(length - stay, rows_local)
    normed_own, normed_near, pre_part = call(
        normed_kernel, 4,
        [
            pl.BlockSpec((length, features), lambda c, place: (0, c)),
            whole((length, inner)), whole((length, wide_cols)),
            rows_of(features, inner), rows_of(features, wide_cols),
        ],
        [
            pl.BlockSpec((stay, features), lambda c, place: (0, c)),
            pl.BlockSpec((leave, features), lambda c, place: (0, c)),
            pl.BlockSpec((8, features), lambda c, place: (0, c)),
        ],
        [((stay, model), bf16), ((leave, model), bf16), ((8, model), f32)],
    )(place_tensor, normed, d_gate, columns, full_gate, full_scan)
    normed_terms = near_first(normed_own, [normed_near], TP)
    if narrow:
        normed_terms = [(exchange_blocks(array, DP, dp, True), k) for array, k in normed_terms]
    (input_grad,) = call(
        input_kernel(blocks, len(normed_terms)), slabs,
        [rows_of(slab, model)] * 2 + [whole((1, model))]
        + [one_block(k) for _, k in normed_terms],
        [out_block], [((rows_local, 1, model), f32)], [pltpu.VMEM((slab, model), f32)],
    )(place_entry, tokens_local, upstream_local, gain_in, *[array for array, _ in normed_terms])

    grad_w_scan = sum(block_of(term, share) for term in scan_terms)
    grad_w_out = sum(block_of(term, share) for term in out_terms).T
    grad_w_gate = sum(block_of(term, share) for term in gate_terms)
    cols = max(inner, twice + LANES)
    cols += -cols % 512
    if narrow:
        pre_part = exchange_blocks(pre_part, DP, dp, True)
    rows = 24 + max(model // cols, 8)
    (packed,) = call(
        pack_kernel(blocks, cols), 1,
        [
            whole((8, inner)), whole((8, inner)), whole((8, twice)), whole((8, LANES)),
            whole((8, model)), whole((1, model)),
        ],
        [whole((rows, cols))], [((rows, cols), f32)], [pltpu.VMEM((8, model), f32)],
    )(place_entry, grad_x, grad_gain, grad_bc, grad_head, pre_part, gain_in)
    small = all_sum(packed, DP)

    assert cols % twice == 0 and model % cols == 0
    across = [small[16:, k : k + twice] for k in range(0, cols, twice)]
    across = jnp.concatenate(across, axis=0)
    keys_rows = grad_w_scan.shape[0]
    across = jnp.concatenate([grad_w_scan[:, inner : inner + twice], across], axis=0)
    across = total_of(direct_terms(across, TP))
    grad_w_bc = across[:keys_rows]
    of_bc = across[keys_rows:]
    count = rows - 16
    pre_rows = [of_bc[k * count + 8 : k * count + 8 + model // cols] for k in range(cols // twice)]
    sum_pre = jnp.concatenate(pre_rows, axis=1).reshape(-1)
    grad_w_dt = grad_w_scan[:, inner + twice : inner + twice + heads]
    grad_w_zx = jnp.stack([grad_w_gate, grad_w_scan[:, :inner]], axis=1)
    of_x = small[:8, :inner]
    sum_gain = small[8, :inner]
    of_head = small[16:24, twice : twice + LANES]
    return (
        block_output,
        input_grad,
        sum_pre,
        grad_w_zx,
        grad_w_dt,
        grad_w_bc,
        of_x[:width],
        of_x[width],
        of_bc[:width],
        of_bc[width],
        of_head[0, :heads],
        of_head[1, :heads],
        of_x[width + 1].reshape(heads, head_dim).sum(axis=1),
        sum_gain,
        grad_w_out,
    )


def solution(mesh):
    placed = (
        P(TP, DP, None), P(), P(DP, None, TP), P(DP, TP), P(DP, None),
        P(None, TP), P(TP), P(), P(), P(TP), P(TP), P(TP),
        P(TP), P(TP, DP), P(TP, DP, None),
    )
    results = (
        P(TP, DP, None), P(TP, DP, None), P(), P(DP, None, TP),
        P(DP, TP), P(DP, None), P(None, TP), P(TP), P(), P(), P(TP),
        P(TP), P(TP), P(TP), P(TP, DP),
    )

    return jax.shard_map(per_device, mesh=mesh, in_specs=placed, out_specs=results, check_vma=False)
```

```python
import jax
import jax.numpy as jnp
from jax import lax
from jax.experimental import pallas as pl
from jax.experimental.pallas import tpu as pltpu
from jax.sharding import PartitionSpec as P


DP, TP = "dp", "tensor"

CHUNK = 128
ROWS = 256
LANES = 128
epsilon = 1e-05
highest = lax.Precision.HIGHEST
f32 = jnp.float32
bf16 = jnp.bfloat16

NN = (((1,), (0,)), ((), ()))
NT = (((1,), (1,)), ((), ()))
TN = (((0,), (0,)), ((), ()))


def mm(a, b, dims=NN):
    return lax.dot_general(a, b, dims, preferred_element_type=f32)


def halves(v):
    high = v.astype(bf16)
    return high, (v - high.astype(f32)).astype(bf16)


def fine(a, b, dims=NN):
    a_high, a_low = halves(a)
    b_high, b_low = halves(b)
    return mm(a_high, b_high, dims) + mm(a_high, b_low, dims) + mm(a_low, b_high, dims)


def swap(value, axis, bits):
    size = lax.axis_size(axis)
    return lax.ppermute(value, axis, [(i, i ^ bits) for i in range(size)])


def order_of(size):
    return list(range(0, size, 2)) + list(range(1, size, 2))


def position(k, size):
    return k // 2 + (k % 2) * ((size + 1) // 2)


def at_position(p, size):
    half = (size + 1) // 2
    return jnp.where(p < half, 2 * p, 2 * (p - half) + 1)


def gather_far(value, axis):
    pieces = {0: value}
    for k in range(2, lax.axis_size(axis), 2):
        pieces[k] = swap(value, axis, k)
    return pieces


def gather_near(pieces, axis):
    size = lax.axis_size(axis)
    pieces = dict(pieces)
    if size > 1:
        for k in range(0, size, 2):
            pieces[k ^ 1] = swap(pieces[k], axis, 1)
    return [pieces[k] for k in range(size)]


def gather(value, axis):
    return gather_near(gather_far(value, axis), axis)


def near_first(own, near, axis):
    size = lax.axis_size(axis)
    if size == 1:
        return [(own, 0)]
    half = size // 2
    rows = own.shape[0] // half
    terms = [(own, 0)]
    sent_on = []
    start = half
    for sent in near:
        other = swap(sent, axis, 1)
        other, *_ = lax.optimization_barrier((other, *sent_on))
        stop, start = start, start - sent.shape[0] // rows
        for i in range(stop - 1, start - 1, -1):
            if i == 0:
                terms.append((other, 0))
                continue
            got = other[(i - start) * rows : (i - start + 1) * rows]
            both = own[i * rows : (i + 1) * rows].astype(f32) + got.astype(f32)
            sent_on.append(both.astype(bf16))
            terms.append((swap(sent_on[-1], axis, 2 * i), 0))
    return terms


def far_first(pairs, axis):
    if lax.axis_size(axis) == 1:
        return [(pairs[0], 0)]
    rows = pairs[0].shape[0] // 2
    got = [pairs[0]]
    for i in range(1, len(pairs)):
        got.append(swap(pairs[i], axis, 2 * i))
    other = sum(both[rows:].astype(f32) for both in got).astype(bf16)
    return [(both, 0) for both in got] + [(swap(other, axis, 1), 0)]


def direct_terms(value, axis):
    terms = [value]
    for k in range(1, lax.axis_size(axis)):
        terms.append(swap(value, axis, k))
    return terms


def all_sum(value, axis):
    size = lax.axis_size(axis)
    if size == 1:
        return value
    value = value + swap(value, axis, 1)
    total = value
    for k in range(2, size, 2):
        total = total + swap(value, axis, k)
    return total


def softplus(v):
    return jnp.maximum(v, 0.0) + jnp.log1p(jnp.exp(-jnp.abs(v)))


def lower(size):
    return lax.broadcasted_iota(jnp.int32, (size, size), 0) >= lax.broadcasted_iota(
        jnp.int32, (size, size), 1
    )


def pick(values, lane_head):
    out = values[0]
    for j in range(1, len(values)):
        out = jnp.where(lane_head == j, values[j], out)
    return out


def take(out, refs, which):
    for k, ref in enumerate(refs):

        @pl.when(which == k)
        def _(ref=ref):
            out[...] = ref[...]


def join(out, refs, start=0):
    rows = refs[0].shape[0]
    cols = out.shape[1]
    for k, ref in enumerate(refs):
        out[k * rows : (k + 1) * rows, :] = ref[:, start : start + cols]


def forward_kernel(width, head_dim, count, pieces, per, start):
    per_group = LANES // head_dim

    def kernel(place, *refs):
        token_refs, refs = refs[:count], refs[count:]
        weight_refs, refs = refs[:pieces], refs[pieces:]
        taps_x, taps_bc, per_head, skip, *refs = refs
        if start:
            carried, refs = refs[:3], refs[10:]
        pre_x, pre_bc, raw_x, raw_bc, dt_out, mixed, before, state, halo_x, halo_bc = refs[:10]
        if start == 0:
            weights, refs = refs[10], refs[11:]
        else:
            weights, refs = weight_refs[0], refs[10:]
        ext_x, ext_bc, normed = refs
        size = normed.shape[0]
        take(normed, token_refs, ((pl.program_id(0) + start) // per) ^ place[0])
        inner = mixed.shape[1]
        twice = pre_bc.shape[1]
        states = twice // 2

        @pl.when(pl.program_id(0) == 0)
        def _():
            if start:
                state[...] = carried[0][...]
                ext_x[0:8, :] = carried[1][...]
                ext_bc[0:8, :] = carried[2][...]
            else:
                state[...] = jnp.zeros(state.shape, f32)
                ext_x[0:8, :] = jnp.zeros((8, inner), f32)
                ext_bc[0:8, :] = jnp.zeros((8, twice), f32)
                join(weights, weight_refs)

        raw = mm(normed[...], weights[...])

        def conv(ext, values, taps, raw_ref, pre_ref, halo):
            ext[8 : 8 + size, :] = values
            raw_ref[...] = values.astype(bf16)
            total = taps[width : width + 1, :]
            for k in range(width):
                start = 8 - (width - 1) + k
                total = total + taps[k : k + 1, :] * ext[start : start + size, :]
            halo[...] = ext[size : size + 8, :]
            ext[0:8, :] = halo[...]
            pre_ref[...] = total
            return total * jax.nn.sigmoid(total)

        x = conv(ext_x, raw[:, :inner], taps_x, raw_x, pre_x, halo_x)
        bc = conv(ext_bc, raw[:, inner : inner + twice], taps_bc, raw_bc, pre_bc, halo_bc)
        dt = raw[:, inner + twice :] + per_head[0:1, :]
        dt_out[...] = dt
        steps = softplus(dt)
        below = lower(size)
        logs = lax.dot_general(
            below.astype(f32), steps * per_head[1:2, :], NN, precision=highest,
            preferred_element_type=f32,
        )
        logs_t = logs.T
        keys = bc[:, :states]
        keys_t = keys.T
        queries = bc[:, states:]
        scores = jnp.where(below, fine(queries, keys, NT), 0.0)
        lane_head = lax.broadcasted_iota(jnp.int32, (size, LANES), 1) // head_dim
        for group in range(inner // LANES):
            lanes = slice(group * LANES, (group + 1) * LANES)
            x_g = x[:, lanes]
            heads = [group * per_group + j for j in range(per_group)]
            step_e = pick(
                [jnp.broadcast_to(steps[:, h : h + 1], (size, LANES)) for h in heads], lane_head
            )
            log_e = pick(
                [jnp.broadcast_to(logs[:, h : h + 1], (size, LANES)) for h in heads], lane_head
            )
            xs = x_g * step_e
            xs_half = xs.astype(bf16)
            total = skip[0:1, lanes] * x_g
            for j, h in enumerate(heads):
                gap = logs[:, h : h + 1] - logs_t[h : h + 1, :]
                weights_h = (scores * jnp.exp(jnp.minimum(gap, 0.0))).astype(bf16)
                total = total + mm(weights_h, jnp.where(lane_head == j, xs_half, 0.0))
            old = state[:, lanes]
            before[0, :, lanes] = old.astype(bf16)
            total = total + jnp.exp(log_e) * fine(queries, old)
            mixed[:, lanes] = total
            last = log_e[size - 1 : size, :]
            fresh = fine(keys_t, jnp.exp(last - log_e) * xs)
            state[:, lanes] = jnp.exp(last) * old + fresh

    return kernel


def backward_kernel(width, head_dim, resumed):
    per_group = LANES // head_dim

    def kernel(place, *refs):
        d_mixed, pre_x, pre_bc, raw_x, raw_bc, dt_in, mixed, before, *refs = refs
        taps_x, taps_bc, per_head, skip, *refs = refs
        if resumed:
            carried, refs = refs[:7], refs[8:]
        columns, *results, ext_x, ext_bc = refs
        grad_x, grad_bc, grad_head, d_state, after, halo_x, halo_bc = results
        size = d_mixed.shape[0]
        inner = d_mixed.shape[1]
        twice = pre_bc.shape[1]
        states = twice // 2

        @pl.when(pl.program_id(0) == 0)
        def _():
            for k, result in enumerate(results):
                result[...] = carried[k][...] if resumed else jnp.zeros(result.shape, f32)
            ext_x[size : size + 8, :] = halo_x[...]
            ext_bc[size : size + 8, :] = halo_bc[...]

        dt = dt_in[...]
        steps = softplus(dt)
        rates = per_head[1:2, :]
        below = lower(size)
        logs = lax.dot_general(
            below.astype(f32), steps * rates, NN, precision=highest, preferred_element_type=f32
        )
        logs_t = logs.T
        p_bc = pre_bc[...]
        sig_bc = jax.nn.sigmoid(p_bc)
        bc = p_bc * sig_bc
        keys = bc[:, :states].astype(bf16)
        queries = bc[:, states:].astype(bf16)
        queries_t = bc[:, states:].T
        above = lax.broadcasted_iota(jnp.int32, (size, size), 0) <= lax.broadcasted_iota(
            jnp.int32, (size, size), 1
        )
        scores_t = jnp.where(above, mm(keys, queries, NT), 0.0)
        lane_head = lax.broadcasted_iota(jnp.int32, (size, LANES), 1) // head_dim
        d_scores_t = jnp.zeros((size, size), f32)
        d_keys = jnp.zeros((size, states), f32)
        d_queries = jnp.zeros((size, states), f32)
        head_of = lax.broadcasted_iota(jnp.int32, (LANES, LANES), 0) // head_dim
        lane_of = lax.broadcasted_iota(jnp.int32, (LANES, LANES), 1)
        log_sum = jnp.zeros((size, LANES), f32)
        step_sum = jnp.zeros((size, LANES), f32)
        end_sum = jnp.zeros((8, LANES), f32)
        for group in range(inner // LANES):
            lanes = slice(group * LANES, (group + 1) * LANES)
            heads = [group * per_group + j for j in range(per_group)]
            p_x = pre_x[:, lanes]
            sig_x = jax.nn.sigmoid(p_x)
            x_g = p_x * sig_x
            dy = d_mixed[:, lanes]
            step_e = pick(
                [jnp.broadcast_to(steps[:, h : h + 1], (size, LANES)) for h in heads], lane_head
            )
            log_e = pick(
                [jnp.broadcast_to(logs[:, h : h + 1], (size, LANES)) for h in heads], lane_head
            )
            xs = x_g * step_e
            xs_half, dy_half = xs.astype(bf16), dy.astype(bf16)
            last = log_e[size - 1 : size, :]
            fade = jnp.exp(last - log_e)
            old = before[0, :, lanes]
            d_new = d_state[:, lanes]
            d_new_half = d_new.astype(bf16)
            dxs = fade * mm(keys, d_new_half)
            for j, h in enumerate(heads):
                mine = lane_head == j
                gap = logs_t[h : h + 1, :] - logs[:, h : h + 1]
                decay = jnp.exp(jnp.minimum(gap, 0.0))
                dxs = dxs + mm(
                    (scores_t * decay).astype(bf16), jnp.where(mine, dy_half, 0.0)
                )
                d_scores_t = d_scores_t + decay * mm(jnp.where(mine, xs_half, 0.0), dy_half, NT)
            e_dy = jnp.exp(log_e) * dy
            d_queries = d_queries + sum(mm(half, old, NT) for half in halves(e_dy))
            d_keys = d_keys + fine(fade * xs, d_new, NT)
            skip_g = skip[0:1, lanes]
            log_lane = dy * (mixed[:, lanes] - skip_g * x_g) - xs * dxs
            step_lane = dxs * x_g
            end_lane = jnp.sum(d_new * after[:, lanes], axis=0, keepdims=True)
            to_head = (head_of + group * per_group == lane_of).astype(bf16)
            for high_low in halves(log_lane):
                log_sum = log_sum + mm(high_low, to_head)
            for high_low in halves(step_lane):
                step_sum = step_sum + mm(high_low, to_head)
            for high_low in halves(jnp.broadcast_to(end_lane, (8, LANES))):
                end_sum = end_sum + mm(high_low, to_head)
            d_state[:, lanes] = jnp.exp(last) * d_new + fine(queries_t, e_dy)
            after[:, lanes] = old.astype(f32)
            grad_x[width + 1 : width + 2, lanes] += jnp.sum(dy * x_g, axis=0, keepdims=True)
            dx = dxs * step_e + skip_g * dy
            d_pre = dx * (sig_x + x_g * (1.0 - sig_x))
            ext_x[0:size, lanes] = d_pre
            grad_x[width : width + 1, lanes] += jnp.sum(d_pre, axis=0, keepdims=True)
            total = jnp.zeros((size, LANES), f32)
            raw = raw_x[:, lanes].astype(f32)
            for k in range(width):
                moved = ext_x[width - 1 - k : width - 1 - k + size, lanes]
                total = total + taps_x[k : k + 1, lanes] * moved
                grad_x[k : k + 1, lanes] += jnp.sum(raw * moved, axis=0, keepdims=True)
            columns[:, lanes] = total.astype(bf16)
            halo_x[:, lanes] = ext_x[0:8, lanes]
            ext_x[size : size + 8, lanes] = halo_x[:, lanes]
        d_scores_t = jnp.where(above, d_scores_t, 0.0)
        d_keys = d_keys + fine(d_scores_t, bc[:, states:])
        d_queries = d_queries + fine(d_scores_t.T, bc[:, :states])
        at_end = lax.broadcasted_iota(jnp.int32, (size, LANES), 0) == size - 1
        d_log = log_sum + jnp.where(at_end, end_sum[0:1, :], 0.0)
        d_rate = lax.dot_general(
            above.astype(f32), d_log, NN, precision=highest, preferred_element_type=f32
        )
        grad_head[1:2, :] += rates * jnp.sum(steps * d_rate, axis=0, keepdims=True)
        d_dt = (step_sum + rates * d_rate) * jax.nn.sigmoid(dt)
        grad_head[0:1, :] += jnp.sum(d_dt, axis=0, keepdims=True)
        columns[:, inner + twice :] = d_dt.astype(bf16)
        slope = sig_bc + bc * (1.0 - sig_bc)
        ext_bc[0:size, :states] = d_keys * slope[:, :states]
        ext_bc[0:size, states:] = d_queries * slope[:, states:]
        grad_bc[width : width + 1, :] += jnp.sum(ext_bc[0:size, :], axis=0, keepdims=True)
        total = jnp.zeros((size, twice), f32)
        raw = raw_bc[...].astype(f32)
        for k in range(width):
            moved = ext_bc[width - 1 - k : width - 1 - k + size, :]
            total = total + taps_bc[k : k + 1, :] * moved
            grad_bc[k : k + 1, :] += jnp.sum(raw * moved, axis=0, keepdims=True)
        columns[:, inner : inner + twice] = total.astype(bf16)
        halo_bc[...] = ext_bc[0:8, :]
        ext_bc[size : size + 8, :] = halo_bc[...]

    return kernel


def gate_kernel(count, pieces, parts):
    def kernel(place, *refs):
        normed_refs, upstream_refs, refs = refs[:count], refs[count : 2 * count], refs[2 * count :]
        weight_refs, refs = refs[:pieces], refs[pieces:]
        mixed, gain, gate_raw, grad_scaled, sums, normed, upstream, w_gate, w_out = refs

        @pl.when(pl.program_id(0) == 0)
        def _():
            join(w_gate, [weight_refs[k] for k in order_of(pieces)])
            join(w_out, weight_refs, w_gate.shape[1])

        take(normed, normed_refs, pl.program_id(0) // parts)
        take(upstream, upstream_refs, pl.program_id(0) // parts)
        gate_body(normed, upstream, w_gate, w_out, mixed, gain, gate_raw, grad_scaled, sums)

    return kernel


def gate_body(normed, upstream, w_gate, w_out, mixed, gain, gate_raw, grad_scaled, sums):
    gate = mm(normed[...], w_gate[...])
    grads = mm(upstream[...], w_out[...])
    gate_raw[...] = gate
    grad_scaled[...] = grads
    gated = mixed[...] * (gate * jax.nn.sigmoid(gate))
    ones = jnp.ones((8, gated.shape[1]), bf16)
    rows = lax.broadcasted_iota(jnp.int32, sums.shape[1:], 0)
    square = sum(mm(ones, part, NT) for part in halves(gated * gated))
    cross = sum(mm(ones, part, NT) for part in halves(gated * (grads * gain[...])))
    sums[0] = jnp.where(rows == 0, square, cross)


def norm_kernel(inner_total, count):
    def kernel(place, *refs):
        terms, refs = refs[:count], refs[count:]
        gate_raw, grad_scaled, mixed, gain, scaled, d_mixed, d_gate, grad_gain = refs

        @pl.when(pl.program_id(0) == 0)
        def _():
            grad_gain[...] = jnp.zeros(grad_gain.shape, f32)

        total = terms[0][0]
        for term in terms[1:]:
            total = total + term[0]
        column = total.T
        inverse = lax.rsqrt(column[:, 0:1] / inner_total + epsilon)
        pull = inverse * inverse * inverse * (column[:, 1:2] / inner_total)
        gate = gate_raw[...]
        sig = jax.nn.sigmoid(gate)
        act = gate * sig
        mix = mixed[...]
        grads = grad_scaled[...]
        unit = mix * act * inverse
        scaled[...] = (unit * gain[...]).astype(bf16)
        grad_gain[0:1, :] += jnp.sum(grads * unit, axis=0, keepdims=True)
        d_gated = inverse * (grads * gain[...]) - (mix * act) * pull
        d_mixed[...] = d_gated * act
        d_gate[...] = (d_gated * mix * (sig + act * (1.0 - sig))).astype(bf16)

    return kernel


def place_of(place, k, blocks, size):
    return pl.multiple_of(position(place[0] ^ k, blocks) * size, size)


def entry_kernel(blocks):
    def kernel(place, tokens, upstream, gain, normed_out, upstream_out):
        size = tokens.shape[1] // blocks
        wide = tokens[...].astype(f32)
        inverse = lax.rsqrt(jnp.mean(wide * wide, axis=-1, keepdims=True) + epsilon)
        normed = (wide * inverse * gain[...]).astype(bf16)
        for k in range(blocks):
            at = pl.ds(place_of(place, k, blocks, size), size)
            normed_out[:, at] = normed[:, k * size : (k + 1) * size]
            at = pl.ds(pl.multiple_of((place[0] ^ k) * size, size), size)
            upstream_out[:, at] = upstream[:, k * size : (k + 1) * size]

    return kernel


def pack_kernel(blocks, cols):
    def kernel(place, grad_x, grad_gain, grad_bc, grad_head, pre_part, gain, out, row):
        twice = grad_bc.shape[1]
        inner = grad_x.shape[1]
        model = row.shape[1]
        size = model // blocks
        out[...] = jnp.zeros(out.shape, f32)
        out[0:8, :inner] = grad_x[...]
        out[8:16, :inner] = grad_gain[...]
        out[16:24, :twice] = grad_bc[...]
        out[16:24, twice : twice + LANES] = grad_head[...]
        for k in range(blocks):
            at = pl.ds(place_of(place, k, blocks, size), size)
            row[:, k * size : (k + 1) * size] = pre_part[:, at]
        for k in range(model // cols):
            part = slice(k * cols, (k + 1) * cols)
            out[24 + k : 25 + k, :] = row[0:1, part] / gain[0:1, part]

    return kernel


def output_kernel(blocks, count):
    def kernel(place, tokens, *refs):
        out = refs[count]
        size = tokens.shape[1] // blocks
        for k in range(blocks):
            at = pl.multiple_of((place[0] ^ k) * size, size)
            total = tokens[:, k * size : (k + 1) * size].astype(f32)
            for term in refs[:count]:
                total = total + term[:, pl.ds(at, size)].astype(f32)
            out[:, 0, k * size : (k + 1) * size] = total

    return kernel


def input_kernel(blocks, count):
    def kernel(place, tokens, upstream, gain, *refs):
        out, grads = refs[count:]
        model = tokens.shape[1]
        size = model // blocks
        wide = tokens[...].astype(f32)
        inverse = lax.rsqrt(jnp.mean(wide * wide, axis=-1, keepdims=True) + epsilon)
        for k in range(blocks):
            at = place_of(place, k, blocks, size)
            total = refs[0][:, pl.ds(at, size)].astype(f32)
            for term in refs[1:count]:
                total = total + term[:, pl.ds(at, size)].astype(f32)
            grads[:, k * size : (k + 1) * size] = total
        weighted = grads[...] * gain[...]
        inner_dot = jnp.mean(weighted * wide, axis=-1, keepdims=True)
        out[:, 0, :] = (
            upstream[...].astype(f32)
            + inverse * weighted
            - wide * (inverse * inverse * inverse * inner_dot)
        )

    return kernel


def normed_kernel(place, tokens, d_gate, columns, w_gate, w_scan, own, near, grad_gain):
    total = mm(d_gate[...], w_gate[...], NT) + mm(columns[...], w_scan[...], NT)
    own[...] = total[: own.shape[0]].astype(bf16)
    near[...] = total[-near.shape[0] :].astype(bf16)
    total = total * tokens[...].astype(f32)
    grad_gain[...] = jnp.broadcast_to(jnp.sum(total, axis=0, keepdims=True), grad_gain.shape)


def weights_kernel(counts, inner, twice):
    def kernel(place, *refs):
        groups = []
        for count in counts:
            groups.append(refs[:count])
            refs = refs[count:]
        grad_zx, grad_out, grad_dt, grad_bc = refs

        def total(terms):
            return sum(term[...].astype(f32) for term in terms)

        scan, gate, out = (total(group) for group in groups)
        grad_zx[:, 0, :] = gate
        grad_zx[:, 1, :] = scan[:, :inner]
        grad_out[...] = out.T
        grad_bc[...] = scan[:, inner : inner + twice]
        grad_dt[...] = scan[:, inner + twice : inner + twice + grad_dt.shape[1]]

    return kernel


def shared_kernel(count, rows, cols):
    def kernel(place, *refs):
        grad_w, of_conv, of_pre = refs[count:]
        total = refs[0][...]
        for term in refs[1:count]:
            total = total + term[...]
        share, twice = grad_w.shape
        grad_w[...] = total[:share]
        of_conv[...] = total[share : share + 8]
        for r in range(of_pre.shape[1] // cols):
            for k in range(cols // twice):
                at = share + k * rows + 8 + r
                start = r * cols + k * twice
                of_pre[:, start : start + twice] = total[at : at + 1]

    return kernel


def whole(shape):
    return pl.BlockSpec(shape, lambda c, place: (0,) * len(shape))


def rows_of(size, cols, column=0):
    return pl.BlockSpec((size, cols), lambda c, place: (c, column))


def call(kernel, grid, ins, outs, shapes, scratch=(), aliases=None):
    return pl.pallas_call(
        kernel,
        grid_spec=pltpu.PrefetchScalarGridSpec(
            num_scalar_prefetch=1, grid=(grid,), in_specs=ins, out_specs=outs,
            scratch_shapes=scratch,
        ),
        out_shape=[jax.ShapeDtypeStruct(*one) for one in shapes],
        input_output_aliases=aliases or {},
    )


def exchange_blocks(values, axis, blocks, back=False, ordered=True):
    index = lax.axis_index(axis)
    order = order_of(blocks)
    blocked = values.reshape(values.shape[0], blocks, -1)
    if back and ordered:
        blocked = jnp.stack([blocked[:, order.index(k)] for k in range(blocks)], axis=1)
    bits = 1
    while bits < blocks:
        split = blocked.reshape(blocked.shape[0], blocks // (2 * bits), 2, -1)
        blocked = jnp.where((index & bits) != 0, split[:, :, ::-1], split)
        blocked = blocked.reshape(blocked.shape[0], blocks, -1)
        bits *= 2
    if ordered and not back:
        blocked = jnp.stack([blocked[:, k] for k in order], axis=1)
    return blocked.reshape(values.shape)


def per_device(
    block_input, pre_gain, w_zx, w_dt, w_bc, conv_x_w, conv_x_b, conv_bc_w, conv_bc_b,
    dt_bias, a_log, d_skip, gate_gain, w_out, cotangent,
):
    rows_local, seqs, model = block_input.shape
    assert seqs == 1
    dp = lax.axis_size(DP)
    tensor = lax.axis_size(TP)
    length = rows_local * tensor
    inner = w_zx.shape[2]
    twice = w_bc.shape[1]
    states = twice // 2
    heads = w_dt.shape[1]
    head_dim = inner // heads
    width = conv_x_w.shape[0]
    wide_cols = inner + twice + LANES
    inner_total = inner * tensor
    chunk = min(CHUNK, rows_local)
    block = min(ROWS, rows_local)
    chunks = length // chunk
    place_dp = lax.axis_index(DP).astype(jnp.int32).reshape(1)
    place_tensor = lax.axis_index(TP).astype(jnp.int32).reshape(1)
    narrow = (model // dp) % LANES != 0
    blocks = 1 if narrow else dp
    place_entry = place_dp * 0 if narrow else place_dp

    slab = rows_local
    tokens_local = block_input.reshape(rows_local, model)
    upstream_local = cotangent.reshape(rows_local, model)
    gain_in = pre_gain.reshape(1, model)
    w_scan = jnp.concatenate(
        [w_zx[:, 1, :], w_bc, w_dt, jnp.zeros((w_dt.shape[0], LANES - heads), bf16)], axis=1
    )
    w_late = jnp.concatenate([w_zx[:, 0, :], w_out.T], axis=1)
    normed_local, upstream_sent = call(
        entry_kernel(blocks), rows_local // slab,
        [rows_of(slab, model), rows_of(slab, model), whole((1, model))],
        [rows_of(slab, model)] * 2,
        [((rows_local, model), bf16)] * 2,
    )(place_entry, tokens_local, upstream_local, gain_in)
    if narrow:
        normed_local = exchange_blocks(normed_local, DP, dp)
        upstream_sent = exchange_blocks(upstream_sent, DP, dp, ordered=False)

    def stack(rows, cols):
        rows = [r.reshape(-1, r.shape[-1]) for r in rows]
        packed = jnp.concatenate(rows, axis=0)
        return jnp.pad(packed, ((0, 8 - packed.shape[0]), (0, cols - packed.shape[1])))

    taps_x = stack([conv_x_w, conv_x_b], inner)
    taps_bc = stack([conv_bc_w, conv_bc_b], twice)
    per_head = stack([dt_bias, -jnp.exp(a_log)], LANES)
    skip = jnp.repeat(d_skip, head_dim).reshape(1, inner)
    gain = gate_gain.reshape(1, inner)
    forward_shapes = [((states, inner), f32), ((8, inner), f32), ((8, twice), f32)]
    backward_shapes = [((8, inner), f32), ((8, twice), f32), ((8, LANES), f32)]
    backward_shapes += [((states, inner), f32)] * 2 + [((8, inner), f32), ((8, twice), f32)]

    scan_far = gather_far(w_scan, DP)
    scan_far[0], taps_x, taps_bc, per_head, skip, gain = lax.optimization_barrier(
        (scan_far[0], taps_x, taps_bc, per_head, skip, gain)
    )
    scan_pieces = gather_near(scan_far, DP)
    normed_pieces = gather(normed_local, TP)
    late_pieces = gather(w_late, DP)
    upstream_pieces = gather(upstream_sent, TP)
    dp_order, tensor_order = order_of(dp), order_of(tensor)

    per = rows_local // chunk

    def stored(c, place):
        return position((c // per) ^ place[0], tensor) * per + c % per

    def ahead(cols, start):
        return pl.BlockSpec((chunk, cols), lambda c, place: (stored(c + start, place), 0))

    def back(cols, start):
        return pl.BlockSpec((chunk, cols), lambda c, place: (stored(start - c, place), 0))

    def token_piece(k, start):
        def index(c, place):
            c = c + start
            return jnp.where((c // per) ^ place[0] == k, c % per, 0), 0

        return pl.BlockSpec((chunk, model), index)

    anywhere = pl.BlockSpec(memory_space=pl.ANY)
    calls = 2 if chunks % 2 == 0 else 1
    span = chunks // calls
    first = -(-chunks * 5 // 8)
    carry, saved, weights = [], [], [scan_pieces[k] for k in dp_order]
    for start, stop in ((0, first), (first, chunks)):
        results = call(
            forward_kernel(width, head_dim, tensor, len(weights), per, start),
            stop - start,
            [token_piece(k, start) for k in range(tensor)]
            + [whole(one.shape) for one in weights]
            + [whole((8, inner)), whole((8, twice)), whole((8, LANES)), whole((1, inner))]
            + [whole(one.shape) for one in carry]
            + [anywhere] * len(saved),
            [ahead(cols, start) for cols in (inner, twice, inner, twice, LANES, inner)]
            + [pl.BlockSpec((1, states, inner), lambda c, place, start=start: (c + start, 0, 0))]
            + [whole(one) for one, _ in forward_shapes]
            + [whole((model, wide_cols))] * (start == 0),
            [
                ((length, inner), f32), ((length, twice), f32), ((length, inner), bf16),
                ((length, twice), bf16), ((length, LANES), f32), ((length, inner), f32),
                ((chunks, states, inner), bf16), *forward_shapes,
            ]
            + [((model, wide_cols), bf16)] * (start == 0),
            [
                pltpu.VMEM((chunk + 8, inner), f32), pltpu.VMEM((chunk + 8, twice), f32),
                pltpu.VMEM((chunk, model), bf16),
            ],
            {1 + tensor + len(weights) + 7 + k: k for k in range(len(saved))},
        )(place_tensor, *normed_pieces, *weights, taps_x, taps_bc, per_head, skip, *carry, *saved)
        saved, carry = results[:7], results[7:10]
        if start == 0:
            full_scan = results[10]
            weights = [full_scan]
    pre_x, pre_bc, raw_x, raw_bc, dt, mixed, before = saved

    parts = rows_local // block
    in_order = pl.BlockSpec(
        (1, 8, block), lambda c, place: ((at_position(c // parts, tensor) ^ place[0]) * parts + c % parts, 0, 0)
    )

    def gate_piece(p):
        return pl.BlockSpec(
            (block, model), lambda c, place: (jnp.where(c // parts == p, c % parts, 0), 0)
        )

    gate_raw, grad_scaled, sums, normed, upstream, full_gate, full_out = call(
        gate_kernel(tensor, dp, parts), length // block,
        [gate_piece(p) for p in range(tensor)] * 2
        + [whole((model // dp, 2 * inner))] * dp
        + [rows_of(block, inner), whole((1, inner))],
        [
            rows_of(block, inner), rows_of(block, inner), in_order, rows_of(block, model),
            rows_of(block, model), whole((model, inner)), whole((model, inner)),
        ],
        [
            ((length, inner), f32), ((length, inner), f32), ((length // block, 8, block), f32),
            ((length, model), bf16), ((length, model), bf16), ((model, inner), bf16),
            ((model, inner), bf16),
        ],
    )(
        place_tensor, *[normed_pieces[k] for k in tensor_order],
        *[upstream_pieces[k] for k in tensor_order], *late_pieces,
        mixed, gain,
    )

    sum_terms = direct_terms(sums, TP)

    scaled, d_mixed, d_gate, grad_gain = call(
        norm_kernel(inner_total, tensor), length // block,
        [in_order] * tensor
        + [rows_of(block, inner), rows_of(block, inner), rows_of(block, inner), whole((1, inner))],
        [rows_of(block, inner), rows_of(block, inner), rows_of(block, inner), whole((8, inner))],
        [
            ((length, inner), bf16), ((length, inner), f32), ((length, inner), bf16),
            ((8, inner), f32),
        ],
    )(place_tensor, *sum_terms, gate_raw, grad_scaled, mixed, gain)

    share = model // dp

    def tn(left, right):
        return lax.dot_general(left, right, TN, preferred_element_type=f32).astype(bf16)

    out_part = lax.optimization_barrier(tn(upstream, scaled))
    out_pairs = [out_part[k * share : (k + 2) * share] for k in range(0, dp, 2)]
    even = share * ((dp + 1) // 2)
    gate_part = lax.optimization_barrier(tn(normed, d_gate))
    gate_own, gate_near = gate_part[:even], [gate_part[even:]]
    stay = rows_local * ((tensor + 1) // 2)
    branch_part = lax.optimization_barrier(mm(scaled, full_out, NT).astype(bf16))
    branch_own, branch_near = branch_part[:stay], branch_part[stay:]
    out_terms = far_first(out_pairs, DP)
    gate_terms = near_first(gate_own, gate_near, DP)
    branch_terms = near_first(branch_own, [branch_near], TP)
    if narrow:
        branch_terms = [
            (exchange_blocks(array, DP, dp, True, False), k) for array, k in branch_terms
        ]
    slabs = rows_local // slab
    out_block = pl.BlockSpec((slab, 1, model), lambda c, place: (c, 0, 0))

    def one_block(k):
        return pl.BlockSpec((slab, model), lambda c, place: (k * slabs + c, 0))

    (block_output,) = call(
        output_kernel(blocks, len(branch_terms)), slabs,
        [rows_of(slab, model)] + [one_block(k) for _, k in branch_terms],
        [out_block],
        [((rows_local, 1, model), f32)],
    )(place_entry, tokens_local, *[array for array, _ in branch_terms])

    carry = []
    columns = []
    for at in range(calls):
        start = chunks - 1 - at * span
        columns, *carry = call(
            backward_kernel(width, head_dim, len(columns)), span,
            [back(cols, start) for cols in (inner, inner, twice, inner, twice, LANES, inner)]
            + [pl.BlockSpec((1, states, inner), lambda c, place, start=start: (start - c, 0, 0))]
            + [whole((8, inner)), whole((8, twice)), whole((8, LANES)), whole((1, inner))]
            + [whole(one.shape) for one in carry]
            + [anywhere] * len(columns),
            [back(wide_cols, start)] + [whole(one) for one, _ in backward_shapes],
            [((length, wide_cols), bf16), *backward_shapes],
            [pltpu.VMEM((chunk + 8, inner), f32), pltpu.VMEM((chunk + 8, twice), f32)],
            {1 + 8 + 4 + 7: 0} if columns else {},
        )(
            place_tensor, d_mixed, pre_x, pre_bc, raw_x, raw_bc, dt, mixed, before, taps_x,
            taps_bc, per_head, skip, *carry, *columns,
        )
        columns = [columns]
    columns = columns[0]
    grad_x, grad_bc, grad_head = carry[:3]

    later = even + (model - even) // 2 if dp % 4 == 0 else even
    scan_near = [tn(normed[:, later:], columns)]
    if later > even:
        scan_near.append(tn(normed[:, even:later], columns))
    scan_own = tn(normed[:, :even], columns)
    scan_terms = near_first(scan_own, scan_near, DP)
    features = model // 4
    leave = max(length - stay, rows_local)
    normed_own, normed_near, pre_part = call(
        normed_kernel, 4,
        [
            pl.BlockSpec((length, features), lambda c, place: (0, c)),
            whole((length, inner)), whole((length, wide_cols)),
            rows_of(features, inner), rows_of(features, wide_cols),
        ],
        [
            pl.BlockSpec((stay, features), lambda c, place: (0, c)),
            pl.BlockSpec((leave, features), lambda c, place: (0, c)),
            pl.BlockSpec((8, features), lambda c, place: (0, c)),
        ],
        [((stay, model), bf16), ((leave, model), bf16), ((8, model), f32)],
    )(place_tensor, normed, d_gate, columns, full_gate, full_scan)
    normed_terms = near_first(normed_own, [normed_near], TP)
    if narrow:
        normed_terms = [(exchange_blocks(array, DP, dp, True), k) for array, k in normed_terms]
    (input_grad,) = call(
        input_kernel(blocks, len(normed_terms)), slabs,
        [rows_of(slab, model)] * 2 + [whole((1, model))]
        + [one_block(k) for _, k in normed_terms],
        [out_block], [((rows_local, 1, model), f32)], [pltpu.VMEM((slab, model), f32)],
    )(place_entry, tokens_local, upstream_local, gain_in, *[array for array, _ in normed_terms])

    groups = (scan_terms, gate_terms, out_terms)
    grad_w_zx, grad_w_out, grad_w_dt, grad_bc_part = call(
        weights_kernel([len(terms) for terms in groups], inner, twice), 1,
        [
            pl.BlockSpec((share, array.shape[1]), lambda c, place, k=k: (k, 0))
            for terms in groups for array, k in terms
        ],
        [whole((share, 2, inner)), whole((inner, share)), whole((share, heads)), whole((share, twice))],
        [
            ((share, 2, inner), f32), ((inner, share), f32), ((share, heads), f32),
            ((share, twice), f32),
        ],
    )(place_entry, *[array for terms in groups for array, _ in terms])
    cols = max(inner, twice + LANES)
    cols += -cols % 512
    if narrow:
        pre_part = exchange_blocks(pre_part, DP, dp, True)
    rows = 24 + max(model // cols, 8)
    (packed,) = call(
        pack_kernel(blocks, cols), 1,
        [
            whole((8, inner)), whole((8, inner)), whole((8, twice)), whole((8, LANES)),
            whole((8, model)), whole((1, model)),
        ],
        [whole((rows, cols))], [((rows, cols), f32)], [pltpu.VMEM((8, model), f32)],
    )(place_entry, grad_x, grad_gain, grad_bc, grad_head, pre_part, gain_in)
    small = all_sum(packed, DP)

    assert cols % twice == 0 and model % cols == 0
    across = [small[16:, k : k + twice] for k in range(0, cols, twice)]
    across = jnp.concatenate(across, axis=0)
    across = direct_terms(jnp.concatenate([grad_bc_part, across], axis=0), TP)
    grad_w_bc, of_bc, sum_pre = call(
        shared_kernel(tensor, rows - 16, cols), 1,
        [whole(across[0].shape)] * tensor,
        [whole((share, twice)), whole((8, twice)), whole((1, model))],
        [((share, twice), f32), ((8, twice), f32), ((1, model), f32)],
    )(place_entry, *across)
    of_x = small[:8, :inner]
    sum_gain = small[8, :inner]
    of_head = small[16:24, twice : twice + LANES]
    return (
        block_output,
        input_grad,
        sum_pre.reshape(model),
        grad_w_zx,
        grad_w_dt,
        grad_w_bc,
        of_x[:width],
        of_x[width],
        of_bc[:width],
        of_bc[width],
        of_head[0, :heads],
        of_head[1, :heads],
        of_x[width + 1].reshape(heads, head_dim).sum(axis=1),
        sum_gain,
        grad_w_out,
    )


def solution(mesh):
    placed = (
        P(TP, DP, None), P(), P(DP, None, TP), P(DP, TP), P(DP, None),
        P(None, TP), P(TP), P(), P(), P(TP), P(TP), P(TP),
        P(TP), P(TP, DP), P(TP, DP, None),
    )
    results = (
        P(TP, DP, None), P(TP, DP, None), P(), P(DP, None, TP),
        P(DP, TP), P(DP, None), P(None, TP), P(TP), P(), P(), P(TP),
        P(TP), P(TP), P(TP), P(TP, DP),
    )

    return jax.shard_map(per_device, mesh=mesh, in_specs=placed, out_specs=results, check_vma=False)
```

```python
import jax
import jax.numpy as jnp
from jax import lax
from jax.experimental import pallas as pl
from jax.experimental.pallas import tpu as pltpu
from jax.sharding import PartitionSpec as P


DP, TP = "dp", "tensor"

CHUNK = 128
ROWS = 256
LANES = 128
epsilon = 1e-05
highest = lax.Precision.HIGHEST
f32 = jnp.float32
bf16 = jnp.bfloat16

NN = (((1,), (0,)), ((), ()))
NT = (((1,), (1,)), ((), ()))
TN = (((0,), (0,)), ((), ()))


def mm(a, b, dims=NN):
    return lax.dot_general(a, b, dims, preferred_element_type=f32)


def halves(v):
    high = v.astype(bf16)
    return high, (v - high.astype(f32)).astype(bf16)


def fine(a, b, dims=NN):
    a_high, a_low = halves(a)
    b_high, b_low = halves(b)
    return mm(a_high, b_high, dims) + mm(a_high, b_low, dims) + mm(a_low, b_high, dims)


def swap(value, axis, bits):
    size = lax.axis_size(axis)
    return lax.ppermute(value, axis, [(i, i ^ bits) for i in range(size)])


def order_of(size):
    return list(range(0, size, 2)) + list(range(1, size, 2))


def position(k, size):
    return k // 2 + (k % 2) * ((size + 1) // 2)


def at_position(p, size):
    half = (size + 1) // 2
    return jnp.where(p < half, 2 * p, 2 * (p - half) + 1)


def gather_far(value, axis):
    pieces = {0: value}
    for k in range(2, lax.axis_size(axis), 2):
        pieces[k] = swap(value, axis, k)
    return pieces


def gather_near(pieces, axis):
    size = lax.axis_size(axis)
    pieces = dict(pieces)
    if size > 1:
        for k in range(0, size, 2):
            pieces[k ^ 1] = swap(pieces[k], axis, 1)
    return [pieces[k] for k in range(size)]


def gather(value, axis):
    return gather_near(gather_far(value, axis), axis)


def near_first(own, near, axis):
    size = lax.axis_size(axis)
    if size == 1:
        return [(own, 0)]
    half = size // 2
    rows = own.shape[0] // half
    terms = [(own, 0)]
    sent_on = []
    start = half
    for sent in near:
        other = swap(sent, axis, 1)
        other, *_ = lax.optimization_barrier((other, *sent_on))
        stop, start = start, start - sent.shape[0] // rows
        for i in range(stop - 1, start - 1, -1):
            if i == 0:
                terms.append((other, 0))
                continue
            got = other[(i - start) * rows : (i - start + 1) * rows]
            both = own[i * rows : (i + 1) * rows].astype(f32) + got.astype(f32)
            sent_on.append(both.astype(bf16))
            terms.append((swap(sent_on[-1], axis, 2 * i), 0))
    return terms


def far_first(pairs, axis):
    if lax.axis_size(axis) == 1:
        return [(pairs[0], 0)]
    rows = pairs[0].shape[0] // 2
    got = [pairs[0]]
    for i in range(1, len(pairs)):
        got.append(swap(pairs[i], axis, 2 * i))
    other = sum(both[rows:].astype(f32) for both in got).astype(bf16)
    return [(both, 0) for both in got] + [(swap(other, axis, 1), 0)]


def direct_terms(value, axis):
    terms = [value]
    for k in range(1, lax.axis_size(axis)):
        terms.append(swap(value, axis, k))
    return terms


def all_sum(value, axis):
    size = lax.axis_size(axis)
    if size == 1:
        return value
    value = value + swap(value, axis, 1)
    total = value
    for k in range(2, size, 2):
        total = total + swap(value, axis, k)
    return total


def softplus(v):
    return jnp.maximum(v, 0.0) + jnp.log1p(jnp.exp(-jnp.abs(v)))


def lower(size):
    return lax.broadcasted_iota(jnp.int32, (size, size), 0) >= lax.broadcasted_iota(
        jnp.int32, (size, size), 1
    )


def pick(values, lane_head):
    out = values[0]
    for j in range(1, len(values)):
        out = jnp.where(lane_head == j, values[j], out)
    return out


def take(out, refs, which):
    for k, ref in enumerate(refs):

        @pl.when(which == k)
        def _(ref=ref):
            out[...] = ref[...]


def join(out, refs, start=0):
    rows = refs[0].shape[0]
    cols = out.shape[1]
    for k, ref in enumerate(refs):
        out[k * rows : (k + 1) * rows, :] = ref[:, start : start + cols]


def forward_kernel(width, head_dim, count, pieces, per, start):
    per_group = LANES // head_dim

    def kernel(place, *refs):
        token_refs, refs = refs[:count], refs[count:]
        weight_refs, refs = refs[:pieces], refs[pieces:]
        taps_x, taps_bc, per_head, skip, *refs = refs
        if start:
            carried, refs = refs[:3], refs[10:]
        pre_x, pre_bc, raw_x, raw_bc, dt_out, mixed, before, state, halo_x, halo_bc = refs[:10]
        if start == 0:
            weights, refs = refs[10], refs[11:]
        else:
            weights, refs = weight_refs[0], refs[10:]
        ext_x, ext_bc, normed = refs
        size = normed.shape[0]
        take(normed, token_refs, ((pl.program_id(0) + start) // per) ^ place[0])
        inner = mixed.shape[1]
        twice = pre_bc.shape[1]
        states = twice // 2

        @pl.when(pl.program_id(0) == 0)
        def _():
            if start:
                state[...] = carried[0][...]
                ext_x[0:8, :] = carried[1][...]
                ext_bc[0:8, :] = carried[2][...]
            else:
                state[...] = jnp.zeros(state.shape, f32)
                ext_x[0:8, :] = jnp.zeros((8, inner), f32)
                ext_bc[0:8, :] = jnp.zeros((8, twice), f32)
                join(weights, weight_refs)

        raw = mm(normed[...], weights[...])

        def conv(ext, values, taps, raw_ref, pre_ref, halo):
            ext[8 : 8 + size, :] = values
            raw_ref[...] = values.astype(bf16)
            total = taps[width : width + 1, :]
            for k in range(width):
                start = 8 - (width - 1) + k
                total = total + taps[k : k + 1, :] * ext[start : start + size, :]
            halo[...] = ext[size : size + 8, :]
            ext[0:8, :] = halo[...]
            pre_ref[...] = total
            return total * jax.nn.sigmoid(total)

        x = conv(ext_x, raw[:, :inner], taps_x, raw_x, pre_x, halo_x)
        bc = conv(ext_bc, raw[:, inner : inner + twice], taps_bc, raw_bc, pre_bc, halo_bc)
        dt = raw[:, inner + twice :] + per_head[0:1, :]
        dt_out[...] = dt
        steps = softplus(dt)
        below = lower(size)
        logs = lax.dot_general(
            below.astype(f32), steps * per_head[1:2, :], NN, precision=highest,
            preferred_element_type=f32,
        )
        logs_t = logs.T
        keys = bc[:, :states]
        keys_t = keys.T
        queries = bc[:, states:]
        scores = jnp.where(below, fine(queries, keys, NT), 0.0)
        lane_head = lax.broadcasted_iota(jnp.int32, (size, LANES), 1) // head_dim
        for group in range(inner // LANES):
            lanes = slice(group * LANES, (group + 1) * LANES)
            x_g = x[:, lanes]
            heads = [group * per_group + j for j in range(per_group)]
            step_e = pick(
                [jnp.broadcast_to(steps[:, h : h + 1], (size, LANES)) for h in heads], lane_head
            )
            log_e = pick(
                [jnp.broadcast_to(logs[:, h : h + 1], (size, LANES)) for h in heads], lane_head
            )
            xs = x_g * step_e
            xs_half = xs.astype(bf16)
            total = skip[0:1, lanes] * x_g
            for j, h in enumerate(heads):
                gap = logs[:, h : h + 1] - logs_t[h : h + 1, :]
                weights_h = (scores * jnp.exp(jnp.minimum(gap, 0.0))).astype(bf16)
                total = total + mm(weights_h, jnp.where(lane_head == j, xs_half, 0.0))
            old = state[:, lanes]
            before[0, :, lanes] = old.astype(bf16)
            total = total + jnp.exp(log_e) * fine(queries, old)
            mixed[:, lanes] = total
            last = log_e[size - 1 : size, :]
            fresh = fine(keys_t, jnp.exp(last - log_e) * xs)
            state[:, lanes] = jnp.exp(last) * old + fresh

    return kernel


def backward_kernel(width, head_dim, resumed):
    per_group = LANES // head_dim

    def kernel(place, *refs):
        d_mixed, pre_x, pre_bc, raw_x, raw_bc, dt_in, mixed, before, *refs = refs
        taps_x, taps_bc, per_head, skip, *refs = refs
        if resumed:
            carried, refs = refs[:7], refs[8:]
        columns, *results, ext_x, ext_bc = refs
        grad_x, grad_bc, grad_head, d_state, after, halo_x, halo_bc = results
        size = d_mixed.shape[0]
        inner = d_mixed.shape[1]
        twice = pre_bc.shape[1]
        states = twice // 2

        @pl.when(pl.program_id(0) == 0)
        def _():
            for k, result in enumerate(results):
                result[...] = carried[k][...] if resumed else jnp.zeros(result.shape, f32)
            ext_x[size : size + 8, :] = halo_x[...]
            ext_bc[size : size + 8, :] = halo_bc[...]

        dt = dt_in[...]
        steps = softplus(dt)
        rates = per_head[1:2, :]
        below = lower(size)
        logs = lax.dot_general(
            below.astype(f32), steps * rates, NN, precision=highest, preferred_element_type=f32
        )
        logs_t = logs.T
        p_bc = pre_bc[...]
        sig_bc = jax.nn.sigmoid(p_bc)
        bc = p_bc * sig_bc
        keys = bc[:, :states].astype(bf16)
        queries = bc[:, states:].astype(bf16)
        queries_t = bc[:, states:].T
        above = lax.broadcasted_iota(jnp.int32, (size, size), 0) <= lax.broadcasted_iota(
            jnp.int32, (size, size), 1
        )
        scores_t = jnp.where(above, mm(keys, queries, NT), 0.0)
        lane_head = lax.broadcasted_iota(jnp.int32, (size, LANES), 1) // head_dim
        d_scores_t = jnp.zeros((size, size), f32)
        d_keys = jnp.zeros((size, states), f32)
        d_queries = jnp.zeros((size, states), f32)
        head_of = lax.broadcasted_iota(jnp.int32, (LANES, LANES), 0) // head_dim
        lane_of = lax.broadcasted_iota(jnp.int32, (LANES, LANES), 1)
        log_sum = jnp.zeros((size, LANES), f32)
        step_sum = jnp.zeros((size, LANES), f32)
        end_sum = jnp.zeros((8, LANES), f32)
        for group in range(inner // LANES):
            lanes = slice(group * LANES, (group + 1) * LANES)
            heads = [group * per_group + j for j in range(per_group)]
            p_x = pre_x[:, lanes]
            sig_x = jax.nn.sigmoid(p_x)
            x_g = p_x * sig_x
            dy = d_mixed[:, lanes]
            step_e = pick(
                [jnp.broadcast_to(steps[:, h : h + 1], (size, LANES)) for h in heads], lane_head
            )
            log_e = pick(
                [jnp.broadcast_to(logs[:, h : h + 1], (size, LANES)) for h in heads], lane_head
            )
            xs = x_g * step_e
            xs_half, dy_half = xs.astype(bf16), dy.astype(bf16)
            last = log_e[size - 1 : size, :]
            fade = jnp.exp(last - log_e)
            old = before[0, :, lanes]
            d_new = d_state[:, lanes]
            d_new_half = d_new.astype(bf16)
            dxs = fade * mm(keys, d_new_half)
            for j, h in enumerate(heads):
                mine = lane_head == j
                gap = logs_t[h : h + 1, :] - logs[:, h : h + 1]
                decay = jnp.exp(jnp.minimum(gap, 0.0))
                dxs = dxs + mm(
                    (scores_t * decay).astype(bf16), jnp.where(mine, dy_half, 0.0)
                )
                d_scores_t = d_scores_t + decay * mm(jnp.where(mine, xs_half, 0.0), dy_half, NT)
            e_dy = jnp.exp(log_e) * dy
            d_queries = d_queries + sum(mm(half, old, NT) for half in halves(e_dy))
            d_keys = d_keys + fine(fade * xs, d_new, NT)
            skip_g = skip[0:1, lanes]
            log_lane = dy * (mixed[:, lanes] - skip_g * x_g) - xs * dxs
            step_lane = dxs * x_g
            end_lane = jnp.sum(d_new * after[:, lanes], axis=0, keepdims=True)
            to_head = (head_of + group * per_group == lane_of).astype(bf16)
            for high_low in halves(log_lane):
                log_sum = log_sum + mm(high_low, to_head)
            for high_low in halves(step_lane):
                step_sum = step_sum + mm(high_low, to_head)
            for high_low in halves(jnp.broadcast_to(end_lane, (8, LANES))):
                end_sum = end_sum + mm(high_low, to_head)
            d_state[:, lanes] = jnp.exp(last) * d_new + fine(queries_t, e_dy)
            after[:, lanes] = old.astype(f32)
            grad_x[width + 1 : width + 2, lanes] += jnp.sum(dy * x_g, axis=0, keepdims=True)
            dx = dxs * step_e + skip_g * dy
            d_pre = dx * (sig_x + x_g * (1.0 - sig_x))
            ext_x[0:size, lanes] = d_pre
            grad_x[width : width + 1, lanes] += jnp.sum(d_pre, axis=0, keepdims=True)
            total = jnp.zeros((size, LANES), f32)
            raw = raw_x[:, lanes].astype(f32)
            for k in range(width):
                moved = ext_x[width - 1 - k : width - 1 - k + size, lanes]
                total = total + taps_x[k : k + 1, lanes] * moved
                grad_x[k : k + 1, lanes] += jnp.sum(raw * moved, axis=0, keepdims=True)
            columns[:, lanes] = total.astype(bf16)
            halo_x[:, lanes] = ext_x[0:8, lanes]
            ext_x[size : size + 8, lanes] = halo_x[:, lanes]
        d_scores_t = jnp.where(above, d_scores_t, 0.0)
        d_keys = d_keys + fine(d_scores_t, bc[:, states:])
        d_queries = d_queries + fine(d_scores_t.T, bc[:, :states])
        at_end = lax.broadcasted_iota(jnp.int32, (size, LANES), 0) == size - 1
        d_log = log_sum + jnp.where(at_end, end_sum[0:1, :], 0.0)
        d_rate = lax.dot_general(
            above.astype(f32), d_log, NN, precision=highest, preferred_element_type=f32
        )
        grad_head[1:2, :] += rates * jnp.sum(steps * d_rate, axis=0, keepdims=True)
        d_dt = (step_sum + rates * d_rate) * jax.nn.sigmoid(dt)
        grad_head[0:1, :] += jnp.sum(d_dt, axis=0, keepdims=True)
        columns[:, inner + twice :] = d_dt.astype(bf16)
        slope = sig_bc + bc * (1.0 - sig_bc)
        ext_bc[0:size, :states] = d_keys * slope[:, :states]
        ext_bc[0:size, states:] = d_queries * slope[:, states:]
        grad_bc[width : width + 1, :] += jnp.sum(ext_bc[0:size, :], axis=0, keepdims=True)
        total = jnp.zeros((size, twice), f32)
        raw = raw_bc[...].astype(f32)
        for k in range(width):
            moved = ext_bc[width - 1 - k : width - 1 - k + size, :]
            total = total + taps_bc[k : k + 1, :] * moved
            grad_bc[k : k + 1, :] += jnp.sum(raw * moved, axis=0, keepdims=True)
        columns[:, inner : inner + twice] = total.astype(bf16)
        halo_bc[...] = ext_bc[0:8, :]
        ext_bc[size : size + 8, :] = halo_bc[...]

    return kernel


def gate_kernel(count, pieces, parts):
    def kernel(place, *refs):
        normed_refs, upstream_refs, refs = refs[:count], refs[count : 2 * count], refs[2 * count :]
        weight_refs, refs = refs[:pieces], refs[pieces:]
        mixed, gain, gate_raw, grad_scaled, sums, normed, upstream, w_gate, w_out = refs

        @pl.when(pl.program_id(0) == 0)
        def _():
            join(w_gate, [weight_refs[k] for k in order_of(pieces)])
            join(w_out, weight_refs, w_gate.shape[1])

        take(normed, normed_refs, pl.program_id(0) // parts)
        take(upstream, upstream_refs, pl.program_id(0) // parts)
        gate_body(normed, upstream, w_gate, w_out, mixed, gain, gate_raw, grad_scaled, sums)

    return kernel


def gate_body(normed, upstream, w_gate, w_out, mixed, gain, gate_raw, grad_scaled, sums):
    gate = mm(normed[...], w_gate[...])
    grads = mm(upstream[...], w_out[...])
    gate_raw[...] = gate
    grad_scaled[...] = grads
    gated = mixed[...] * (gate * jax.nn.sigmoid(gate))
    ones = jnp.ones((8, gated.shape[1]), bf16)
    rows = lax.broadcasted_iota(jnp.int32, sums.shape[1:], 0)
    square = sum(mm(ones, part, NT) for part in halves(gated * gated))
    cross = sum(mm(ones, part, NT) for part in halves(gated * (grads * gain[...])))
    sums[0] = jnp.where(rows == 0, square, cross)


def norm_kernel(inner_total, count):
    def kernel(place, *refs):
        terms, refs = refs[:count], refs[count:]
        gate_raw, grad_scaled, mixed, gain, scaled, d_mixed, d_gate, grad_gain = refs

        @pl.when(pl.program_id(0) == 0)
        def _():
            grad_gain[...] = jnp.zeros(grad_gain.shape, f32)

        total = terms[0][0]
        for term in terms[1:]:
            total = total + term[0]
        column = total.T
        inverse = lax.rsqrt(column[:, 0:1] / inner_total + epsilon)
        pull = inverse * inverse * inverse * (column[:, 1:2] / inner_total)
        gate = gate_raw[...]
        sig = jax.nn.sigmoid(gate)
        act = gate * sig
        mix = mixed[...]
        grads = grad_scaled[...]
        unit = mix * act * inverse
        scaled[...] = (unit * gain[...]).astype(bf16)
        grad_gain[0:1, :] += jnp.sum(grads * unit, axis=0, keepdims=True)
        d_gated = inverse * (grads * gain[...]) - (mix * act) * pull
        d_mixed[...] = d_gated * act
        d_gate[...] = (d_gated * mix * (sig + act * (1.0 - sig))).astype(bf16)

    return kernel


def place_of(place, k, blocks, size):
    return pl.multiple_of(position(place[0] ^ k, blocks) * size, size)


def entry_kernel(blocks):
    def kernel(place, tokens, upstream, gain, normed_out, upstream_out):
        size = tokens.shape[1] // blocks
        wide = tokens[...].astype(f32)
        inverse = lax.rsqrt(jnp.mean(wide * wide, axis=-1, keepdims=True) + epsilon)
        normed = (wide * inverse * gain[...]).astype(bf16)
        for k in range(blocks):
            at = pl.ds(place_of(place, k, blocks, size), size)
            normed_out[:, at] = normed[:, k * size : (k + 1) * size]
            at = pl.ds(pl.multiple_of((place[0] ^ k) * size, size), size)
            upstream_out[:, at] = upstream[:, k * size : (k + 1) * size]

    return kernel


def pack_kernel(blocks, cols):
    def kernel(place, grad_x, grad_gain, grad_bc, grad_head, pre_part, gain, out, row):
        twice = grad_bc.shape[1]
        inner = grad_x.shape[1]
        model = row.shape[1]
        size = model // blocks
        out[...] = jnp.zeros(out.shape, f32)
        out[0:8, :inner] = grad_x[...]
        out[8:16, :inner] = grad_gain[...]
        out[16:24, :twice] = grad_bc[...]
        out[16:24, twice : twice + LANES] = grad_head[...]
        for k in range(blocks):
            at = pl.ds(place_of(place, k, blocks, size), size)
            row[:, k * size : (k + 1) * size] = pre_part[:, at]
        for k in range(model // cols):
            part = slice(k * cols, (k + 1) * cols)
            out[24 + k : 25 + k, :] = row[0:1, part] / gain[0:1, part]

    return kernel


def output_kernel(blocks, count):
    def kernel(place, tokens, *refs):
        out = refs[count]
        size = tokens.shape[1] // blocks
        for k in range(blocks):
            at = pl.multiple_of((place[0] ^ k) * size, size)
            total = tokens[:, k * size : (k + 1) * size].astype(f32)
            for term in refs[:count]:
                total = total + term[:, pl.ds(at, size)].astype(f32)
            out[:, 0, k * size : (k + 1) * size] = total

    return kernel


def input_kernel(blocks, count):
    def kernel(place, tokens, upstream, gain, *refs):
        out, grads = refs[count:]
        model = tokens.shape[1]
        size = model // blocks
        wide = tokens[...].astype(f32)
        inverse = lax.rsqrt(jnp.mean(wide * wide, axis=-1, keepdims=True) + epsilon)
        for k in range(blocks):
            at = place_of(place, k, blocks, size)
            total = refs[0][:, pl.ds(at, size)].astype(f32)
            for term in refs[1:count]:
                total = total + term[:, pl.ds(at, size)].astype(f32)
            grads[:, k * size : (k + 1) * size] = total
        weighted = grads[...] * gain[...]
        inner_dot = jnp.mean(weighted * wide, axis=-1, keepdims=True)
        out[:, 0, :] = (
            upstream[...].astype(f32)
            + inverse * weighted
            - wide * (inverse * inverse * inverse * inner_dot)
        )

    return kernel


def normed_kernel(place, tokens, d_gate, columns, w_gate, w_scan, own, near, grad_gain):
    total = mm(d_gate[...], w_gate[...], NT) + mm(columns[...], w_scan[...], NT)
    own[...] = total[: own.shape[0]].astype(bf16)
    near[...] = total[-near.shape[0] :].astype(bf16)
    total = total * tokens[...].astype(f32)
    grad_gain[...] = jnp.broadcast_to(jnp.sum(total, axis=0, keepdims=True), grad_gain.shape)


def weights_kernel(counts, inner, twice):
    def kernel(place, *refs):
        groups = []
        for count in counts:
            groups.append(refs[:count])
            refs = refs[count:]
        grad_zx, grad_out, grad_dt, grad_bc = refs

        def total(terms):
            return sum(term[...].astype(f32) for term in terms)

        scan, gate, out = (total(group) for group in groups)
        grad_zx[:, 0, :] = gate
        grad_zx[:, 1, :] = scan[:, :inner]
        grad_out[...] = out.T
        grad_bc[...] = scan[:, inner : inner + twice]
        grad_dt[...] = scan[:, inner + twice : inner + twice + grad_dt.shape[1]]

    return kernel


def shared_kernel(count, rows, cols):
    def kernel(place, *refs):
        grad_w, of_taps, of_bias, of_pre = refs[count:]
        width = of_taps.shape[0]
        total = refs[0][...]
        for term in refs[1:count]:
            total = total + term[...]
        share, twice = grad_w.shape
        grad_w[...] = total[:share]
        of_taps[...] = total[share : share + width]
        of_bias[...] = total[share + width : share + width + 1]
        for r in range(of_pre.shape[1] // cols):
            for k in range(cols // twice):
                at = share + k * rows + 8 + r
                start = r * cols + k * twice
                of_pre[:, start : start + twice] = total[at : at + 1]

    return kernel


def whole(shape):
    return pl.BlockSpec(shape, lambda c, place: (0,) * len(shape))


def rows_of(size, cols, column=0):
    return pl.BlockSpec((size, cols), lambda c, place: (c, column))


def call(kernel, grid, ins, outs, shapes, scratch=(), aliases=None):
    return pl.pallas_call(
        kernel,
        grid_spec=pltpu.PrefetchScalarGridSpec(
            num_scalar_prefetch=1, grid=(grid,), in_specs=ins, out_specs=outs,
            scratch_shapes=scratch,
        ),
        out_shape=[jax.ShapeDtypeStruct(*one) for one in shapes],
        input_output_aliases=aliases or {},
    )


def exchange_blocks(values, axis, blocks, back=False, ordered=True):
    index = lax.axis_index(axis)
    order = order_of(blocks)
    blocked = values.reshape(values.shape[0], blocks, -1)
    if back and ordered:
        blocked = jnp.stack([blocked[:, order.index(k)] for k in range(blocks)], axis=1)
    bits = 1
    while bits < blocks:
        split = blocked.reshape(blocked.shape[0], blocks // (2 * bits), 2, -1)
        blocked = jnp.where((index & bits) != 0, split[:, :, ::-1], split)
        blocked = blocked.reshape(blocked.shape[0], blocks, -1)
        bits *= 2
    if ordered and not back:
        blocked = jnp.stack([blocked[:, k] for k in order], axis=1)
    return blocked.reshape(values.shape)


def per_device(
    block_input, pre_gain, w_zx, w_dt, w_bc, conv_x_w, conv_x_b, conv_bc_w, conv_bc_b,
    dt_bias, a_log, d_skip, gate_gain, w_out, cotangent,
):
    rows_local, seqs, model = block_input.shape
    assert seqs == 1
    dp = lax.axis_size(DP)
    tensor = lax.axis_size(TP)
    length = rows_local * tensor
    inner = w_zx.shape[2]
    twice = w_bc.shape[1]
    states = twice // 2
    heads = w_dt.shape[1]
    head_dim = inner // heads
    width = conv_x_w.shape[0]
    wide_cols = inner + twice + LANES
    inner_total = inner * tensor
    chunk = min(CHUNK, rows_local)
    block = min(ROWS, rows_local)
    chunks = length // chunk
    place_dp = lax.axis_index(DP).astype(jnp.int32).reshape(1)
    place_tensor = lax.axis_index(TP).astype(jnp.int32).reshape(1)
    narrow = (model // dp) % LANES != 0
    blocks = 1 if narrow else dp
    place_entry = place_dp * 0 if narrow else place_dp

    slab = rows_local
    tokens_local = block_input.reshape(rows_local, model)
    upstream_local = cotangent.reshape(rows_local, model)
    gain_in = pre_gain.reshape(1, model)
    w_scan = jnp.concatenate(
        [w_zx[:, 1, :], w_bc, w_dt, jnp.zeros((w_dt.shape[0], LANES - heads), bf16)], axis=1
    )
    w_late = jnp.concatenate([w_zx[:, 0, :], w_out.T], axis=1)
    normed_local, upstream_sent = call(
        entry_kernel(blocks), rows_local // slab,
        [rows_of(slab, model), rows_of(slab, model), whole((1, model))],
        [rows_of(slab, model)] * 2,
        [((rows_local, model), bf16)] * 2,
    )(place_entry, tokens_local, upstream_local, gain_in)
    if narrow:
        normed_local = exchange_blocks(normed_local, DP, dp)
        upstream_sent = exchange_blocks(upstream_sent, DP, dp, ordered=False)

    def stack(rows, cols):
        rows = [r.reshape(-1, r.shape[-1]) for r in rows]
        packed = jnp.concatenate(rows, axis=0)
        return jnp.pad(packed, ((0, 8 - packed.shape[0]), (0, cols - packed.shape[1])))

    taps_x = stack([conv_x_w, conv_x_b], inner)
    taps_bc = stack([conv_bc_w, conv_bc_b], twice)
    per_head = stack([dt_bias, -jnp.exp(a_log)], LANES)
    skip = jnp.repeat(d_skip, head_dim).reshape(1, inner)
    gain = gate_gain.reshape(1, inner)
    forward_shapes = [((states, inner), f32), ((8, inner), f32), ((8, twice), f32)]
    backward_shapes = [((8, inner), f32), ((8, twice), f32), ((8, LANES), f32)]
    backward_shapes += [((states, inner), f32)] * 2 + [((8, inner), f32), ((8, twice), f32)]

    scan_far = gather_far(w_scan, DP)
    scan_far[0], taps_x, taps_bc, per_head, skip, gain = lax.optimization_barrier(
        (scan_far[0], taps_x, taps_bc, per_head, skip, gain)
    )
    scan_pieces = gather_near(scan_far, DP)
    normed_pieces = gather(normed_local, TP)
    late_pieces = gather(w_late, DP)
    upstream_pieces = gather(upstream_sent, TP)
    dp_order, tensor_order = order_of(dp), order_of(tensor)

    per = rows_local // chunk

    def stored(c, place):
        return position((c // per) ^ place[0], tensor) * per + c % per

    def ahead(cols, start):
        return pl.BlockSpec((chunk, cols), lambda c, place: (stored(c + start, place), 0))

    def back(cols, start):
        return pl.BlockSpec((chunk, cols), lambda c, place: (stored(start - c, place), 0))

    def token_piece(k, start):
        def index(c, place):
            c = c + start
            return jnp.where((c // per) ^ place[0] == k, c % per, 0), 0

        return pl.BlockSpec((chunk, model), index)

    anywhere = pl.BlockSpec(memory_space=pl.ANY)
    calls = 2 if chunks % 2 == 0 else 1
    span = chunks // calls
    first = -(-chunks * 5 // 8)
    carry, saved, weights = [], [], [scan_pieces[k] for k in dp_order]
    for start, stop in ((0, first), (first, chunks)):
        results = call(
            forward_kernel(width, head_dim, tensor, len(weights), per, start),
            stop - start,
            [token_piece(k, start) for k in range(tensor)]
            + [whole(one.shape) for one in weights]
            + [whole((8, inner)), whole((8, twice)), whole((8, LANES)), whole((1, inner))]
            + [whole(one.shape) for one in carry]
            + [anywhere] * len(saved),
            [ahead(cols, start) for cols in (inner, twice, inner, twice, LANES, inner)]
            + [pl.BlockSpec((1, states, inner), lambda c, place, start=start: (c + start, 0, 0))]
            + [whole(one) for one, _ in forward_shapes]
            + [whole((model, wide_cols))] * (start == 0),
            [
                ((length, inner), f32), ((length, twice), f32), ((length, inner), bf16),
                ((length, twice), bf16), ((length, LANES), f32), ((length, inner), f32),
                ((chunks, states, inner), bf16), *forward_shapes,
            ]
            + [((model, wide_cols), bf16)] * (start == 0),
            [
                pltpu.VMEM((chunk + 8, inner), f32), pltpu.VMEM((chunk + 8, twice), f32),
                pltpu.VMEM((chunk, model), bf16),
            ],
            {1 + tensor + len(weights) + 7 + k: k for k in range(len(saved))},
        )(place_tensor, *normed_pieces, *weights, taps_x, taps_bc, per_head, skip, *carry, *saved)
        saved, carry = results[:7], results[7:10]
        if start == 0:
            full_scan = results[10]
            weights = [full_scan]
    pre_x, pre_bc, raw_x, raw_bc, dt, mixed, before = saved

    parts = rows_local // block
    in_order = pl.BlockSpec(
        (1, 8, block), lambda c, place: ((at_position(c // parts, tensor) ^ place[0]) * parts + c % parts, 0, 0)
    )

    def gate_piece(p):
        return pl.BlockSpec(
            (block, model), lambda c, place: (jnp.where(c // parts == p, c % parts, 0), 0)
        )

    gate_raw, grad_scaled, sums, normed, upstream, full_gate, full_out = call(
        gate_kernel(tensor, dp, parts), length // block,
        [gate_piece(p) for p in range(tensor)] * 2
        + [whole((model // dp, 2 * inner))] * dp
        + [rows_of(block, inner), whole((1, inner))],
        [
            rows_of(block, inner), rows_of(block, inner), in_order, rows_of(block, model),
            rows_of(block, model), whole((model, inner)), whole((model, inner)),
        ],
        [
            ((length, inner), f32), ((length, inner), f32), ((length // block, 8, block), f32),
            ((length, model), bf16), ((length, model), bf16), ((model, inner), bf16),
            ((model, inner), bf16),
        ],
    )(
        place_tensor, *[normed_pieces[k] for k in tensor_order],
        *[upstream_pieces[k] for k in tensor_order], *late_pieces,
        mixed, gain,
    )

    sum_terms = direct_terms(sums, TP)

    scaled, d_mixed, d_gate, grad_gain = call(
        norm_kernel(inner_total, tensor), length // block,
        [in_order] * tensor
        + [rows_of(block, inner), rows_of(block, inner), rows_of(block, inner), whole((1, inner))],
        [rows_of(block, inner), rows_of(block, inner), rows_of(block, inner), whole((8, inner))],
        [
            ((length, inner), bf16), ((length, inner), f32), ((length, inner), bf16),
            ((8, inner), f32),
        ],
    )(place_tensor, *sum_terms, gate_raw, grad_scaled, mixed, gain)

    share = model // dp

    def tn(left, right):
        return lax.dot_general(left, right, TN, preferred_element_type=f32).astype(bf16)

    out_part = lax.optimization_barrier(tn(upstream, scaled))
    out_pairs = [out_part[k * share : (k + 2) * share] for k in range(0, dp, 2)]
    even = share * ((dp + 1) // 2)
    gate_part = lax.optimization_barrier(tn(normed, d_gate))
    gate_own, gate_near = gate_part[:even], [gate_part[even:]]
    stay = rows_local * ((tensor + 1) // 2)
    branch_part = lax.optimization_barrier(mm(scaled, full_out, NT).astype(bf16))
    branch_own, branch_near = branch_part[:stay], branch_part[stay:]
    out_terms = far_first(out_pairs, DP)
    gate_terms = near_first(gate_own, gate_near, DP)
    branch_terms = near_first(branch_own, [branch_near], TP)
    if narrow:
        branch_terms = [
            (exchange_blocks(array, DP, dp, True, False), k) for array, k in branch_terms
        ]
    slabs = rows_local // slab
    out_block = pl.BlockSpec((slab, 1, model), lambda c, place: (c, 0, 0))

    def one_block(k):
        return pl.BlockSpec((slab, model), lambda c, place: (k * slabs + c, 0))

    (block_output,) = call(
        output_kernel(blocks, len(branch_terms)), slabs,
        [rows_of(slab, model)] + [one_block(k) for _, k in branch_terms],
        [out_block],
        [((rows_local, 1, model), f32)],
    )(place_entry, tokens_local, *[array for array, _ in branch_terms])

    carry = []
    columns = []
    for at in range(calls):
        start = chunks - 1 - at * span
        columns, *carry = call(
            backward_kernel(width, head_dim, len(columns)), span,
            [back(cols, start) for cols in (inner, inner, twice, inner, twice, LANES, inner)]
            + [pl.BlockSpec((1, states, inner), lambda c, place, start=start: (start - c, 0, 0))]
            + [whole((8, inner)), whole((8, twice)), whole((8, LANES)), whole((1, inner))]
            + [whole(one.shape) for one in carry]
            + [anywhere] * len(columns),
            [back(wide_cols, start)] + [whole(one) for one, _ in backward_shapes],
            [((length, wide_cols), bf16), *backward_shapes],
            [pltpu.VMEM((chunk + 8, inner), f32), pltpu.VMEM((chunk + 8, twice), f32)],
            {1 + 8 + 4 + 7: 0} if columns else {},
        )(
            place_tensor, d_mixed, pre_x, pre_bc, raw_x, raw_bc, dt, mixed, before, taps_x,
            taps_bc, per_head, skip, *carry, *columns,
        )
        columns = [columns]
    columns = columns[0]
    grad_x, grad_bc, grad_head = carry[:3]

    later = model - share if model - share > even else even
    scan_near = [tn(normed[:, later:], columns)]
    if later > even:
        scan_near.append(tn(normed[:, even:later], columns))
    scan_own = tn(normed[:, :even], columns)
    scan_terms = near_first(scan_own, scan_near, DP)
    features = model // 4
    leave = max(length - stay, rows_local)
    normed_own, normed_near, pre_part = call(
        normed_kernel, 4,
        [
            pl.BlockSpec((length, features), lambda c, place: (0, c)),
            whole((length, inner)), whole((length, wide_cols)),
            rows_of(features, inner), rows_of(features, wide_cols),
        ],
        [
            pl.BlockSpec((stay, features), lambda c, place: (0, c)),
            pl.BlockSpec((leave, features), lambda c, place: (0, c)),
            pl.BlockSpec((8, features), lambda c, place: (0, c)),
        ],
        [((stay, model), bf16), ((leave, model), bf16), ((8, model), f32)],
    )(place_tensor, normed, d_gate, columns, full_gate, full_scan)
    normed_terms = near_first(normed_own, [normed_near], TP)
    if narrow:
        normed_terms = [(exchange_blocks(array, DP, dp, True), k) for array, k in normed_terms]
    (input_grad,) = call(
        input_kernel(blocks, len(normed_terms)), slabs,
        [rows_of(slab, model)] * 2 + [whole((1, model))]
        + [one_block(k) for _, k in normed_terms],
        [out_block], [((rows_local, 1, model), f32)], [pltpu.VMEM((slab, model), f32)],
    )(place_entry, tokens_local, upstream_local, gain_in, *[array for array, _ in normed_terms])

    groups = (scan_terms, gate_terms, out_terms)
    grad_w_zx, grad_w_out, grad_w_dt, grad_bc_part = call(
        weights_kernel([len(terms) for terms in groups], inner, twice), 1,
        [
            pl.BlockSpec((share, array.shape[1]), lambda c, place, k=k: (k, 0))
            for terms in groups for array, k in terms
        ],
        [whole((share, 2, inner)), whole((inner, share)), whole((share, heads)), whole((share, twice))],
        [
            ((share, 2, inner), f32), ((inner, share), f32), ((share, heads), f32),
            ((share, twice), f32),
        ],
    )(place_entry, *[array for terms in groups for array, _ in terms])
    cols = max(inner, twice + LANES)
    cols += -cols % 512
    if narrow:
        pre_part = exchange_blocks(pre_part, DP, dp, True)
    rows = 24 + max(model // cols, 8)
    (packed,) = call(
        pack_kernel(blocks, cols), 1,
        [
            whole((8, inner)), whole((8, inner)), whole((8, twice)), whole((8, LANES)),
            whole((8, model)), whole((1, model)),
        ],
        [whole((rows, cols))], [((rows, cols), f32)], [pltpu.VMEM((8, model), f32)],
    )(place_entry, grad_x, grad_gain, grad_bc, grad_head, pre_part, gain_in)
    small = all_sum(packed, DP)

    assert cols % twice == 0 and model % cols == 0
    across = [small[16:, k : k + twice] for k in range(0, cols, twice)]
    across = jnp.concatenate(across, axis=0)
    across = direct_terms(jnp.concatenate([grad_bc_part, across], axis=0), TP)
    grad_w_bc, sum_taps, sum_bias, sum_pre = call(
        shared_kernel(tensor, rows - 16, cols), 1,
        [whole(across[0].shape)] * tensor,
        [whole((share, twice)), whole((width, twice)), whole((1, twice)), whole((1, model))],
        [((share, twice), f32), ((width, twice), f32), ((1, twice), f32), ((1, model), f32)],
    )(place_entry, *across)
    of_x = small[:8, :inner]
    sum_gain = small[8, :inner]
    of_head = small[16:24, twice : twice + LANES]
    return (
        block_output,
        input_grad,
        sum_pre.reshape(model),
        grad_w_zx,
        grad_w_dt,
        grad_w_bc,
        of_x[:width],
        of_x[width],
        sum_taps,
        sum_bias.reshape(twice),
        of_head[0, :heads],
        of_head[1, :heads],
        of_x[width + 1].reshape(heads, head_dim).sum(axis=1),
        sum_gain,
        grad_w_out,
    )


def solution(mesh):
    placed = (
        P(TP, DP, None), P(), P(DP, None, TP), P(DP, TP), P(DP, None),
        P(None, TP), P(TP), P(), P(), P(TP), P(TP), P(TP),
        P(TP), P(TP, DP), P(TP, DP, None),
    )
    results = (
        P(TP, DP, None), P(TP, DP, None), P(), P(DP, None, TP),
        P(DP, TP), P(DP, None), P(None, TP), P(TP), P(), P(), P(TP),
        P(TP), P(TP), P(TP), P(TP, DP),
    )

    return jax.shard_map(per_device, mesh=mesh, in_specs=placed, out_specs=results, check_vma=False)
```
